32 devices in a mesh: tm: 4 (over y, core), space: 8 (over z, x).
Axes of the slice: x: 2, y: 2, z: 4, core: 2. Of those that a mesh axis runs over, the one named last changes fastest.
Arguments:
- initial: float32 [24, 192, 256], P('space'), may hold values from -1 to 1
- coarse_guess: float32 [4, 24, 192, 256], P('tm', 'space'), may hold values from -1 to 1
- react_rate: float32 [24, 192, 256], P('space'), may hold values from 0.5 to 3
Outputs:
- corrected: float32 [4, 24, 192, 256], P('tm', 'space')
- defect: float32 [4, 24, 192, 256], P('tm', 'space')
The draws below stay inside these ranges and needn't reach their ends.
All inputs are finite; a program needn't handle non-finite values.
Results may differ from the reference program's by a relative error of at most 0.00002.
Values sent between devices are 32-bit elements; how exact they have to be, the bound alone decides.
A program may use at most 64 MiB of HBM per device.

```python
import math
import jax
import jax.numpy as jnp
from jax import lax

NX = 192
NY = 256
STEPS = 3
NZ = 24
INTERVALS = 4


def levels(own_key, dims, cuts, smallest, largest):
    gain, own = 1.0, jax.random.fold_in(own_key, 6)
    for axis_at, parts in cuts:
        steps = jnp.exp(jax.random.uniform(jax.random.fold_in(own, axis_at), (parts,), jnp.float32, smallest / len(cuts), largest / len(cuts)))
        gain = gain * jnp.repeat(steps, dims[axis_at] // parts).reshape([-1 if axis == axis_at else 1 for axis in range(len(dims))])
    return gain


def setup_inputs(seed: int = 0) -> dict:
    key_of = jax.random.split(jax.random.key(seed), 4)
    initial = jnp.clip(jax.random.uniform(key_of[0], (NZ, NX, NY), jnp.float32, -1.0, 1.0) * levels(key_of[0], (NZ, NX, NY), ((0, 8),), -0.4, 0.0), -1.0, 1.0)
    coarse_guess = jnp.clip(jax.random.uniform(key_of[1], (INTERVALS, NZ, NX, NY), jnp.float32, -1.0, 1.0) * levels(key_of[1], (INTERVALS, NZ, NX, NY), ((0, 4), (1, 8)), -0.4, 0.0), -1.0, 1.0)
    react_rate = jnp.clip(jnp.exp(math.log(3.0) - 1.7917595 * jax.random.uniform(key_of[2], (NZ, NX, NY), jnp.float32) ** levels(key_of[2], (NZ, NX, NY), ((0, 8),), -0.2, 0.2)), 0.5, 3.0)
    return dict(initial=initial, coarse_guess=coarse_guess, react_rate=react_rate)


fine_diffuse = 0.04
fine_growth = 0.05
coarse_diffuse = 0.16
coarse_growth = 0.2


def explicit(current, react_rate, diffuse, growth):
    widths = [(0, 0)] * (current.ndim - 3) + [(1, 1)] * 3
    padded = jnp.pad(current, widths)
    beside = padded[..., 2:, 1:-1, 1:-1] + padded[..., :-2, 1:-1, 1:-1]
    beside = beside + padded[..., 1:-1, 2:, 1:-1] + padded[..., 1:-1, :-2, 1:-1]
    beside = beside + padded[..., 1:-1, 1:-1, 2:] + padded[..., 1:-1, 1:-1, :-2]
    return current + diffuse * (beside - 6.0 * current) + (growth * react_rate) * (current - current * current * current)


def reference(initial, coarse_guess, react_rate):
    starts = jnp.concatenate([initial[None], coarse_guess[:-1]], axis=0)
    current = starts
    for repeat in range(STEPS):
        current = explicit(current, react_rate, fine_diffuse, fine_growth)
    relaxed = current
    again = jnp.concatenate([initial[None], relaxed[:-1]], axis=0)
    current = again
    for repeat in range(STEPS):
        current = explicit(current, react_rate, fine_diffuse, fine_growth)
    fine_end = current
    defect = fine_end - relaxed
    offsets = fine_end - explicit(again, react_rate, coarse_diffuse, coarse_growth)

    def chain_turn(before, offset):
        after = explicit(before, react_rate, coarse_diffuse, coarse_growth) + offset
        return after, after

    unused, corrected = lax.scan(chain_turn, initial, offsets)
    return corrected, defect
```

```python
import functools

import jax
import jax.numpy as jnp
from jax import lax
from jax.experimental import pallas as pl
from jax.experimental.pallas import tpu as pltpu
from jax.sharding import PartitionSpec as P

STEPS = 3
SUBLANES = 8

fine_diffuse = 0.04
fine_growth = 0.05
coarse_ratio = 4.0

MESH = pl.DeviceIdType.MESH

PIECES = 4
HALVES = 2


def slots(planes):
    kinds = dict(
        start=2 + PIECES, start_edge=1 + PIECES, rate=1, rate_edge=2, rate_core=3, again=PIECES, again_edge=2 * PIECES,
        chain=2 * planes, chain_edge=2, defect=1, corrected=planes,
    )
    first, total = {}, 0
    for kind, number in kinds.items():
        first[kind] = total
        total += number
    return first, total


def kernel(
    nt, ns, planes, half, wide, slot_of,
    initial, guess, rate_in, corrected_out, defect_out,
    start, rate, again, before, first, second, relaxed, coarse, offset, defect, after, reach,
    send, recv, local,
):
    tm, space = lax.axis_index("tm"), lax.axis_index("space")
    pair, side = lax.div(space, 2), lax.rem(space, 2)
    pairs = ns // 2
    mate = space + 1 - 2 * side
    block = 2 * planes
    length = block + 2 * STEPS
    rows = half + 2 * wide
    has_low, has_high = pair > 0, pair < pairs - 1
    has_next, has_previous = tm < nt - 1, tm > 0
    own = pl.ds(STEPS, block)

    for ref in (start, rate, again, before):
        zero_plane = jnp.zeros((STEPS,) + ref.shape[1:], jnp.float32)
        zero_rows = jnp.zeros((block, wide, ref.shape[2]), jnp.float32)
        ref[0:STEPS] = zero_plane
        ref[STEPS + block : length] = zero_plane
        ref[STEPS : STEPS + block, 0:wide] = zero_rows
        ref[STEPS : STEPS + block, wide + half : rows] = zero_rows

    barrier = pltpu.get_barrier_semaphore()
    count = jnp.int32(0)
    for step in (-1, 0, 1):
        for place in ("own", "mate", "low", "high"):
            if step == 0 and place == "own":
                continue
            there = {"own": space, "mate": mate, "low": space - 2, "high": space + 2}[place]
            tests = []
            if step:
                tests.append(has_next if step > 0 else has_previous)
            if place in ("low", "high"):
                tests.append(has_low if place == "low" else has_high)
            target = {"tm": tm + step, "space": there}
            if tests:
                valid = functools.reduce(jnp.logical_and, tests)

                @pl.when(valid)
                def _(target=target):
                    pl.semaphore_signal(barrier, inc=1, device_id=target, device_id_type=MESH)

                count = count + valid.astype(jnp.int32)
            else:
                pl.semaphore_signal(barrier, inc=1, device_id=target, device_id_type=MESH)
                count = count + 1
    for here, there in ((tm == 0, nt - 1), (tm == nt - 1, 0)):

        @pl.when(here)
        def _(there=there):
            pl.semaphore_signal(
                barrier, inc=1, device_id={"tm": there, "space": mate}, device_id_type=MESH
            )

        count = count + here.astype(jnp.int32)
    pl.semaphore_wait(barrier, count)

    def remote(src, dst, slot, to_tm, to_space):
        return pltpu.make_async_remote_copy(
            src_ref=src,
            dst_ref=dst,
            send_sem=send.at[slot],
            recv_sem=recv.at[slot],
            device_id={"tm": to_tm, "space": to_space},
            device_id_type=MESH,
        )

    def cut(ref, target):
        return ref.at[:, pl.ds(pl.multiple_of(target * (half - wide), SUBLANES), half + wide), :]

    def spot(ref, target, begin, size):
        at = pl.multiple_of(wide * (1 - target), SUBLANES)
        return ref.at[pl.ds(begin, size), pl.ds(at, half + wide), :]

    slab = STEPS + planes * side
    other = STEPS + planes * (1 - side)

    core = lax.rem(tm, 2)
    twin = tm + 1 - 2 * core
    lanes = start.shape[2] // 2

    def lane_half(ref, which):
        return ref.at[:, :, pl.ds(pl.multiple_of(which * lanes, lanes), lanes)]

    groups = (half + wide) // SUBLANES
    bounds = [groups * piece // PIECES * SUBLANES for piece in range(PIECES + 1)]

    def piece_of(ref, begin, size, piece, target=side):
        at = pl.multiple_of(wide * (1 - target) + bounds[piece], SUBLANES)
        return ref.at[pl.ds(begin, size), pl.ds(at, bounds[piece + 1] - bounds[piece]), :]

    def cut_piece(ref, target, piece):
        at = pl.multiple_of(target * (half - wide) + bounds[piece], SUBLANES)
        return ref.at[:, pl.ds(at, bounds[piece + 1] - bounds[piece]), :]

    rate_own = pltpu.make_async_copy(cut(rate_in, side), spot(rate, side, slab, planes), local.at[0])
    rate_mate = remote(
        lane_half(cut(rate_in, 1 - side), core),
        lane_half(spot(rate, 1 - side, slab, planes), core),
        slot_of["rate"],
        tm,
        mate,
    )
    initial_own = pltpu.make_async_copy(cut(initial, side), spot(start, side, slab, planes), local.at[1])
    guess_own = remote(
        cut(guess, side), spot(start, side, slab, planes), slot_of["start"], tm + 1, space
    )

    def to_mate(ref, to_tm):
        return [
            remote(
                cut_piece(ref, 1 - side, piece),
                piece_of(start, slab, planes, piece, 1 - side),
                slot_of["start"] + 1 + piece,
                to_tm,
                mate,
            )
            for piece in range(PIECES)
        ]

    guess_mate = to_mate(guess, tm + 1)
    initial_mate = to_mate(initial, 0)
    is_last = tm == nt - 1

    rate_mate.start()
    rate_own.start()

    @pl.when(has_next)
    def _():
        guess_own.start()
        for copy in guess_mate:
            copy.start()

    @pl.when(is_last)
    def _():
        for copy in initial_mate:
            copy.start()

    @pl.when(tm == 0)
    def _():
        initial_own.start()

    for ref in (first, second):
        @pl.when(jnp.logical_not(has_low))
        def _(ref=ref):
            ref[0:STEPS] = jnp.zeros((STEPS,) + ref.shape[1:], jnp.float32)

        @pl.when(jnp.logical_not(has_high))
        def _(ref=ref):
            ref[STEPS + block : length] = jnp.zeros((STEPS,) + ref.shape[1:], jnp.float32)

    row = lax.broadcasted_iota(jnp.int32, reach.shape, 0)
    outside = jnp.logical_or(
        jnp.logical_and(side == 0, row < wide), jnp.logical_and(side == 1, row >= wide + half)
    )
    reach[...] = jnp.where(outside, 0.0, fine_diffuse)

    low_place, high_place = STEPS + block, 0

    def edge_pieces(piece):
        slot = slot_of["start_edge"] + 1 + piece
        low = remote(
            piece_of(start, STEPS, STEPS, piece), piece_of(start, low_place, STEPS, piece),
            slot, tm, space - 2,
        )
        high = remote(
            piece_of(start, block, STEPS, piece), piece_of(start, high_place, STEPS, piece),
            slot, tm, space + 2,
        )
        return low, high

    start_edges = [edge_pieces(piece) for piece in range(PIECES)]
    start_low = remote(
        spot(start, side, STEPS, STEPS), spot(start, side, low_place, STEPS),
        slot_of["start_edge"], tm, space - 2,
    )
    start_high = remote(
        spot(start, side, block, STEPS), spot(start, side, high_place, STEPS),
        slot_of["start_edge"], tm, space + 2,
    )
    reach_rate = STEPS - 1
    rate_low_spot = lane_half(spot(rate, side, low_place, reach_rate), core)
    rate_high_spot = lane_half(spot(rate, side, high_place + 1, reach_rate), core)
    rate_low = remote(
        lane_half(spot(rate, side, STEPS, reach_rate), core), rate_low_spot,
        slot_of["rate_edge"], tm, space - 2,
    )
    rate_high = remote(
        lane_half(spot(rate, side, STEPS + block - reach_rate, reach_rate), core), rate_high_spot,
        slot_of["rate_edge"] + 1, tm, space + 2,
    )
    rate_other_spot = lane_half(spot(rate, side, other, planes), core)
    twin_mate = remote(rate_other_spot, rate_other_spot, slot_of["rate_core"], twin, space)
    twin_low = remote(rate_low_spot, rate_low_spot, slot_of["rate_core"] + 1, twin, space)
    twin_high = remote(rate_high_spot, rate_high_spot, slot_of["rate_core"] + 2, twin, space)

    own_low = jnp.logical_and(side == 0, has_low)
    own_high = jnp.logical_and(side == 1, has_high)
    other_low = jnp.logical_and(side == 1, has_low)
    other_high = jnp.logical_and(side == 0, has_high)

    rate_own.wait()
    pl.when(own_low)(rate_low.start)
    pl.when(own_high)(rate_high.start)

    @pl.when(tm == 0)
    def _():
        initial_own.wait()

    @pl.when(has_previous)
    def _():
        guess_own.wait_recv()

    pl.when(own_low)(start_low.start)
    pl.when(own_high)(start_high.start)

    rate_mate.wait_recv()
    pl.when(other_low)(rate_low.start)
    pl.when(other_high)(rate_high.start)
    twin_mate.start()

    for piece in range(PIECES):
        guess_mate[piece].wait_recv()
        pl.when(other_low)(start_edges[piece][0].start)
        pl.when(other_high)(start_edges[piece][1].start)

    @pl.when(has_high)
    def _():
        rate_low.wait_recv()
        twin_low.start()

    @pl.when(has_low)
    def _():
        rate_high.wait_recv()
        twin_high.start()

    twin_mate.wait_recv()
    pl.when(has_high)(twin_low.wait_recv)
    pl.when(has_low)(twin_high.wait_recv)

    @pl.when(jnp.logical_and(side == 0, has_high))
    def _():
        start_low.wait_recv()

    @pl.when(jnp.logical_and(side == 1, has_low))
    def _():
        start_high.wait_recv()

    @pl.when(jnp.logical_and(side == 1, has_high))
    def _():
        for low, high in start_edges:
            low.wait_recv()

    @pl.when(jnp.logical_and(side == 0, has_low))
    def _():
        for low, high in start_edges:
            high.wait_recv()

    keep = pltpu.make_async_copy(start, again, local.at[1])

    @pl.when(tm == 0)
    def _():
        keep.start()

    width = start.shape[2]
    lane = lax.broadcasted_iota(jnp.int32, reach.shape, 1)

    def change(ref, z):
        middle = ref[z]
        beside = ref[z + 1] + ref[z - 1]
        beside = beside + pltpu.roll(middle, 1, 0) + pltpu.roll(middle, rows - 1, 0)
        beside = beside + jnp.where(lane == 0, 0.0, pltpu.roll(middle, 1, 1))
        beside = beside + jnp.where(lane == width - 1, 0.0, pltpu.roll(middle, width - 1, 1))
        growth = rate[z] * (fine_growth - fine_growth * (middle * middle))
        return middle, reach[...] * beside + middle * (growth - 6.0 * fine_diffuse)

    def span(step):
        low = jnp.where(has_low, step, max(step, STEPS))
        high = jnp.where(has_high, length - step, min(length - step, STEPS + block))
        return low, high

    def fine(src, dst, step):
        def plane(z, carry):
            middle, delta = change(src, z)
            dst[z] = middle + delta
            return carry

        lax.fori_loop(*span(step), plane, 0)

    fine(start, first, 1)
    fine(first, second, 2)
    fine(second, relaxed, 3)

    given, given_low, given_high = [], [], []
    for piece in range(PIECES):
        slot = slot_of["again_edge"] + 2 * piece
        given.append(
            remote(
                piece_of(relaxed, STEPS, block, piece),
                piece_of(again, STEPS, block, piece),
                slot_of["again"] + piece,
                tm + 1,
                space,
            )
        )
        given_low.append(
            remote(
                piece_of(again, STEPS, STEPS, piece),
                piece_of(again, STEPS + block, STEPS, piece),
                slot,
                tm,
                space - 2,
            )
        )
        given_high.append(
            remote(
                piece_of(again, block, STEPS, piece),
                piece_of(again, 0, STEPS, piece),
                slot + 1,
                tm,
                space + 2,
            )
        )

    @pl.when(has_next)
    def _():
        for piece in range(PIECES):
            given[piece].start()

    @pl.when(tm == 0)
    def _():
        keep.wait()

    @pl.when(has_previous)
    def _():
        for piece in range(PIECES):
            given[piece].wait_recv()
            pl.when(has_low)(given_low[piece].start)
            pl.when(has_high)(given_high[piece].start)
        for piece in range(PIECES):
            pl.when(has_high)(given_low[piece].wait_recv)
            pl.when(has_low)(given_high[piece].wait_recv)

    def first_plane(z, carry):
        middle, delta = change(again, z)
        first[z] = middle + delta
        coarse[z] = middle + coarse_ratio * delta
        return carry

    lax.fori_loop(*span(1), first_plane, 0)
    fine(first, second, 2)

    order = []
    for depth in range(planes):
        order += [STEPS + depth, STEPS + block - 1 - depth]

    def row_span(z):
        at = pl.multiple_of(wide * (1 - side), SUBLANES)
        return (pl.ds(z, 1), pl.ds(at, half + wide), slice(None))

    passed = {
        z: remote(
            after.at[row_span(z)], before.at[row_span(z)], slot_of["chain"] + z - STEPS, tm + 1, space
        )
        for z in order
    }
    low_edge, high_edge = STEPS, STEPS + block - 1
    passed_low = remote(
        before.at[row_span(low_edge)], before.at[row_span(high_edge + 1)],
        slot_of["chain_edge"], tm, space - 2,
    )
    passed_high = remote(
        before.at[row_span(high_edge)], before.at[row_span(low_edge - 1)],
        slot_of["chain_edge"] + 1, tm, space + 2,
    )

    mine = pl.ds(pl.multiple_of(side * half, SUBLANES), half)
    middle_rows = pl.ds(wide, half)
    defect_stay = pltpu.make_async_copy(
        defect.at[pl.ds(slab, planes), middle_rows, :], defect_out.at[:, mine, :], local.at[2]
    )
    defect_go = remote(
        defect.at[pl.ds(other, planes), middle_rows, :], defect_out.at[:, mine, :],
        slot_of["defect"], tm, mate,
    )
    stay, go = {}, {}
    for z in order:
        place = (z - STEPS) % planes
        src = after.at[pl.ds(z, 1), middle_rows, :]
        dst = corrected_out.at[pl.ds(place, 1), mine, :]
        stay[z] = pltpu.make_async_copy(src, dst, local.at[3 + place])
        go[z] = remote(src, dst, slot_of["corrected"] + place, tm, mate)

    def at_home(z):
        return side == (z - STEPS) // planes

    def hand_in(z):
        pl.when(at_home(z))(stay[z].start)
        pl.when(jnp.logical_not(at_home(z)))(go[z].start)

    def last_plane(z):
        middle, delta = change(second, z)
        end = middle + delta
        defect[z] = end - relaxed[z]
        shift = end - coarse[z]
        offset[z] = shift
        after[z] = coarse[z] + shift

    def take_edges():
        passed[low_edge].wait_recv()
        pl.when(has_low)(passed_low.start)
        passed[high_edge].wait_recv()
        pl.when(has_high)(passed_high.start)

    pl.when(tm == 2)(take_edges)
    opens = jnp.logical_and(tm == 1, has_next)
    for index, z in enumerate(order):
        last_plane(z)
        if index:
            pl.when(opens)(passed[order[index - 1]].start)
    pl.when(opens)(passed[order[-1]].start)
    defect_go.start()
    defect_stay.start()

    later = tm > 1

    @pl.when(jnp.logical_not(later))
    def _():
        for z in order:
            hand_in(z)

    @pl.when(later)
    def _():
        pl.when(tm > 2)(take_edges)
        queue = order[2:]
        waiting = set(queue)

        def leave(z):
            pl.when(has_next)(passed[z].start)
            hand_in(z)

        for index, z in enumerate(order):
            while waiting & {z - 1, z, z + 1}:
                come = queue.pop(0)
                waiting.remove(come)
                passed[come].wait_recv()
            if z == low_edge:
                pl.when(has_low)(passed_high.wait_recv)
            if z == high_edge:
                pl.when(has_high)(passed_low.wait_recv)
            middle, delta = change(before, z)
            after[z] = middle + coarse_ratio * delta + offset[z]
            if index:
                leave(order[index - 1])
        leave(order[-1])
        pl.when(has_low)(passed_low.wait_send)
        pl.when(has_high)(passed_high.wait_send)

    onward = jnp.logical_and(tm > 0, has_next)

    @pl.when(is_last)
    def _():
        for copy in initial_mate:
            copy.wait_send()

    @pl.when(has_next)
    def _():
        guess_own.wait_send()
        for copy in guess_mate:
            copy.wait_send()

    rate_mate.wait_send()
    twin_mate.wait_send()
    pl.when(has_high)(twin_low.wait_send)
    pl.when(has_low)(twin_high.wait_send)
    pl.when(has_low)(rate_low.wait_send)
    pl.when(has_high)(rate_high.wait_send)
    pl.when(own_low)(start_low.wait_send)
    pl.when(own_high)(start_high.wait_send)

    @pl.when(other_low)
    def _():
        for low, high in start_edges:
            low.wait_send()

    @pl.when(other_high)
    def _():
        for low, high in start_edges:
            high.wait_send()

    @pl.when(has_next)
    def _():
        for piece in range(PIECES):
            given[piece].wait_send()

    @pl.when(has_previous)
    def _():
        for piece in range(PIECES):
            pl.when(has_low)(given_low[piece].wait_send)
            pl.when(has_high)(given_high[piece].wait_send)

    @pl.when(onward)
    def _():
        for z in order:
            passed[z].wait_send()

    defect_stay.wait()
    defect_go.wait()
    for z in order:
        pl.when(at_home(z))(stay[z].wait)
        pl.when(at_home(z))(go[z].wait_recv)
        pl.when(jnp.logical_not(at_home(z)))(go[z].wait_send)


def quarter_slots(nt):
    kinds = dict(
        start=nt * HALVES, rate=1, low_start=nt * HALVES, high_start=nt * HALVES, low_rate=1, high_rate=1,
        low_again=nt, high_again=nt, low_first=1, high_first=1, low_offset=nt, high_offset=nt,
        corrected=nt, defect=nt,
    )
    first, total = {}, 0
    for kind, number in kinds.items():
        first[kind] = total
        total += number
    return first, total


def quarter_kernel(
    nt, ns, planes, part, wide, recv_of, recv_total,
    initial, guess, rate_in, corrected_out, defect_out,
    start, again, rate, first, second, coarse, chain, offset, defect, reach,
    send, recv,
):
    tm, space = lax.axis_index("tm"), lax.axis_index("space")
    y, core = lax.div(tm, 2), lax.rem(tm, 2)
    pair, x = lax.div(space, 2), lax.rem(space, 2)
    levels, pairs = nt // 2, ns // 2
    length = planes + 2 * STEPS
    rows = part + 2 * wide
    across, width = initial.shape[1], initial.shape[2]
    low_own, high_own = STEPS, STEPS + planes
    slab = 2 * pair + core
    has_low, has_high = slab > 0, slab < ns - 1
    quarter = 2 * y + x
    low_to = {"tm": tm + 1 - 2 * core, "space": space - 2 * (1 - core)}
    high_to = {"tm": tm + 1 - 2 * core, "space": space + 2 * core}

    def window(which):
        begin = jnp.clip(part * which - wide, 0, across - rows)
        at = begin - part * which + 2 * wide
        return pl.multiple_of(begin, SUBLANES), pl.multiple_of(at, SUBLANES)

    my_begin, my_at = window(quarter)
    body = pl.ds(wide, rows)
    mine = pl.ds(2 * wide, part)

    first_row, last_row = y + x == 0, quarter == nt - 1
    edge_zero = jnp.zeros((length, wide, width), jnp.float32)
    plane_zero = jnp.zeros((STEPS,) + start.shape[2:], jnp.float32)

    def clear_rows(ref, k):
        @pl.when(first_row)
        def _():
            ref[k, :, wide : 2 * wide] = edge_zero

        @pl.when(last_row)
        def _():
            ref[k, :, 2 * wide + part : 3 * wide + part] = edge_zero

    def clear_planes(ref, k):
        @pl.when(jnp.logical_not(has_low))
        def _():
            ref[k, 0:low_own] = plane_zero

        @pl.when(jnp.logical_not(has_high))
        def _():
            ref[k, high_own:length] = plane_zero

    for k in range(nt):
        clear_rows(start, k)
        clear_planes(start, k)
        clear_planes(again, k)
        clear_planes(chain, k)
    clear_rows(rate, 0)
    clear_planes(rate, 0)
    clear_planes(first, 0)
    clear_planes(second, 0)

    barrier = pltpu.get_barrier_semaphore()
    for dy in range(levels):
        for dx in range(2):
            for dc in range(2):
                if dy or dx or dc:
                    there = {
                        "tm": 2 * lax.rem(y + dy, levels) + lax.rem(core + dc, 2),
                        "space": 2 * pair + lax.rem(x + dx, 2),
                    }
                    pl.semaphore_signal(barrier, inc=1, device_id=there, device_id_type=MESH)
    count = jnp.int32(2 * nt - 1)
    for far, there in (
        (jnp.logical_and(core == 0, has_low), low_to),
        (jnp.logical_and(core == 1, has_high), high_to),
    ):

        @pl.when(far)
        def _(there=there):
            pl.semaphore_signal(barrier, inc=1, device_id=there, device_id_type=MESH)

        count = count + far.astype(jnp.int32)
    pl.semaphore_wait(barrier, count)

    sends = []
    send_count = [0]

    def remote(src, dst, slot, there, condition):
        number = send_count[0]
        send_count[0] += 1
        copy = pltpu.make_async_remote_copy(
            src_ref=src, dst_ref=dst, send_sem=send.at[number], recv_sem=recv.at[slot],
            device_id=there, device_id_type=MESH,
        )
        sends.append((copy, condition))
        return copy

    def launch(src, dst, slot, there, condition):
        copy = remote(src, dst, slot, there, condition)
        pl.when(condition)(copy.start)

    def arrive(dst, slot, condition=None):
        copy = pltpu.make_async_copy(dst, dst, recv.at[slot])
        if condition is None:
            copy.wait()
        else:
            pl.when(condition)(copy.wait)

    size = rows // HALVES
    own = pl.ds(low_own, planes)
    home = core == x
    away = jnp.logical_not(home)

    def source(ref, begin, half):
        return ref.at[:, pl.ds(pl.multiple_of(begin + half * size, SUBLANES), size), :]

    def place(ref, k, at, half, zs=own):
        return ref.at[k, zs, pl.ds(pl.multiple_of(at + half * size, SUBLANES), size), :]

    def whole(ref, k, at, zs=own):
        return ref.at[k, zs, pl.ds(at, rows), :]

    @pl.when(home)
    def _():
        pltpu.make_async_copy(
            rate_in.at[:, pl.ds(my_begin, rows), :], whole(rate, 0, my_at), recv.at[recv_of["rate"]]
        ).start()
        for half in range(HALVES):
            pltpu.make_async_copy(
                source(initial, my_begin, half), place(start, 0, my_at, half), recv.at[recv_of["start"] + half]
            ).start()

    rate_level = tm - levels
    gives_rate = rate_level >= 0
    rate_begin, rate_at = window(2 * rate_level + 1 - x)
    launch(
        rate_in.at[:, pl.ds(rate_begin, rows), :], whole(rate, 0, rate_at), recv_of["rate"],
        {"tm": 2 * rate_level + x, "space": space + 1 - 2 * x}, gives_rate,
    )
    there_begin, there_at = window(2 * y + 1 - x)
    for half in range(HALVES):
        launch(
            source(initial, there_begin, half), place(start, 0, there_at, half), recv_of["start"] + half,
            {"tm": 2 * y + x, "space": space + 1 - 2 * x}, core == half % 2,
        )
    gives_guess = tm < nt - 1
    for half in range(HALVES):
        slot = recv_of["start"] + (tm + 1) * HALVES + half
        for dy in range(levels):
            for dx in (1, 0):
                to_y, to_x = lax.rem(y + dy, levels), lax.rem(x + dx, 2)
                begin, at = window(2 * to_y + to_x)
                src, dst = source(guess, begin, half), place(start, tm + 1, at, half)
                there = {"tm": 2 * to_y + x, "space": 2 * pair + to_x}
                if dy or dx:
                    launch(src, dst, slot, there, gives_guess)
                else:
                    launch(src, dst, slot, there, jnp.logical_and(gives_guess, away))

                    @pl.when(jnp.logical_and(gives_guess, home))
                    def _(src=src, dst=dst, slot=slot):
                        pltpu.make_async_copy(src, dst, recv.at[slot]).start()

    row = lax.broadcasted_iota(jnp.int32, reach.shape, 0)
    outside = jnp.logical_or(
        jnp.logical_and(first_row, row < wide), jnp.logical_and(last_row, row >= wide + part)
    )
    reach[...] = jnp.where(outside, 0.0, fine_diffuse)
    lane = lax.broadcasted_iota(jnp.int32, reach.shape, 1)

    def share(src_of, depth, high_slot, low_slot):
        launch(
            src_of(pl.ds(low_own, depth)), src_of(pl.ds(high_own, depth)), high_slot, low_to, has_low
        )
        launch(
            src_of(pl.ds(high_own - depth, depth)), src_of(pl.ds(low_own - depth, depth)), low_slot, high_to, has_high
        )

    def shared(dst_of, depth, high_slot, low_slot):
        arrive(dst_of(pl.ds(high_own, depth)), high_slot, has_high)
        arrive(dst_of(pl.ds(low_own - depth, depth)), low_slot, has_low)

    def start_view(k, half):
        return lambda zs: place(start, k, my_at, half, zs)

    def relay_start(k, half):
        at = k * HALVES + half
        arrive(place(start, k, my_at, half), recv_of["start"] + at)
        share(start_view(k, half), STEPS, recv_of["high_start"] + at, recv_of["low_start"] + at)

    def start_ready(k):
        for half in range(HALVES):
            at = k * HALVES + half
            shared(start_view(k, half), STEPS, recv_of["high_start"] + at, recv_of["low_start"] + at)

    def rate_view(zs):
        return whole(rate, 0, my_at, zs)

    def body_view(ref, k):
        return lambda zs: ref.at[k, zs, body, :]

    def change(ref, k, z):
        middle = ref[k, z, body, :]
        beside = ref[k, z + 1, body, :] + ref[k, z - 1, body, :]
        beside = beside + pltpu.roll(middle, 1, 0) + pltpu.roll(middle, rows - 1, 0)
        beside = beside + jnp.where(lane == 0, 0.0, pltpu.roll(middle, 1, 1))
        beside = beside + jnp.where(lane == width - 1, 0.0, pltpu.roll(middle, width - 1, 1))
        growth = rate[0, z, body, :] * (fine_growth - fine_growth * (middle * middle))
        return middle, reach[...] * beside + middle * (growth - 6.0 * fine_diffuse)

    def span(halo):
        low = jnp.where(has_low, low_own - halo, low_own)
        high = jnp.where(has_high, high_own + halo, high_own)
        return low, high

    def fine(src, source_k, dst, dst_k, halo, rough=False):
        def plane(z, carry):
            middle, delta = change(src, source_k, z)
            dst[dst_k, z, body, :] = middle + delta
            if rough:
                coarse[0, z, body, :] = middle + coarse_ratio * delta
            return carry

        lax.fori_loop(*span(halo), plane, 0)

    def hand_in(ref, k, out, kind, j):
        there_space = 2 * pair + core
        src = ref.at[k, own, mine, :]
        dst = out.at[:, pl.ds(pl.multiple_of(part * quarter, SUBLANES), part), :]
        slot = recv_of[kind] + quarter
        stays = jnp.logical_and(tm == j, home)
        launch(src, dst, slot, {"tm": j, "space": there_space}, jnp.logical_not(stays))

        @pl.when(stays)
        def _():
            pltpu.make_async_copy(src, dst, recv.at[slot]).start()

    def relax(k):
        fine(start, k, first, 0, 2, rough=k == 0)
        fine(first, 0, second, 0, 1)
        if k:
            fine(second, 0, again, k, 0)
            return

        def plane(z, carry):
            middle, delta = change(second, 0, z)
            value = middle + delta
            again[0, z, body, :] = value
            defect[0, z, body, :] = value - value
            base = coarse[0, z, body, :]
            chain[0, z, body, :] = base + (value - base)
            return carry

        lax.fori_loop(low_own, high_own, plane, 0)

    def send_again(k):
        share(body_view(again, k), STEPS, recv_of["high_again"] + k, recv_of["low_again"] + k)

    def finish(k):
        shared(body_view(again, k), STEPS, recv_of["high_again"] + k, recv_of["low_again"] + k)
        fine(again, k, first, 0, 2, rough=True)
        fine(first, 0, second, 0, 1)

        def plane(z, carry):
            middle, delta = change(second, 0, z)
            value = middle + delta
            defect[k + 1, z, body, :] = value - again[k + 1, z, body, :]
            base = coarse[0, z, body, :]
            if k:
                offset[k + 1, z, body, :] = value - base
            else:
                chain[1, z, body, :] = base + (value - base)
            return carry

        lax.fori_loop(low_own, high_own, plane, 0)

    arrive(rate_view(own), recv_of["rate"])
    share(rate_view, STEPS - 1, recv_of["high_rate"], recv_of["low_rate"])
    for half in range(HALVES):
        relay_start(0, half)
    for half in range(HALVES):
        for k in range(1, nt - 1):
            relay_start(k, half)

    shared(rate_view, STEPS - 1, recv_of["high_rate"], recv_of["low_rate"])
    start_ready(0)
    relax(0)
    send_again(0)
    hand_in(chain, 0, corrected_out, "corrected", 0)
    hand_in(defect, 0, defect_out, "defect", 0)
    for half in range(HALVES):
        relay_start(nt - 1, half)
    for k in range(1, nt - 1):
        start_ready(k)
        relax(k)
        send_again(k)

    reaches = nt - 2
    finish(0)
    share(body_view(chain, 1), reaches, recv_of["high_first"], recv_of["low_first"])
    hand_in(chain, 1, corrected_out, "corrected", 1)
    hand_in(defect, 1, defect_out, "defect", 1)
    start_ready(nt - 1)
    relax(nt - 1)
    for k in range(1, nt - 1):
        finish(k)
        j = k + 1
        if nt - 1 - j:
            share(body_view(offset, j), nt - 1 - j, recv_of["high_offset"] + j, recv_of["low_offset"] + j)
        hand_in(defect, j, defect_out, "defect", j)

    shared(body_view(chain, 1), reaches, recv_of["high_first"], recv_of["low_first"])
    for j in range(2, nt):
        halo = nt - 1 - j
        if halo:
            shared(body_view(offset, j), halo, recv_of["high_offset"] + j, recv_of["low_offset"] + j)

        def plane(z, carry, j=j):
            middle, delta = change(chain, j - 1, z)
            chain[j, z, body, :] = middle + coarse_ratio * delta + offset[j, z, body, :]
            return carry

        lax.fori_loop(*span(halo), plane, 0)
        hand_in(chain, j, corrected_out, "corrected", j)

    for copy, condition in sends:
        pl.when(condition)(copy.wait_send)
    for out, kind in ((corrected_out, "corrected"), (defect_out, "defect")):
        for q in range(nt):
            arrive(out.at[:, pl.ds(part * q, part), :], recv_of[kind] + q)


def quarter_device(nt, ns, initial, coarse_guess, react_rate):
    planes, across, width = initial.shape
    part = across // nt
    wide = -(-(2 * STEPS + max(nt - 2, 0)) // SUBLANES) * SUBLANES
    length = planes + 2 * STEPS
    tall = part + 4 * wide
    recv_of, recv_total = quarter_slots(nt)

    def field(number):
        return pltpu.VMEM((number, length, tall, width), jnp.float32)

    shape = jax.ShapeDtypeStruct(initial.shape, jnp.float32)
    corrected, defect = pl.pallas_call(
        functools.partial(quarter_kernel, nt, ns, planes, part, wide, recv_of, recv_total),
        out_shape=(shape, shape),
        in_specs=[pl.BlockSpec(memory_space=pl.ANY)] * 3,
        out_specs=[pl.BlockSpec(memory_space=pl.ANY)] * 2,
        scratch_shapes=[
            field(nt), field(nt), field(1), field(1), field(1), field(1), field(nt), field(nt), field(nt),
            pltpu.VMEM((part + 2 * wide, width), jnp.float32),
            pltpu.SemaphoreType.DMA((200,)),
            pltpu.SemaphoreType.DMA((recv_total,)),
        ],
        compiler_params=pltpu.CompilerParams(collective_id=0, has_side_effects=True),
    )(initial, coarse_guess[0], react_rate)
    return corrected[None], defect[None]


def takes_quarters(nt, planes, across):
    part = across // nt
    wide = -(-(2 * STEPS + max(nt - 2, 0)) // SUBLANES) * SUBLANES
    fits = across % (nt * SUBLANES) == 0 and part + 2 * wide <= across and nt - 2 <= planes
    return nt % 2 == 0 and nt > 2 and planes >= STEPS and fits


def on_device(nt, ns, initial, coarse_guess, react_rate):
    planes, across, width = initial.shape
    if takes_quarters(nt, planes, across):
        return quarter_device(nt, ns, initial, coarse_guess, react_rate)
    half = across // 2
    wide = -(-(2 * STEPS + max(nt - 2, 0)) // SUBLANES) * SUBLANES
    length = 2 * planes + 2 * STEPS
    field = pltpu.VMEM((length, half + 2 * wide, width), jnp.float32)
    slot_of, total = slots(planes)
    shape = jax.ShapeDtypeStruct(initial.shape, jnp.float32)
    corrected, defect = pl.pallas_call(
        functools.partial(kernel, nt, ns, planes, half, wide, slot_of),
        out_shape=(shape, shape),
        in_specs=[pl.BlockSpec(memory_space=pl.ANY)] * 3,
        out_specs=[pl.BlockSpec(memory_space=pl.ANY)] * 2,
        scratch_shapes=[field] * 11
        + [
            pltpu.VMEM((half + 2 * wide, width), jnp.float32),
            pltpu.SemaphoreType.DMA((total,)),
            pltpu.SemaphoreType.DMA((total,)),
            pltpu.SemaphoreType.DMA((3 + planes,)),
        ],
        compiler_params=pltpu.CompilerParams(collective_id=0, has_side_effects=True),
    )(initial, coarse_guess[0], react_rate)
    return corrected[None], defect[None]


def solution(mesh):
    in_specs = (P("space", None, None), P("tm", "space", None, None), P("space", None, None))
    out_specs = (P("tm", "space", None, None), P("tm", "space", None, None))
    return jax.shard_map(
        functools.partial(on_device, mesh.shape["tm"], mesh.shape["space"]),
        mesh=mesh, in_specs=in_specs, out_specs=out_specs, check_vma=False,
    )
```

```python
import functools

import jax
import jax.numpy as jnp
from jax import lax
from jax.experimental import pallas as pl
from jax.experimental.pallas import tpu as pltpu
from jax.sharding import PartitionSpec as P

STEPS = 3
SUBLANES = 8

fine_diffuse = 0.04
fine_growth = 0.05
coarse_ratio = 4.0

MESH = pl.DeviceIdType.MESH

PIECES = 4
SHARES = 4
VMEM_BYTES = 40 << 20


def slots(planes):
    kinds = dict(
        start=2 + PIECES, start_edge=1 + PIECES, rate=1, rate_edge=2, rate_core=3, again=PIECES, again_edge=2 * PIECES,
        chain=2 * planes, chain_edge=2, defect=1, corrected=planes,
    )
    first, total = {}, 0
    for kind, number in kinds.items():
        first[kind] = total
        total += number
    return first, total


def kernel(
    nt, ns, planes, half, wide, slot_of,
    initial, guess, rate_in, corrected_out, defect_out,
    start, rate, again, before, first, second, relaxed, coarse, offset, defect, after, reach,
    send, recv, local,
):
    tm, space = lax.axis_index("tm"), lax.axis_index("space")
    pair, side = lax.div(space, 2), lax.rem(space, 2)
    pairs = ns // 2
    mate = space + 1 - 2 * side
    block = 2 * planes
    length = block + 2 * STEPS
    rows = half + 2 * wide
    has_low, has_high = pair > 0, pair < pairs - 1
    has_next, has_previous = tm < nt - 1, tm > 0
    own = pl.ds(STEPS, block)

    for ref in (start, rate, again, before):
        zero_plane = jnp.zeros((STEPS,) + ref.shape[1:], jnp.float32)
        zero_rows = jnp.zeros((block, wide, ref.shape[2]), jnp.float32)
        ref[0:STEPS] = zero_plane
        ref[STEPS + block : length] = zero_plane
        ref[STEPS : STEPS + block, 0:wide] = zero_rows
        ref[STEPS : STEPS + block, wide + half : rows] = zero_rows

    barrier = pltpu.get_barrier_semaphore()
    count = jnp.int32(0)
    for step in (-1, 0, 1):
        for place in ("own", "mate", "low", "high"):
            if step == 0 and place == "own":
                continue
            there = {"own": space, "mate": mate, "low": space - 2, "high": space + 2}[place]
            tests = []
            if step:
                tests.append(has_next if step > 0 else has_previous)
            if place in ("low", "high"):
                tests.append(has_low if place == "low" else has_high)
            target = {"tm": tm + step, "space": there}
            if tests:
                valid = functools.reduce(jnp.logical_and, tests)

                @pl.when(valid)
                def _(target=target):
                    pl.semaphore_signal(barrier, inc=1, device_id=target, device_id_type=MESH)

                count = count + valid.astype(jnp.int32)
            else:
                pl.semaphore_signal(barrier, inc=1, device_id=target, device_id_type=MESH)
                count = count + 1
    for here, there in ((tm == 0, nt - 1), (tm == nt - 1, 0)):

        @pl.when(here)
        def _(there=there):
            pl.semaphore_signal(
                barrier, inc=1, device_id={"tm": there, "space": mate}, device_id_type=MESH
            )

        count = count + here.astype(jnp.int32)
    pl.semaphore_wait(barrier, count)

    def remote(src, dst, slot, to_tm, to_space):
        return pltpu.make_async_remote_copy(
            src_ref=src,
            dst_ref=dst,
            send_sem=send.at[slot],
            recv_sem=recv.at[slot],
            device_id={"tm": to_tm, "space": to_space},
            device_id_type=MESH,
        )

    def cut(ref, target):
        return ref.at[:, pl.ds(pl.multiple_of(target * (half - wide), SUBLANES), half + wide), :]

    def spot(ref, target, begin, size):
        at = pl.multiple_of(wide * (1 - target), SUBLANES)
        return ref.at[pl.ds(begin, size), pl.ds(at, half + wide), :]

    slab = STEPS + planes * side
    other = STEPS + planes * (1 - side)

    core = lax.rem(tm, 2)
    twin = tm + 1 - 2 * core
    lanes = start.shape[2] // 2

    def lane_half(ref, which):
        return ref.at[:, :, pl.ds(pl.multiple_of(which * lanes, lanes), lanes)]

    groups = (half + wide) // SUBLANES
    bounds = [groups * piece // PIECES * SUBLANES for piece in range(PIECES + 1)]

    def piece_of(ref, begin, size, piece, target=side):
        at = pl.multiple_of(wide * (1 - target) + bounds[piece], SUBLANES)
        return ref.at[pl.ds(begin, size), pl.ds(at, bounds[piece + 1] - bounds[piece]), :]

    def cut_piece(ref, target, piece):
        at = pl.multiple_of(target * (half - wide) + bounds[piece], SUBLANES)
        return ref.at[:, pl.ds(at, bounds[piece + 1] - bounds[piece]), :]

    rate_own = pltpu.make_async_copy(cut(rate_in, side), spot(rate, side, slab, planes), local.at[0])
    rate_mate = remote(
        lane_half(cut(rate_in, 1 - side), core),
        lane_half(spot(rate, 1 - side, slab, planes), core),
        slot_of["rate"],
        tm,
        mate,
    )
    initial_own = pltpu.make_async_copy(cut(initial, side), spot(start, side, slab, planes), local.at[1])
    guess_own = remote(
        cut(guess, side), spot(start, side, slab, planes), slot_of["start"], tm + 1, space
    )

    def to_mate(ref, to_tm):
        return [
            remote(
                cut_piece(ref, 1 - side, piece),
                piece_of(start, slab, planes, piece, 1 - side),
                slot_of["start"] + 1 + piece,
                to_tm,
                mate,
            )
            for piece in range(PIECES)
        ]

    guess_mate = to_mate(guess, tm + 1)
    initial_mate = to_mate(initial, 0)
    is_last = tm == nt - 1

    rate_mate.start()
    rate_own.start()

    @pl.when(has_next)
    def _():
        guess_own.start()
        for copy in guess_mate:
            copy.start()

    @pl.when(is_last)
    def _():
        for copy in initial_mate:
            copy.start()

    @pl.when(tm == 0)
    def _():
        initial_own.start()

    for ref in (first, second):
        @pl.when(jnp.logical_not(has_low))
        def _(ref=ref):
            ref[0:STEPS] = jnp.zeros((STEPS,) + ref.shape[1:], jnp.float32)

        @pl.when(jnp.logical_not(has_high))
        def _(ref=ref):
            ref[STEPS + block : length] = jnp.zeros((STEPS,) + ref.shape[1:], jnp.float32)

    row = lax.broadcasted_iota(jnp.int32, reach.shape, 0)
    outside = jnp.logical_or(
        jnp.logical_and(side == 0, row < wide), jnp.logical_and(side == 1, row >= wide + half)
    )
    reach[...] = jnp.where(outside, 0.0, fine_diffuse)

    low_place, high_place = STEPS + block, 0

    def edge_pieces(piece):
        slot = slot_of["start_edge"] + 1 + piece
        low = remote(
            piece_of(start, STEPS, STEPS, piece), piece_of(start, low_place, STEPS, piece),
            slot, tm, space - 2,
        )
        high = remote(
            piece_of(start, block, STEPS, piece), piece_of(start, high_place, STEPS, piece),
            slot, tm, space + 2,
        )
        return low, high

    start_edges = [edge_pieces(piece) for piece in range(PIECES)]
    start_low = remote(
        spot(start, side, STEPS, STEPS), spot(start, side, low_place, STEPS),
        slot_of["start_edge"], tm, space - 2,
    )
    start_high = remote(
        spot(start, side, block, STEPS), spot(start, side, high_place, STEPS),
        slot_of["start_edge"], tm, space + 2,
    )
    reach_rate = STEPS - 1
    rate_low_spot = lane_half(spot(rate, side, low_place, reach_rate), core)
    rate_high_spot = lane_half(spot(rate, side, high_place + 1, reach_rate), core)
    rate_low = remote(
        lane_half(spot(rate, side, STEPS, reach_rate), core), rate_low_spot,
        slot_of["rate_edge"], tm, space - 2,
    )
    rate_high = remote(
        lane_half(spot(rate, side, STEPS + block - reach_rate, reach_rate), core), rate_high_spot,
        slot_of["rate_edge"] + 1, tm, space + 2,
    )
    rate_other_spot = lane_half(spot(rate, side, other, planes), core)
    twin_mate = remote(rate_other_spot, rate_other_spot, slot_of["rate_core"], twin, space)
    twin_low = remote(rate_low_spot, rate_low_spot, slot_of["rate_core"] + 1, twin, space)
    twin_high = remote(rate_high_spot, rate_high_spot, slot_of["rate_core"] + 2, twin, space)

    own_low = jnp.logical_and(side == 0, has_low)
    own_high = jnp.logical_and(side == 1, has_high)
    other_low = jnp.logical_and(side == 1, has_low)
    other_high = jnp.logical_and(side == 0, has_high)

    rate_own.wait()
    pl.when(own_low)(rate_low.start)
    pl.when(own_high)(rate_high.start)

    @pl.when(tm == 0)
    def _():
        initial_own.wait()

    @pl.when(has_previous)
    def _():
        guess_own.wait_recv()

    pl.when(own_low)(start_low.start)
    pl.when(own_high)(start_high.start)

    rate_mate.wait_recv()
    pl.when(other_low)(rate_low.start)
    pl.when(other_high)(rate_high.start)
    twin_mate.start()

    for piece in range(PIECES):
        guess_mate[piece].wait_recv()
        pl.when(other_low)(start_edges[piece][0].start)
        pl.when(other_high)(start_edges[piece][1].start)

    @pl.when(has_high)
    def _():
        rate_low.wait_recv()
        twin_low.start()

    @pl.when(has_low)
    def _():
        rate_high.wait_recv()
        twin_high.start()

    twin_mate.wait_recv()
    pl.when(has_high)(twin_low.wait_recv)
    pl.when(has_low)(twin_high.wait_recv)

    @pl.when(jnp.logical_and(side == 0, has_high))
    def _():
        start_low.wait_recv()

    @pl.when(jnp.logical_and(side == 1, has_low))
    def _():
        start_high.wait_recv()

    @pl.when(jnp.logical_and(side == 1, has_high))
    def _():
        for low, high in start_edges:
            low.wait_recv()

    @pl.when(jnp.logical_and(side == 0, has_low))
    def _():
        for low, high in start_edges:
            high.wait_recv()

    keep = pltpu.make_async_copy(start, again, local.at[1])

    @pl.when(tm == 0)
    def _():
        keep.start()

    width = start.shape[2]
    lane = lax.broadcasted_iota(jnp.int32, reach.shape, 1)

    def change(ref, z):
        middle = ref[z]
        beside = ref[z + 1] + ref[z - 1]
        beside = beside + pltpu.roll(middle, 1, 0) + pltpu.roll(middle, rows - 1, 0)
        beside = beside + jnp.where(lane == 0, 0.0, pltpu.roll(middle, 1, 1))
        beside = beside + jnp.where(lane == width - 1, 0.0, pltpu.roll(middle, width - 1, 1))
        growth = rate[z] * (fine_growth - fine_growth * (middle * middle))
        return middle, reach[...] * beside + middle * (growth - 6.0 * fine_diffuse)

    def span(step):
        low = jnp.where(has_low, step, max(step, STEPS))
        high = jnp.where(has_high, length - step, min(length - step, STEPS + block))
        return low, high

    def fine(src, dst, step):
        def plane(z, carry):
            middle, delta = change(src, z)
            dst[z] = middle + delta
            return carry

        lax.fori_loop(*span(step), plane, 0)

    fine(start, first, 1)
    fine(first, second, 2)
    fine(second, relaxed, 3)

    given, given_low, given_high = [], [], []
    for piece in range(PIECES):
        slot = slot_of["again_edge"] + 2 * piece
        given.append(
            remote(
                piece_of(relaxed, STEPS, block, piece),
                piece_of(again, STEPS, block, piece),
                slot_of["again"] + piece,
                tm + 1,
                space,
            )
        )
        given_low.append(
            remote(
                piece_of(again, STEPS, STEPS, piece),
                piece_of(again, STEPS + block, STEPS, piece),
                slot,
                tm,
                space - 2,
            )
        )
        given_high.append(
            remote(
                piece_of(again, block, STEPS, piece),
                piece_of(again, 0, STEPS, piece),
                slot + 1,
                tm,
                space + 2,
            )
        )

    @pl.when(has_next)
    def _():
        for piece in range(PIECES):
            given[piece].start()

    @pl.when(tm == 0)
    def _():
        keep.wait()

    @pl.when(has_previous)
    def _():
        for piece in range(PIECES):
            given[piece].wait_recv()
            pl.when(has_low)(given_low[piece].start)
            pl.when(has_high)(given_high[piece].start)
        for piece in range(PIECES):
            pl.when(has_high)(given_low[piece].wait_recv)
            pl.when(has_low)(given_high[piece].wait_recv)

    def first_plane(z, carry):
        middle, delta = change(again, z)
        first[z] = middle + delta
        coarse[z] = middle + coarse_ratio * delta
        return carry

    lax.fori_loop(*span(1), first_plane, 0)
    fine(first, second, 2)

    order = []
    for depth in range(planes):
        order += [STEPS + depth, STEPS + block - 1 - depth]

    def row_span(z):
        at = pl.multiple_of(wide * (1 - side), SUBLANES)
        return (pl.ds(z, 1), pl.ds(at, half + wide), slice(None))

    passed = {
        z: remote(
            after.at[row_span(z)], before.at[row_span(z)], slot_of["chain"] + z - STEPS, tm + 1, space
        )
        for z in order
    }
    low_edge, high_edge = STEPS, STEPS + block - 1
    passed_low = remote(
        before.at[row_span(low_edge)], before.at[row_span(high_edge + 1)],
        slot_of["chain_edge"], tm, space - 2,
    )
    passed_high = remote(
        before.at[row_span(high_edge)], before.at[row_span(low_edge - 1)],
        slot_of["chain_edge"] + 1, tm, space + 2,
    )

    mine = pl.ds(pl.multiple_of(side * half, SUBLANES), half)
    middle_rows = pl.ds(wide, half)
    defect_stay = pltpu.make_async_copy(
        defect.at[pl.ds(slab, planes), middle_rows, :], defect_out.at[:, mine, :], local.at[2]
    )
    defect_go = remote(
        defect.at[pl.ds(other, planes), middle_rows, :], defect_out.at[:, mine, :],
        slot_of["defect"], tm, mate,
    )
    stay, go = {}, {}
    for z in order:
        place = (z - STEPS) % planes
        src = after.at[pl.ds(z, 1), middle_rows, :]
        dst = corrected_out.at[pl.ds(place, 1), mine, :]
        stay[z] = pltpu.make_async_copy(src, dst, local.at[3 + place])
        go[z] = remote(src, dst, slot_of["corrected"] + place, tm, mate)

    def at_home(z):
        return side == (z - STEPS) // planes

    def hand_in(z):
        pl.when(at_home(z))(stay[z].start)
        pl.when(jnp.logical_not(at_home(z)))(go[z].start)

    def last_plane(z):
        middle, delta = change(second, z)
        end = middle + delta
        defect[z] = end - relaxed[z]
        shift = end - coarse[z]
        offset[z] = shift
        after[z] = coarse[z] + shift

    def take_edges():
        passed[low_edge].wait_recv()
        pl.when(has_low)(passed_low.start)
        passed[high_edge].wait_recv()
        pl.when(has_high)(passed_high.start)

    pl.when(tm == 2)(take_edges)
    opens = jnp.logical_and(tm == 1, has_next)
    for index, z in enumerate(order):
        last_plane(z)
        if index:
            pl.when(opens)(passed[order[index - 1]].start)
    pl.when(opens)(passed[order[-1]].start)
    defect_go.start()
    defect_stay.start()

    later = tm > 1

    @pl.when(jnp.logical_not(later))
    def _():
        for z in order:
            hand_in(z)

    @pl.when(later)
    def _():
        pl.when(tm > 2)(take_edges)
        queue = order[2:]
        waiting = set(queue)

        def leave(z):
            pl.when(has_next)(passed[z].start)
            hand_in(z)

        for index, z in enumerate(order):
            while waiting & {z - 1, z, z + 1}:
                come = queue.pop(0)
                waiting.remove(come)
                passed[come].wait_recv()
            if z == low_edge:
                pl.when(has_low)(passed_high.wait_recv)
            if z == high_edge:
                pl.when(has_high)(passed_low.wait_recv)
            middle, delta = change(before, z)
            after[z] = middle + coarse_ratio * delta + offset[z]
            if index:
                leave(order[index - 1])
        leave(order[-1])
        pl.when(has_low)(passed_low.wait_send)
        pl.when(has_high)(passed_high.wait_send)

    onward = jnp.logical_and(tm > 0, has_next)

    @pl.when(is_last)
    def _():
        for copy in initial_mate:
            copy.wait_send()

    @pl.when(has_next)
    def _():
        guess_own.wait_send()
        for copy in guess_mate:
            copy.wait_send()

    rate_mate.wait_send()
    twin_mate.wait_send()
    pl.when(has_high)(twin_low.wait_send)
    pl.when(has_low)(twin_high.wait_send)
    pl.when(has_low)(rate_low.wait_send)
    pl.when(has_high)(rate_high.wait_send)
    pl.when(own_low)(start_low.wait_send)
    pl.when(own_high)(start_high.wait_send)

    @pl.when(other_low)
    def _():
        for low, high in start_edges:
            low.wait_send()

    @pl.when(other_high)
    def _():
        for low, high in start_edges:
            high.wait_send()

    @pl.when(has_next)
    def _():
        for piece in range(PIECES):
            given[piece].wait_send()

    @pl.when(has_previous)
    def _():
        for piece in range(PIECES):
            pl.when(has_low)(given_low[piece].wait_send)
            pl.when(has_high)(given_high[piece].wait_send)

    @pl.when(onward)
    def _():
        for z in order:
            passed[z].wait_send()

    defect_stay.wait()
    defect_go.wait()
    for z in order:
        pl.when(at_home(z))(stay[z].wait)
        pl.when(at_home(z))(go[z].wait_recv)
        pl.when(jnp.logical_not(at_home(z)))(go[z].wait_send)


def quarter_slots(nt):
    kinds = dict(
        start=nt * SHARES, rate=SHARES, low_start=nt * SHARES, high_start=nt * SHARES,
        low_rate=SHARES, high_rate=SHARES,
        low_again=nt, high_again=nt, low_first=1, high_first=1, low_offset=nt, high_offset=nt,
        corrected=nt, defect=nt,
    )
    first, total = {}, 0
    for kind, number in kinds.items():
        first[kind] = total
        total += number
    return first, total


def quarter_kernel(
    nt, ns, planes, part, wide, recv_of, recv_total,
    initial, guess, rate_in, corrected_out, defect_out,
    start, again, rate, first, second, coarse, chain, offset, defect, end, reach,
    send, recv,
):
    tm, space = lax.axis_index("tm"), lax.axis_index("space")
    y, core = lax.div(tm, 2), lax.rem(tm, 2)
    pair, x = lax.div(space, 2), lax.rem(space, 2)
    levels, pairs = nt // 2, ns // 2
    length = planes + 2 * STEPS
    rows = part + 2 * wide
    across, width = initial.shape[1], initial.shape[2]
    low_own, high_own = STEPS, STEPS + planes
    slab = 2 * pair + core
    has_low, has_high = slab > 0, slab < ns - 1
    quarter = 2 * y + x
    low_to = {"tm": tm + 1 - 2 * core, "space": space - 2 * (1 - core)}
    high_to = {"tm": tm + 1 - 2 * core, "space": space + 2 * core}

    def window(which):
        begin = jnp.clip(part * which - wide, 0, across - rows)
        at = begin - part * which + 2 * wide
        return pl.multiple_of(begin, SUBLANES), pl.multiple_of(at, SUBLANES)

    my_begin, my_at = window(quarter)
    body = pl.ds(wide, rows)
    mine = pl.ds(2 * wide, part)

    first_row, last_row = y + x == 0, quarter == nt - 1
    edge_zero = jnp.zeros((length, wide, width), jnp.float32)
    plane_zero = jnp.zeros((STEPS,) + start.shape[2:], jnp.float32)

    def clear_rows(ref, k):
        @pl.when(first_row)
        def _():
            ref[k, :, wide : 2 * wide] = edge_zero

        @pl.when(last_row)
        def _():
            ref[k, :, 2 * wide + part : 3 * wide + part] = edge_zero

    def clear_planes(ref, k):
        @pl.when(jnp.logical_not(has_low))
        def _():
            ref[k, 0:low_own] = plane_zero

        @pl.when(jnp.logical_not(has_high))
        def _():
            ref[k, high_own:length] = plane_zero

    barrier = pltpu.get_barrier_semaphore()
    for dy in range(levels):
        for dx in range(2):
            for dc in range(2):
                if dy or dx or dc:
                    there = {
                        "tm": 2 * lax.rem(y + dy, levels) + lax.rem(core + dc, 2),
                        "space": 2 * pair + lax.rem(x + dx, 2),
                    }
                    pl.semaphore_signal(barrier, inc=1, device_id=there, device_id_type=MESH)
    count = jnp.int32(2 * nt - 1)
    for far, there in (
        (jnp.logical_and(core == 0, has_low), low_to),
        (jnp.logical_and(core == 1, has_high), high_to),
    ):

        @pl.when(far)
        def _(there=there):
            pl.semaphore_signal(barrier, inc=1, device_id=there, device_id_type=MESH)

        count = count + far.astype(jnp.int32)

    for k in range(nt):
        clear_rows(start, k)
        clear_planes(start, k)
        clear_planes(again, k)
        clear_planes(chain, k)
    clear_rows(rate, 0)
    clear_planes(rate, 0)
    clear_planes(first, 0)
    clear_planes(second, 0)

    pl.semaphore_wait(barrier, count)

    sends = []
    send_count = [0]

    def remote(src, dst, slot, there, condition):
        number = send_count[0]
        send_count[0] += 1
        copy = pltpu.make_async_remote_copy(
            src_ref=src, dst_ref=dst, send_sem=send.at[number], recv_sem=recv.at[slot],
            device_id=there, device_id_type=MESH,
        )
        sends.append((copy, condition))
        return copy

    def launch(src, dst, slot, there, condition):
        copy = remote(src, dst, slot, there, condition)
        pl.when(condition)(copy.start)

    def arrive(dst, slot, condition=None):
        copy = pltpu.make_async_copy(dst, dst, recv.at[slot])
        if condition is None:
            copy.wait()
        else:
            pl.when(condition)(copy.wait)

    size = rows // SHARES
    own = pl.ds(low_own, planes)
    home = core == x
    away = jnp.logical_not(home)

    def source(ref, begin, share_at):
        return ref.at[:, pl.ds(pl.multiple_of(begin + share_at * size, SUBLANES), size), :]

    def place(ref, k, at, share_at, zs=own):
        return ref.at[k, zs, pl.ds(pl.multiple_of(at + share_at * size, SUBLANES), size), :]

    @pl.when(home)
    def _():
        for ref, k, src, kind in ((start, 0, initial, "start"), (rate, 0, rate_in, "rate")):
            for share_at in range(SHARES):
                pltpu.make_async_copy(
                    source(src, my_begin, share_at), place(ref, k, my_at, share_at), recv.at[recv_of[kind] + share_at]
                ).start()

    there_begin, there_at = window(2 * y + 1 - x)
    for share_at in range(SHARES):
        launch(
            source(initial, there_begin, share_at), place(start, 0, there_at, share_at),
            recv_of["start"] + share_at, {"tm": 2 * y + x, "space": space + 1 - 2 * x}, core == share_at % 2,
        )
    for to_y in range(levels):
        begin, at = window(2 * to_y + 1 - x)
        for share_at in range(SHARES):
            launch(
                source(rate_in, begin, share_at), place(rate, 0, at, share_at), recv_of["rate"] + share_at,
                {"tm": 2 * to_y + x, "space": space + 1 - 2 * x},
                jnp.logical_and(y == levels - 1, core == share_at % 2),
            )

    def give_guess(turn):
        gives = jnp.logical_and(tm < nt - 1, core == turn)
        for share_at in range(SHARES):
            slot = recv_of["start"] + (tm + 1) * SHARES + share_at
            for dy in range(levels):
                for dx in (1, 0):
                    to_y, to_x = lax.rem(y + dy, levels), lax.rem(x + dx, 2)
                    begin, at = window(2 * to_y + to_x)
                    src, dst = source(guess, begin, share_at), place(start, tm + 1, at, share_at)
                    there = {"tm": 2 * to_y + x, "space": 2 * pair + to_x}
                    if dy or dx:
                        launch(src, dst, slot, there, gives)
                    else:
                        launch(src, dst, slot, there, jnp.logical_and(gives, away))

                        @pl.when(jnp.logical_and(gives, home))
                        def _(src=src, dst=dst, slot=slot):
                            pltpu.make_async_copy(src, dst, recv.at[slot]).start()

    give_guess(0)

    row = lax.broadcasted_iota(jnp.int32, reach.shape, 0)
    outside = jnp.logical_or(
        jnp.logical_and(first_row, row < wide), jnp.logical_and(last_row, row >= wide + part)
    )
    reach[...] = jnp.where(outside, 0.0, fine_diffuse)
    lane = lax.broadcasted_iota(jnp.int32, reach.shape, 1)

    def share(src_of, depth, high_slot, low_slot):
        launch(
            src_of(pl.ds(low_own, depth)), src_of(pl.ds(high_own, depth)), high_slot, low_to, has_low
        )
        launch(
            src_of(pl.ds(high_own - depth, depth)), src_of(pl.ds(low_own - depth, depth)), low_slot, high_to, has_high
        )

    def shared(dst_of, depth, high_slot, low_slot):
        arrive(dst_of(pl.ds(high_own, depth)), high_slot, has_high)
        arrive(dst_of(pl.ds(low_own - depth, depth)), low_slot, has_low)

    def start_view(k, share_at):
        return lambda zs: place(start, k, my_at, share_at, zs)

    def relay_start(k):
        for share_at in range(SHARES):
            at = k * SHARES + share_at
            arrive(place(start, k, my_at, share_at), recv_of["start"] + at)
            share(start_view(k, share_at), STEPS, recv_of["high_start"] + at, recv_of["low_start"] + at)

    def start_ready(k):
        for share_at in range(SHARES):
            at = k * SHARES + share_at
            shared(start_view(k, share_at), STEPS, recv_of["high_start"] + at, recv_of["low_start"] + at)

    def rate_view(share_at):
        return lambda zs: place(rate, 0, my_at, share_at, zs)

    def relay_rate():
        for at in range(SHARES):
            arrive(place(rate, 0, my_at, at), recv_of["rate"] + at)
            share(rate_view(at), STEPS - 1, recv_of["high_rate"] + at, recv_of["low_rate"] + at)

    def rate_ready():
        for at in range(SHARES):
            shared(rate_view(at), STEPS - 1, recv_of["high_rate"] + at, recv_of["low_rate"] + at)

    def body_view(ref, k):
        return lambda zs: ref.at[k, zs, body, :]

    def change(ref, k, z):
        middle = ref[k, z, body, :]
        beside = ref[k, z + 1, body, :] + ref[k, z - 1, body, :]
        beside = beside + pltpu.roll(middle, 1, 0) + pltpu.roll(middle, rows - 1, 0)
        beside = beside + jnp.where(lane == 0, 0.0, pltpu.roll(middle, 1, 1))
        beside = beside + jnp.where(lane == width - 1, 0.0, pltpu.roll(middle, width - 1, 1))
        growth = rate[0, z, body, :] * (fine_growth - fine_growth * (middle * middle))
        return middle, reach[...] * beside + middle * (growth - 6.0 * fine_diffuse)

    def span(halo):
        low = jnp.where(has_low, low_own - halo, low_own)
        high = jnp.where(has_high, high_own + halo, high_own)
        return low, high

    def fine(src, source_k, dst, dst_k, halo, rough=False):
        def plane(z, carry):
            middle, delta = change(src, source_k, z)
            dst[dst_k, z, body, :] = middle + delta
            if rough:
                coarse[0, z, body, :] = middle + coarse_ratio * delta
            return carry

        lax.fori_loop(*span(halo), plane, 0)

    def hand_in(ref, k, out, kind, j):
        there_space = 2 * pair + core
        src = ref.at[k, own, mine, :]
        dst = out.at[:, pl.ds(pl.multiple_of(part * quarter, SUBLANES), part), :]
        slot = recv_of[kind] + quarter
        stays = jnp.logical_and(tm == j, home)
        launch(src, dst, slot, {"tm": j, "space": there_space}, jnp.logical_not(stays))

        @pl.when(stays)
        def _():
            pltpu.make_async_copy(src, dst, recv.at[slot]).start()

    def relax(k):
        fine(start, k, first, 0, 2, rough=k == 0)
        fine(first, 0, second, 0, 1)

        def plane(z, carry):
            middle, delta = change(second, 0, z)
            value = middle + delta
            if k == nt - 1:
                defect[k, z, body, :] = end[0, z, body, :] - value
                return carry
            again[k, z, body, :] = value
            if k == 0:
                defect[0, z, body, :] = value - value
                base = coarse[0, z, body, :]
                chain[0, z, body, :] = base + (value - base)
            return carry

        lax.fori_loop(low_own, high_own, plane, 0)

    def send_again(k):
        share(body_view(again, k), STEPS, recv_of["high_again"] + k, recv_of["low_again"] + k)

    def finish(k):
        shared(body_view(again, k), STEPS, recv_of["high_again"] + k, recv_of["low_again"] + k)
        fine(again, k, first, 0, 2, rough=True)
        fine(first, 0, second, 0, 1)

        def plane(z, carry):
            middle, delta = change(second, 0, z)
            value = middle + delta
            if k + 1 < nt - 1:
                defect[k + 1, z, body, :] = value - again[k + 1, z, body, :]
            else:
                end[0, z, body, :] = value
            base = coarse[0, z, body, :]
            if k:
                offset[k + 1, z, body, :] = value - base
            else:
                chain[1, z, body, :] = base + (value - base)
            return carry

        lax.fori_loop(low_own, high_own, plane, 0)

    def lift_between(j, low, high):
        def plane(z, carry):
            middle, delta = change(chain, j - 1, z)
            chain[j, z, body, :] = middle + coarse_ratio * delta + offset[j, z, body, :]
            return carry

        lax.fori_loop(low, high, plane, 0)

    def edges_of(j):
        slots = recv_of["high_offset"] + j, recv_of["low_offset"] + j
        return body_view(offset, j), nt - 1 - j, *slots

    def lift_around(j):
        if nt - 1 - j:
            shared(*edges_of(j))
            low, high = span(nt - 1 - j)
            lift_between(j, low, low_own)
            lift_between(j, high_own, high)

    relay_start(0)
    relay_rate()
    give_guess(1)
    relay_start(1)
    start_ready(0)
    rate_ready()
    relax(0)
    send_again(0)
    hand_in(chain, 0, corrected_out, "corrected", 0)
    hand_in(defect, 0, defect_out, "defect", 0)
    relay_start(2)
    start_ready(1)
    relax(1)
    send_again(1)
    finish(0)
    first_edges = body_view(chain, 1), nt - 2, recv_of["high_first"], recv_of["low_first"]
    share(*first_edges)
    hand_in(chain, 1, corrected_out, "corrected", 1)
    hand_in(defect, 1, defect_out, "defect", 1)
    for j in range(2, nt):
        if j < nt - 1:
            start_ready(j)
            relax(j)
            send_again(j)
        if j + 1 < nt:
            relay_start(j + 1)
        finish(j - 1)
        if j < nt - 1:
            hand_in(defect, j, defect_out, "defect", j)
            share(*edges_of(j))
        if j == 2:
            shared(*first_edges)
        else:
            lift_around(j - 1)
        lift_between(j, low_own, high_own)
        hand_in(chain, j, corrected_out, "corrected", j)
    start_ready(nt - 1)
    relax(nt - 1)
    hand_in(defect, nt - 1, defect_out, "defect", nt - 1)

    for copy, condition in sends:
        pl.when(condition)(copy.wait_send)
    for out, kind in ((corrected_out, "corrected"), (defect_out, "defect")):
        for q in range(nt):
            arrive(out.at[:, pl.ds(part * q, part), :], recv_of[kind] + q)


def settle_kernel(corrected, defect, corrected_out, defect_out, local):
    copies = (
        pltpu.make_async_copy(corrected, corrected_out.at[0], local.at[0]),
        pltpu.make_async_copy(defect, defect_out.at[0], local.at[1]),
    )
    for copy in copies:
        copy.start()
    for copy in copies:
        copy.wait()


def settle(corrected, defect):
    shape = jax.ShapeDtypeStruct((1,) + corrected.shape, jnp.float32)
    return pl.pallas_call(
        settle_kernel,
        out_shape=(shape, shape),
        in_specs=[pl.BlockSpec(memory_space=pl.ANY)] * 2,
        out_specs=[pl.BlockSpec(memory_space=pl.ANY)] * 2,
        scratch_shapes=[pltpu.SemaphoreType.DMA((2,))],
        compiler_params=pltpu.CompilerParams(vmem_limit_bytes=1 << 20),
    )(corrected, defect)


def quarter_device(nt, ns, initial, coarse_guess, react_rate):
    planes, across, width = initial.shape
    part = across // nt
    wide = -(-(2 * STEPS + max(nt - 2, 0)) // SUBLANES) * SUBLANES
    length = planes + 2 * STEPS
    tall = part + 4 * wide
    recv_of, recv_total = quarter_slots(nt)

    def field(number):
        return pltpu.VMEM((number, length, tall, width), jnp.float32)

    shape = jax.ShapeDtypeStruct(initial.shape, jnp.float32)
    corrected, defect = pl.pallas_call(
        functools.partial(quarter_kernel, nt, ns, planes, part, wide, recv_of, recv_total),
        out_shape=(shape, shape),
        in_specs=[pl.BlockSpec(memory_space=pltpu.HBM)] * 3,
        out_specs=[pl.BlockSpec(memory_space=pl.ANY)] * 2,
        scratch_shapes=[
            field(nt), field(nt), field(1), field(1), field(1), field(1), field(nt), field(nt), field(nt), field(1),
            pltpu.VMEM((part + 2 * wide, width), jnp.float32),
            pltpu.SemaphoreType.DMA((SHARES * (4 * nt + nt // 2 + 3) + 6 * nt - 6,)),
            pltpu.SemaphoreType.DMA((recv_total,)),
        ],
        compiler_params=pltpu.CompilerParams(collective_id=0, has_side_effects=True, vmem_limit_bytes=VMEM_BYTES),
    )(*(pltpu.with_memory_space_constraint(ref, pltpu.HBM) for ref in (initial, coarse_guess[0], react_rate)))
    return settle(corrected, defect)


def takes_quarters(nt, planes, across):
    part = across // nt
    wide = -(-(2 * STEPS + max(nt - 2, 0)) // SUBLANES) * SUBLANES
    fits = across % (nt * SUBLANES) == 0 and part + 2 * wide <= across and nt - 2 <= planes
    return nt % 2 == 0 and nt > 2 and planes >= STEPS and fits


def on_device(nt, ns, initial, coarse_guess, react_rate):
    planes, across, width = initial.shape
    if takes_quarters(nt, planes, across):
        return quarter_device(nt, ns, initial, coarse_guess, react_rate)
    half = across // 2
    wide = -(-(2 * STEPS + max(nt - 2, 0)) // SUBLANES) * SUBLANES
    length = 2 * planes + 2 * STEPS
    field = pltpu.VMEM((length, half + 2 * wide, width), jnp.float32)
    slot_of, total = slots(planes)
    shape = jax.ShapeDtypeStruct(initial.shape, jnp.float32)
    corrected, defect = pl.pallas_call(
        functools.partial(kernel, nt, ns, planes, half, wide, slot_of),
        out_shape=(shape, shape),
        in_specs=[pl.BlockSpec(memory_space=pl.ANY)] * 3,
        out_specs=[pl.BlockSpec(memory_space=pl.ANY)] * 2,
        scratch_shapes=[field] * 11
        + [
            pltpu.VMEM((half + 2 * wide, width), jnp.float32),
            pltpu.SemaphoreType.DMA((total,)),
            pltpu.SemaphoreType.DMA((total,)),
            pltpu.SemaphoreType.DMA((3 + planes,)),
        ],
        compiler_params=pltpu.CompilerParams(collective_id=0, has_side_effects=True),
    )(initial, coarse_guess[0], react_rate)
    return corrected[None], defect[None]


def solution(mesh):
    in_specs = (P("space", None, None), P("tm", "space", None, None), P("space", None, None))
    out_specs = (P("tm", "space", None, None), P("tm", "space", None, None))
    return jax.shard_map(
        functools.partial(on_device, mesh.shape["tm"], mesh.shape["space"]),
        mesh=mesh, in_specs=in_specs, out_specs=out_specs, check_vma=False,
    )
```

```python
import functools

import jax
import jax.numpy as jnp
from jax import lax
from jax.experimental import pallas as pl
from jax.experimental.pallas import tpu as pltpu
from jax.sharding import PartitionSpec as P

STEPS = 3
SUBLANES = 8

fine_diffuse = 0.04
fine_growth = 0.05
coarse_ratio = 4.0

MESH = pl.DeviceIdType.MESH

PIECES = 4
LANES = 128
ROW_SHARES = 2
VMEM_BYTES = 40 << 20


def slots(planes):
    kinds = dict(
        start=2 + PIECES, start_edge=1 + PIECES, rate=1, rate_edge=2, rate_core=3, again=PIECES, again_edge=2 * PIECES,
        chain=2 * planes, chain_edge=2, defect=1, corrected=planes,
    )
    first, total = {}, 0
    for kind, number in kinds.items():
        first[kind] = total
        total += number
    return first, total


def kernel(
    nt, ns, planes, half, wide, slot_of,
    initial, guess, rate_in, corrected_out, defect_out,
    start, rate, again, before, first, second, relaxed, coarse, offset, defect, after, reach,
    send, recv, local,
):
    tm, space = lax.axis_index("tm"), lax.axis_index("space")
    pair, side = lax.div(space, 2), lax.rem(space, 2)
    pairs = ns // 2
    mate = space + 1 - 2 * side
    block = 2 * planes
    length = block + 2 * STEPS
    rows = half + 2 * wide
    has_low, has_high = pair > 0, pair < pairs - 1
    has_next, has_previous = tm < nt - 1, tm > 0
    own = pl.ds(STEPS, block)

    for ref in (start, rate, again, before):
        zero_plane = jnp.zeros((STEPS,) + ref.shape[1:], jnp.float32)
        zero_rows = jnp.zeros((block, wide, ref.shape[2]), jnp.float32)
        ref[0:STEPS] = zero_plane
        ref[STEPS + block : length] = zero_plane
        ref[STEPS : STEPS + block, 0:wide] = zero_rows
        ref[STEPS : STEPS + block, wide + half : rows] = zero_rows

    barrier = pltpu.get_barrier_semaphore()
    count = jnp.int32(0)
    for step in (-1, 0, 1):
        for place in ("own", "mate", "low", "high"):
            if step == 0 and place == "own":
                continue
            there = {"own": space, "mate": mate, "low": space - 2, "high": space + 2}[place]
            tests = []
            if step:
                tests.append(has_next if step > 0 else has_previous)
            if place in ("low", "high"):
                tests.append(has_low if place == "low" else has_high)
            target = {"tm": tm + step, "space": there}
            if tests:
                valid = functools.reduce(jnp.logical_and, tests)

                @pl.when(valid)
                def _(target=target):
                    pl.semaphore_signal(barrier, inc=1, device_id=target, device_id_type=MESH)

                count = count + valid.astype(jnp.int32)
            else:
                pl.semaphore_signal(barrier, inc=1, device_id=target, device_id_type=MESH)
                count = count + 1
    for here, there in ((tm == 0, nt - 1), (tm == nt - 1, 0)):

        @pl.when(here)
        def _(there=there):
            pl.semaphore_signal(
                barrier, inc=1, device_id={"tm": there, "space": mate}, device_id_type=MESH
            )

        count = count + here.astype(jnp.int32)
    pl.semaphore_wait(barrier, count)

    def remote(src, dst, slot, to_tm, to_space):
        return pltpu.make_async_remote_copy(
            src_ref=src,
            dst_ref=dst,
            send_sem=send.at[slot],
            recv_sem=recv.at[slot],
            device_id={"tm": to_tm, "space": to_space},
            device_id_type=MESH,
        )

    def cut(ref, target):
        return ref.at[:, pl.ds(pl.multiple_of(target * (half - wide), SUBLANES), half + wide), :]

    def spot(ref, target, begin, size):
        at = pl.multiple_of(wide * (1 - target), SUBLANES)
        return ref.at[pl.ds(begin, size), pl.ds(at, half + wide), :]

    slab = STEPS + planes * side
    other = STEPS + planes * (1 - side)

    core = lax.rem(tm, 2)
    twin = tm + 1 - 2 * core
    lanes = start.shape[2] // 2

    def lane_half(ref, which):
        return ref.at[:, :, pl.ds(pl.multiple_of(which * lanes, lanes), lanes)]

    groups = (half + wide) // SUBLANES
    bounds = [groups * piece // PIECES * SUBLANES for piece in range(PIECES + 1)]

    def piece_of(ref, begin, size, piece, target=side):
        at = pl.multiple_of(wide * (1 - target) + bounds[piece], SUBLANES)
        return ref.at[pl.ds(begin, size), pl.ds(at, bounds[piece + 1] - bounds[piece]), :]

    def cut_piece(ref, target, piece):
        at = pl.multiple_of(target * (half - wide) + bounds[piece], SUBLANES)
        return ref.at[:, pl.ds(at, bounds[piece + 1] - bounds[piece]), :]

    rate_own = pltpu.make_async_copy(cut(rate_in, side), spot(rate, side, slab, planes), local.at[0])
    rate_mate = remote(
        lane_half(cut(rate_in, 1 - side), core),
        lane_half(spot(rate, 1 - side, slab, planes), core),
        slot_of["rate"],
        tm,
        mate,
    )
    initial_own = pltpu.make_async_copy(cut(initial, side), spot(start, side, slab, planes), local.at[1])
    guess_own = remote(
        cut(guess, side), spot(start, side, slab, planes), slot_of["start"], tm + 1, space
    )

    def to_mate(ref, to_tm):
        return [
            remote(
                cut_piece(ref, 1 - side, piece),
                piece_of(start, slab, planes, piece, 1 - side),
                slot_of["start"] + 1 + piece,
                to_tm,
                mate,
            )
            for piece in range(PIECES)
        ]

    guess_mate = to_mate(guess, tm + 1)
    initial_mate = to_mate(initial, 0)
    is_last = tm == nt - 1

    rate_mate.start()
    rate_own.start()

    @pl.when(has_next)
    def _():
        guess_own.start()
        for copy in guess_mate:
            copy.start()

    @pl.when(is_last)
    def _():
        for copy in initial_mate:
            copy.start()

    @pl.when(tm == 0)
    def _():
        initial_own.start()

    for ref in (first, second):
        @pl.when(jnp.logical_not(has_low))
        def _(ref=ref):
            ref[0:STEPS] = jnp.zeros((STEPS,) + ref.shape[1:], jnp.float32)

        @pl.when(jnp.logical_not(has_high))
        def _(ref=ref):
            ref[STEPS + block : length] = jnp.zeros((STEPS,) + ref.shape[1:], jnp.float32)

    row = lax.broadcasted_iota(jnp.int32, reach.shape, 0)
    outside = jnp.logical_or(
        jnp.logical_and(side == 0, row < wide), jnp.logical_and(side == 1, row >= wide + half)
    )
    reach[...] = jnp.where(outside, 0.0, fine_diffuse)

    low_place, high_place = STEPS + block, 0

    def edge_pieces(piece):
        slot = slot_of["start_edge"] + 1 + piece
        low = remote(
            piece_of(start, STEPS, STEPS, piece), piece_of(start, low_place, STEPS, piece),
            slot, tm, space - 2,
        )
        high = remote(
            piece_of(start, block, STEPS, piece), piece_of(start, high_place, STEPS, piece),
            slot, tm, space + 2,
        )
        return low, high

    start_edges = [edge_pieces(piece) for piece in range(PIECES)]
    start_low = remote(
        spot(start, side, STEPS, STEPS), spot(start, side, low_place, STEPS),
        slot_of["start_edge"], tm, space - 2,
    )
    start_high = remote(
        spot(start, side, block, STEPS), spot(start, side, high_place, STEPS),
        slot_of["start_edge"], tm, space + 2,
    )
    reach_rate = STEPS - 1
    rate_low_spot = lane_half(spot(rate, side, low_place, reach_rate), core)
    rate_high_spot = lane_half(spot(rate, side, high_place + 1, reach_rate), core)
    rate_low = remote(
        lane_half(spot(rate, side, STEPS, reach_rate), core), rate_low_spot,
        slot_of["rate_edge"], tm, space - 2,
    )
    rate_high = remote(
        lane_half(spot(rate, side, STEPS + block - reach_rate, reach_rate), core), rate_high_spot,
        slot_of["rate_edge"] + 1, tm, space + 2,
    )
    rate_other_spot = lane_half(spot(rate, side, other, planes), core)
    twin_mate = remote(rate_other_spot, rate_other_spot, slot_of["rate_core"], twin, space)
    twin_low = remote(rate_low_spot, rate_low_spot, slot_of["rate_core"] + 1, twin, space)
    twin_high = remote(rate_high_spot, rate_high_spot, slot_of["rate_core"] + 2, twin, space)

    own_low = jnp.logical_and(side == 0, has_low)
    own_high = jnp.logical_and(side == 1, has_high)
    other_low = jnp.logical_and(side == 1, has_low)
    other_high = jnp.logical_and(side == 0, has_high)

    rate_own.wait()
    pl.when(own_low)(rate_low.start)
    pl.when(own_high)(rate_high.start)

    @pl.when(tm == 0)
    def _():
        initial_own.wait()

    @pl.when(has_previous)
    def _():
        guess_own.wait_recv()

    pl.when(own_low)(start_low.start)
    pl.when(own_high)(start_high.start)

    rate_mate.wait_recv()
    pl.when(other_low)(rate_low.start)
    pl.when(other_high)(rate_high.start)
    twin_mate.start()

    for piece in range(PIECES):
        guess_mate[piece].wait_recv()
        pl.when(other_low)(start_edges[piece][0].start)
        pl.when(other_high)(start_edges[piece][1].start)

    @pl.when(has_high)
    def _():
        rate_low.wait_recv()
        twin_low.start()

    @pl.when(has_low)
    def _():
        rate_high.wait_recv()
        twin_high.start()

    twin_mate.wait_recv()
    pl.when(has_high)(twin_low.wait_recv)
    pl.when(has_low)(twin_high.wait_recv)

    @pl.when(jnp.logical_and(side == 0, has_high))
    def _():
        start_low.wait_recv()

    @pl.when(jnp.logical_and(side == 1, has_low))
    def _():
        start_high.wait_recv()

    @pl.when(jnp.logical_and(side == 1, has_high))
    def _():
        for low, high in start_edges:
            low.wait_recv()

    @pl.when(jnp.logical_and(side == 0, has_low))
    def _():
        for low, high in start_edges:
            high.wait_recv()

    keep = pltpu.make_async_copy(start, again, local.at[1])

    @pl.when(tm == 0)
    def _():
        keep.start()

    width = start.shape[2]
    lane = lax.broadcasted_iota(jnp.int32, reach.shape, 1)

    def change(ref, z):
        middle = ref[z]
        beside = ref[z + 1] + ref[z - 1]
        beside = beside + pltpu.roll(middle, 1, 0) + pltpu.roll(middle, rows - 1, 0)
        beside = beside + jnp.where(lane == 0, 0.0, pltpu.roll(middle, 1, 1))
        beside = beside + jnp.where(lane == width - 1, 0.0, pltpu.roll(middle, width - 1, 1))
        growth = rate[z] * (fine_growth - fine_growth * (middle * middle))
        return middle, reach[...] * beside + middle * (growth - 6.0 * fine_diffuse)

    def span(step):
        low = jnp.where(has_low, step, max(step, STEPS))
        high = jnp.where(has_high, length - step, min(length - step, STEPS + block))
        return low, high

    def fine(src, dst, step):
        def plane(z, carry):
            middle, delta = change(src, z)
            dst[z] = middle + delta
            return carry

        lax.fori_loop(*span(step), plane, 0)

    fine(start, first, 1)
    fine(first, second, 2)
    fine(second, relaxed, 3)

    given, given_low, given_high = [], [], []
    for piece in range(PIECES):
        slot = slot_of["again_edge"] + 2 * piece
        given.append(
            remote(
                piece_of(relaxed, STEPS, block, piece),
                piece_of(again, STEPS, block, piece),
                slot_of["again"] + piece,
                tm + 1,
                space,
            )
        )
        given_low.append(
            remote(
                piece_of(again, STEPS, STEPS, piece),
                piece_of(again, STEPS + block, STEPS, piece),
                slot,
                tm,
                space - 2,
            )
        )
        given_high.append(
            remote(
                piece_of(again, block, STEPS, piece),
                piece_of(again, 0, STEPS, piece),
                slot + 1,
                tm,
                space + 2,
            )
        )

    @pl.when(has_next)
    def _():
        for piece in range(PIECES):
            given[piece].start()

    @pl.when(tm == 0)
    def _():
        keep.wait()

    @pl.when(has_previous)
    def _():
        for piece in range(PIECES):
            given[piece].wait_recv()
            pl.when(has_low)(given_low[piece].start)
            pl.when(has_high)(given_high[piece].start)
        for piece in range(PIECES):
            pl.when(has_high)(given_low[piece].wait_recv)
            pl.when(has_low)(given_high[piece].wait_recv)

    def first_plane(z, carry):
        middle, delta = change(again, z)
        first[z] = middle + delta
        coarse[z] = middle + coarse_ratio * delta
        return carry

    lax.fori_loop(*span(1), first_plane, 0)
    fine(first, second, 2)

    order = []
    for depth in range(planes):
        order += [STEPS + depth, STEPS + block - 1 - depth]

    def row_span(z):
        at = pl.multiple_of(wide * (1 - side), SUBLANES)
        return (pl.ds(z, 1), pl.ds(at, half + wide), slice(None))

    passed = {
        z: remote(
            after.at[row_span(z)], before.at[row_span(z)], slot_of["chain"] + z - STEPS, tm + 1, space
        )
        for z in order
    }
    low_edge, high_edge = STEPS, STEPS + block - 1
    passed_low = remote(
        before.at[row_span(low_edge)], before.at[row_span(high_edge + 1)],
        slot_of["chain_edge"], tm, space - 2,
    )
    passed_high = remote(
        before.at[row_span(high_edge)], before.at[row_span(low_edge - 1)],
        slot_of["chain_edge"] + 1, tm, space + 2,
    )

    mine = pl.ds(pl.multiple_of(side * half, SUBLANES), half)
    middle_rows = pl.ds(wide, half)
    defect_stay = pltpu.make_async_copy(
        defect.at[pl.ds(slab, planes), middle_rows, :], defect_out.at[:, mine, :], local.at[2]
    )
    defect_go = remote(
        defect.at[pl.ds(other, planes), middle_rows, :], defect_out.at[:, mine, :],
        slot_of["defect"], tm, mate,
    )
    stay, go = {}, {}
    for z in order:
        place = (z - STEPS) % planes
        src = after.at[pl.ds(z, 1), middle_rows, :]
        dst = corrected_out.at[pl.ds(place, 1), mine, :]
        stay[z] = pltpu.make_async_copy(src, dst, local.at[3 + place])
        go[z] = remote(src, dst, slot_of["corrected"] + place, tm, mate)

    def at_home(z):
        return side == (z - STEPS) // planes

    def hand_in(z):
        pl.when(at_home(z))(stay[z].start)
        pl.when(jnp.logical_not(at_home(z)))(go[z].start)

    def last_plane(z):
        middle, delta = change(second, z)
        end = middle + delta
        defect[z] = end - relaxed[z]
        shift = end - coarse[z]
        offset[z] = shift
        after[z] = coarse[z] + shift

    def take_edges():
        passed[low_edge].wait_recv()
        pl.when(has_low)(passed_low.start)
        passed[high_edge].wait_recv()
        pl.when(has_high)(passed_high.start)

    pl.when(tm == 2)(take_edges)
    opens = jnp.logical_and(tm == 1, has_next)
    for index, z in enumerate(order):
        last_plane(z)
        if index:
            pl.when(opens)(passed[order[index - 1]].start)
    pl.when(opens)(passed[order[-1]].start)
    defect_go.start()
    defect_stay.start()

    later = tm > 1

    @pl.when(jnp.logical_not(later))
    def _():
        for z in order:
            hand_in(z)

    @pl.when(later)
    def _():
        pl.when(tm > 2)(take_edges)
        queue = order[2:]
        waiting = set(queue)

        def leave(z):
            pl.when(has_next)(passed[z].start)
            hand_in(z)

        for index, z in enumerate(order):
            while waiting & {z - 1, z, z + 1}:
                come = queue.pop(0)
                waiting.remove(come)
                passed[come].wait_recv()
            if z == low_edge:
                pl.when(has_low)(passed_high.wait_recv)
            if z == high_edge:
                pl.when(has_high)(passed_low.wait_recv)
            middle, delta = change(before, z)
            after[z] = middle + coarse_ratio * delta + offset[z]
            if index:
                leave(order[index - 1])
        leave(order[-1])
        pl.when(has_low)(passed_low.wait_send)
        pl.when(has_high)(passed_high.wait_send)

    onward = jnp.logical_and(tm > 0, has_next)

    @pl.when(is_last)
    def _():
        for copy in initial_mate:
            copy.wait_send()

    @pl.when(has_next)
    def _():
        guess_own.wait_send()
        for copy in guess_mate:
            copy.wait_send()

    rate_mate.wait_send()
    twin_mate.wait_send()
    pl.when(has_high)(twin_low.wait_send)
    pl.when(has_low)(twin_high.wait_send)
    pl.when(has_low)(rate_low.wait_send)
    pl.when(has_high)(rate_high.wait_send)
    pl.when(own_low)(start_low.wait_send)
    pl.when(own_high)(start_high.wait_send)

    @pl.when(other_low)
    def _():
        for low, high in start_edges:
            low.wait_send()

    @pl.when(other_high)
    def _():
        for low, high in start_edges:
            high.wait_send()

    @pl.when(has_next)
    def _():
        for piece in range(PIECES):
            given[piece].wait_send()

    @pl.when(has_previous)
    def _():
        for piece in range(PIECES):
            pl.when(has_low)(given_low[piece].wait_send)
            pl.when(has_high)(given_high[piece].wait_send)

    @pl.when(onward)
    def _():
        for z in order:
            passed[z].wait_send()

    defect_stay.wait()
    defect_go.wait()
    for z in order:
        pl.when(at_home(z))(stay[z].wait)
        pl.when(at_home(z))(go[z].wait_recv)
        pl.when(jnp.logical_not(at_home(z)))(go[z].wait_send)


def quarter_slots(nt, shares):
    kinds = dict(
        start=nt * shares, rate=shares, low_start=nt * shares, high_start=nt * shares,
        low_rate=shares, high_rate=shares,
        low_again=nt, high_again=nt, low_first=1, high_first=1, low_offset=nt, high_offset=nt,
        corrected=nt, defect=nt,
    )
    first, total = {}, 0
    for kind, number in kinds.items():
        first[kind] = total
        total += number
    return first, total


def quarter_kernel(
    nt, ns, planes, part, wide, recv_of,
    initial, guess, rate_in, corrected_out, defect_out,
    start, again, rate, first, second, coarse, chain, offset, defect, end, reach,
    send, recv,
):
    tm, space = lax.axis_index("tm"), lax.axis_index("space")
    y, core = lax.div(tm, 2), lax.rem(tm, 2)
    pair, x = lax.div(space, 2), lax.rem(space, 2)
    levels, pairs = nt // 2, ns // 2
    length = planes + 2 * STEPS
    rows = part + 2 * wide
    across = initial.shape[1]
    tiles = start.shape[2]
    shares = ROW_SHARES * tiles
    low_own, high_own = STEPS, STEPS + planes
    slab = 2 * pair + core
    has_low, has_high = slab > 0, slab < ns - 1
    quarter = 2 * y + x
    low_to = {"tm": tm + 1 - 2 * core, "space": space - 2 * (1 - core)}
    high_to = {"tm": tm + 1 - 2 * core, "space": space + 2 * core}

    def window(which):
        begin = jnp.clip(part * which - wide, 0, across - rows)
        at = begin - part * which + 2 * wide
        return pl.multiple_of(begin, SUBLANES), pl.multiple_of(at, SUBLANES)

    my_begin, my_at = window(quarter)
    body = pl.ds(wide, rows)
    mine = pl.ds(2 * wide, part)

    first_row, last_row = y + x == 0, quarter == nt - 1
    edge_zero = jnp.zeros((length, tiles, wide, LANES), jnp.float32)
    plane_zero = jnp.zeros((STEPS,) + start.shape[2:], jnp.float32)

    def clear_rows(ref, k):
        @pl.when(first_row)
        def _():
            ref[k, :, :, wide : 2 * wide] = edge_zero

        @pl.when(last_row)
        def _():
            ref[k, :, :, 2 * wide + part : 3 * wide + part] = edge_zero

    def clear_planes(ref, k):
        @pl.when(jnp.logical_not(has_low))
        def _():
            ref[k, 0:low_own] = plane_zero

        @pl.when(jnp.logical_not(has_high))
        def _():
            ref[k, high_own:length] = plane_zero

    barrier = pltpu.get_barrier_semaphore()
    for dy in range(levels):
        for dx in range(2):
            for dc in range(2):
                if dy or dx or dc:
                    there = {
                        "tm": 2 * lax.rem(y + dy, levels) + lax.rem(core + dc, 2),
                        "space": 2 * pair + lax.rem(x + dx, 2),
                    }
                    pl.semaphore_signal(barrier, inc=1, device_id=there, device_id_type=MESH)
    count = jnp.int32(2 * nt - 1)
    for far, there in (
        (jnp.logical_and(core == 0, has_low), low_to),
        (jnp.logical_and(core == 1, has_high), high_to),
    ):

        @pl.when(far)
        def _(there=there):
            pl.semaphore_signal(barrier, inc=1, device_id=there, device_id_type=MESH)

        count = count + far.astype(jnp.int32)

    for k in range(nt):
        clear_rows(start, k)
        clear_planes(start, k)
    for k in range(nt - 1):
        clear_planes(again, k)
    clear_rows(rate, 0)
    clear_planes(rate, 0)
    clear_planes(chain, 1)
    for j in range(2, nt - 1):
        clear_planes(offset, j)

    pl.semaphore_wait(barrier, count)

    sends = []
    send_count = [0]

    def remote(src, dst, slot, there, condition):
        number = send_count[0]
        send_count[0] += 1
        copy = pltpu.make_async_remote_copy(
            src_ref=src, dst_ref=dst, send_sem=send.at[number], recv_sem=recv.at[slot],
            device_id=there, device_id_type=MESH,
        )
        sends.append((copy, condition))
        return copy

    def launch(src, dst, slot, there, condition):
        copy = remote(src, dst, slot, there, condition)
        pl.when(condition)(copy.start)

    def arrive(dst, slot, condition=None):
        copy = pltpu.make_async_copy(dst, dst, recv.at[slot])
        if condition is None:
            copy.wait()
        else:
            pl.when(condition)(copy.wait)

    size = rows // ROW_SHARES
    own = pl.ds(low_own, planes)
    home = core == x
    away = jnp.logical_not(home)

    def source(ref, begin, share_at):
        down, tile = divmod(share_at, tiles)
        at = pl.multiple_of(begin + down * size, SUBLANES)
        return ref.at[:, pl.ds(at, size), pl.ds(tile * LANES, LANES)]

    def place(ref, k, at, share_at, zs=own):
        down, tile = divmod(share_at, tiles)
        return ref.at[k, zs, tile, pl.ds(pl.multiple_of(at + down * size, SUBLANES), size), :]

    @pl.when(home)
    def _():
        for ref, k, src, kind in ((start, 0, initial, "start"), (rate, 0, rate_in, "rate")):
            for share_at in range(shares):
                pltpu.make_async_copy(
                    source(src, my_begin, share_at), place(ref, k, my_at, share_at), recv.at[recv_of[kind] + share_at]
                ).start()

    there_begin, there_at = window(2 * y + 1 - x)
    for share_at in range(shares):
        launch(
            source(initial, there_begin, share_at), place(start, 0, there_at, share_at),
            recv_of["start"] + share_at, {"tm": 2 * y + x, "space": space + 1 - 2 * x}, core == share_at % 2,
        )
    for to_y in range(levels):
        begin, at = window(2 * to_y + 1 - x)
        for share_at in range(shares):
            launch(
                source(rate_in, begin, share_at), place(rate, 0, at, share_at), recv_of["rate"] + share_at,
                {"tm": 2 * to_y + x, "space": space + 1 - 2 * x},
                jnp.logical_and(y == levels - 1, core == share_at % 2),
            )

    def give_guess(turn):
        gives = jnp.logical_and(tm < nt - 1, core == turn)
        for share_at in range(shares):
            slot = recv_of["start"] + (tm + 1) * shares + share_at
            for dy in range(levels):
                for dx in (1, 0):
                    to_y, to_x = lax.rem(y + dy, levels), lax.rem(x + dx, 2)
                    begin, at = window(2 * to_y + to_x)
                    src, dst = source(guess, begin, share_at), place(start, tm + 1, at, share_at)
                    there = {"tm": 2 * to_y + x, "space": 2 * pair + to_x}
                    if dy or dx:
                        launch(src, dst, slot, there, gives)
                    else:
                        launch(src, dst, slot, there, jnp.logical_and(gives, away))

                        @pl.when(jnp.logical_and(gives, home))
                        def _(src=src, dst=dst, slot=slot):
                            pltpu.make_async_copy(src, dst, recv.at[slot]).start()

    give_guess(0)

    row = lax.broadcasted_iota(jnp.int32, (rows, LANES), 0)
    outside = jnp.logical_or(
        jnp.logical_and(first_row, row < wide), jnp.logical_and(last_row, row >= wide + part)
    )
    for zone, inside in enumerate((has_low, True, has_high)):
        reach[zone] = jnp.where(jnp.logical_and(inside, jnp.logical_not(outside)), fine_diffuse, 0.0)

    def share(src_of, depth, high_slot, low_slot):
        launch(
            src_of(pl.ds(low_own, depth)), src_of(pl.ds(high_own, depth)), high_slot, low_to, has_low
        )
        launch(
            src_of(pl.ds(high_own - depth, depth)), src_of(pl.ds(low_own - depth, depth)), low_slot, high_to, has_high
        )

    def shared(dst_of, depth, high_slot, low_slot):
        arrive(dst_of(pl.ds(high_own, depth)), high_slot, has_high)
        arrive(dst_of(pl.ds(low_own - depth, depth)), low_slot, has_low)

    def start_view(k, share_at):
        return lambda zs: place(start, k, my_at, share_at, zs)

    def relay_start(k):
        for share_at in range(shares):
            at = k * shares + share_at
            arrive(place(start, k, my_at, share_at), recv_of["start"] + at)
            share(start_view(k, share_at), STEPS, recv_of["high_start"] + at, recv_of["low_start"] + at)

    def start_ready(k):
        for share_at in range(shares):
            at = k * shares + share_at
            shared(start_view(k, share_at), STEPS, recv_of["high_start"] + at, recv_of["low_start"] + at)

    def rate_view(share_at):
        return lambda zs: place(rate, 0, my_at, share_at, zs)

    def relay_rate():
        for at in range(shares):
            arrive(place(rate, 0, my_at, at), recv_of["rate"] + at)
            share(rate_view(at), STEPS - 1, recv_of["high_rate"] + at, recv_of["low_rate"] + at)

    def rate_ready():
        for at in range(shares):
            shared(rate_view(at), STEPS - 1, recv_of["high_rate"] + at, recv_of["low_rate"] + at)

    def body_view(ref, k):
        return lambda zs: ref.at[k, zs, :, body, :]

    tall = next(number for number in (32, 16, 8) if rows % number == 0)
    lane = lax.broadcasted_iota(jnp.int32, (tall, LANES), 1)

    def march(src, k, low, high, emit):
        def block(number, carry):
            at = pl.multiple_of(wide + number * tall, SUBLANES)
            here = pl.ds(at, tall)
            reaches = [reach[zone, pl.ds(pl.multiple_of(number * tall, SUBLANES), tall), :] for zone in range(3)]

            def load(z):
                return [src[k, z, tile, here, :] for tile in range(tiles)]

            under, middle = load(low - 1), load(low)
            for z in range(low, high):
                over = load(z + 1)
                zone = 0 if z < low_own else 1 if z < high_own else 2
                after = [pltpu.roll(part_of, 1, 1) for part_of in middle]
                ahead = [pltpu.roll(part_of, LANES - 1, 1) for part_of in middle]
                for tile in range(tiles):
                    value = middle[tile]
                    left = after[tile - 1] if tile else 0.0
                    right = ahead[tile + 1] if tile + 1 < tiles else 0.0
                    beside = over[tile] + under[tile]
                    beside = beside + src[k, z, tile, pl.ds(at - 1, tall), :] + src[k, z, tile, pl.ds(at + 1, tall), :]
                    beside = beside + jnp.where(lane == 0, left, after[tile])
                    beside = beside + jnp.where(lane == LANES - 1, right, ahead[tile])
                    growth = rate[0, z, tile, here, :] * (fine_growth - fine_growth * (value * value))
                    stepped = reaches[zone] * beside + value * (growth + (1.0 - 6.0 * fine_diffuse))
                    emit((z, tile, here), value, stepped)
                under, middle = middle, over
            return carry

        lax.fori_loop(0, rows // tall, block, 0)

    def rough_of(value, stepped):
        return value + coarse_ratio * (stepped - value)

    def put(ref, k, spot, value):
        z, tile, here = spot
        ref[k, z, tile, here, :] = value

    def get(ref, k, spot):
        z, tile, here = spot
        return ref[k, z, tile, here, :]

    def fine(src, source_k, dst, halo, rough=False):
        def emit(spot, value, stepped):
            put(dst, 0, spot, stepped)
            if rough and low_own <= spot[0] < high_own:
                put(coarse, 0, spot, rough_of(value, stepped))

        march(src, source_k, low_own - halo, high_own + halo, emit)

    def hand_in(ref, k, out, kind, j):
        there_space = 2 * pair + core
        src = ref.at[k, own, :, mine, :]
        dst = out.at[:, :, pl.ds(pl.multiple_of(part * quarter, SUBLANES), part), :]
        slot = recv_of[kind] + quarter
        stays = jnp.logical_and(tm == j, home)
        launch(src, dst, slot, {"tm": j, "space": there_space}, jnp.logical_not(stays))

        @pl.when(stays)
        def _():
            pltpu.make_async_copy(src, dst, recv.at[slot]).start()

    def relax(k):
        fine(start, k, first, STEPS - 1, rough=k == 0)
        fine(first, 0, second, STEPS - 2)

        def emit(spot, value, stepped):
            if k == nt - 1:
                put(defect, k, spot, get(end, 0, spot) - stepped)
                return
            put(again, k, spot, stepped)
            if k == 0:
                put(defect, 0, spot, stepped - stepped)
                base = get(coarse, 0, spot)
                put(chain, 0, spot, base + (stepped - base))

        march(second, 0, low_own, high_own, emit)

    def send_again(k):
        share(body_view(again, k), STEPS, recv_of["high_again"] + k, recv_of["low_again"] + k)

    def finish(k):
        shared(body_view(again, k), STEPS, recv_of["high_again"] + k, recv_of["low_again"] + k)
        fine(again, k, first, STEPS - 1, rough=True)
        fine(first, 0, second, STEPS - 2)

        def emit(spot, value, stepped):
            if k + 1 < nt - 1:
                put(defect, k + 1, spot, stepped - get(again, k + 1, spot))
            else:
                put(end, 0, spot, stepped)
            base = get(coarse, 0, spot)
            if k:
                put(offset, k + 1, spot, stepped - base)
            else:
                put(chain, 1, spot, base + (stepped - base))

        march(second, 0, low_own, high_own, emit)

    def lift_between(j, low, high):
        def emit(spot, value, stepped):
            put(chain, j, spot, rough_of(value, stepped) + get(offset, j, spot))

        march(chain, j - 1, low, high, emit)

    def edges_of(j):
        slots = recv_of["high_offset"] + j, recv_of["low_offset"] + j
        return body_view(offset, j), nt - 1 - j, *slots

    def lift_around(j):
        halo = nt - 1 - j
        if halo:
            shared(*edges_of(j))
            lift_between(j, low_own - halo, low_own)
            lift_between(j, high_own, high_own + halo)

    relay_start(0)
    relay_rate()
    give_guess(1)
    relay_start(1)
    start_ready(0)
    rate_ready()
    relax(0)
    send_again(0)
    hand_in(chain, 0, corrected_out, "corrected", 0)
    hand_in(defect, 0, defect_out, "defect", 0)
    relay_start(2)
    start_ready(1)
    relax(1)
    send_again(1)
    finish(0)
    first_edges = body_view(chain, 1), nt - 2, recv_of["high_first"], recv_of["low_first"]
    share(*first_edges)
    hand_in(chain, 1, corrected_out, "corrected", 1)
    hand_in(defect, 1, defect_out, "defect", 1)
    for j in range(2, nt):
        if j < nt - 1:
            start_ready(j)
            relax(j)
            send_again(j)
        finish(j - 1)
        if j < nt - 1:
            share(*edges_of(j))
            relay_start(j + 1)
            hand_in(defect, j, defect_out, "defect", j)
        if j == 2:
            shared(*first_edges)
        else:
            lift_around(j - 1)
        lift_between(j, low_own, high_own)
        hand_in(chain, j, corrected_out, "corrected", j)
    start_ready(nt - 1)
    relax(nt - 1)
    hand_in(defect, nt - 1, defect_out, "defect", nt - 1)

    for copy, condition in sends:
        pl.when(condition)(copy.wait_send)
    for out, kind in ((corrected_out, "corrected"), (defect_out, "defect")):
        for q in range(nt):
            arrive(out.at[:, :, pl.ds(part * q, part), :], recv_of[kind] + q)


def settle_kernel(corrected, defect, corrected_out, defect_out, local):
    copies = []
    for src, dst in ((corrected, corrected_out), (defect, defect_out)):
        for tile in range(src.shape[1]):
            to = dst.at[0, :, :, pl.ds(tile * LANES, LANES)]
            copies.append(pltpu.make_async_copy(src.at[:, tile], to, local.at[len(copies)]))
    for copy in copies:
        copy.start()
    for copy in copies:
        copy.wait()


def settle(corrected, defect):
    planes, tiles, across, lanes = corrected.shape
    shape = jax.ShapeDtypeStruct((1, planes, across, tiles * lanes), jnp.float32)
    return pl.pallas_call(
        settle_kernel,
        out_shape=(shape, shape),
        in_specs=[pl.BlockSpec(memory_space=pl.ANY)] * 2,
        out_specs=[pl.BlockSpec(memory_space=pl.ANY)] * 2,
        scratch_shapes=[pltpu.SemaphoreType.DMA((2 * tiles,))],
        compiler_params=pltpu.CompilerParams(vmem_limit_bytes=1 << 20),
    )(corrected, defect)


def quarter_device(nt, ns, initial, coarse_guess, react_rate):
    planes, across, width = initial.shape
    part = across // nt
    wide = -(-(2 * STEPS + max(nt - 2, 0)) // SUBLANES) * SUBLANES
    length = planes + 2 * STEPS
    tall = part + 4 * wide
    tiles = width // LANES
    shares = ROW_SHARES * tiles
    recv_of, recv_total = quarter_slots(nt, shares)

    def field(number):
        return pltpu.VMEM((number, length, tiles, tall, LANES), jnp.float32)

    shape = jax.ShapeDtypeStruct((planes, tiles, across, LANES), jnp.float32)
    corrected, defect = pl.pallas_call(
        functools.partial(quarter_kernel, nt, ns, planes, part, wide, recv_of),
        out_shape=(shape, shape),
        in_specs=[pl.BlockSpec(memory_space=pltpu.HBM)] * 3,
        out_specs=[pl.BlockSpec(memory_space=pl.ANY)] * 2,
        scratch_shapes=[
            field(nt), field(nt), field(1), field(1), field(1), field(1), field(nt), field(nt), field(nt), field(1),
            pltpu.VMEM((3, part + 2 * wide, LANES), jnp.float32),
            pltpu.SemaphoreType.DMA((shares * (4 * nt + nt // 2 + 3) + 6 * nt - 6,)),
            pltpu.SemaphoreType.DMA((recv_total,)),
        ],
        compiler_params=pltpu.CompilerParams(collective_id=0, has_side_effects=True, vmem_limit_bytes=VMEM_BYTES),
    )(*(pltpu.with_memory_space_constraint(ref, pltpu.HBM) for ref in (initial, coarse_guess[0], react_rate)))
    return settle(corrected, defect)


def takes_quarters(nt, planes, across, width):
    part = across // nt
    wide = -(-(2 * STEPS + max(nt - 2, 0)) // SUBLANES) * SUBLANES
    fits = across % (nt * SUBLANES) == 0 and part + 2 * wide <= across and nt - 2 <= planes
    return nt % 2 == 0 and nt > 2 and planes >= STEPS and width % LANES == 0 and fits


def on_device(nt, ns, initial, coarse_guess, react_rate):
    planes, across, width = initial.shape
    if takes_quarters(nt, planes, across, width):
        return quarter_device(nt, ns, initial, coarse_guess, react_rate)
    half = across // 2
    wide = -(-(2 * STEPS + max(nt - 2, 0)) // SUBLANES) * SUBLANES
    length = 2 * planes + 2 * STEPS
    field = pltpu.VMEM((length, half + 2 * wide, width), jnp.float32)
    slot_of, total = slots(planes)
    shape = jax.ShapeDtypeStruct(initial.shape, jnp.float32)
    corrected, defect = pl.pallas_call(
        functools.partial(kernel, nt, ns, planes, half, wide, slot_of),
        out_shape=(shape, shape),
        in_specs=[pl.BlockSpec(memory_space=pl.ANY)] * 3,
        out_specs=[pl.BlockSpec(memory_space=pl.ANY)] * 2,
        scratch_shapes=[field] * 11
        + [
            pltpu.VMEM((half + 2 * wide, width), jnp.float32),
            pltpu.SemaphoreType.DMA((total,)),
            pltpu.SemaphoreType.DMA((total,)),
            pltpu.SemaphoreType.DMA((3 + planes,)),
        ],
        compiler_params=pltpu.CompilerParams(collective_id=0, has_side_effects=True),
    )(initial, coarse_guess[0], react_rate)
    return corrected[None], defect[None]


def solution(mesh):
    in_specs = (P("space", None, None), P("tm", "space", None, None), P("space", None, None))
    out_specs = (P("tm", "space", None, None), P("tm", "space", None, None))
    return jax.shard_map(
        functools.partial(on_device, mesh.shape["tm"], mesh.shape["space"]),
        mesh=mesh, in_specs=in_specs, out_specs=out_specs, check_vma=False,
    )
```

```python
import functools

import jax
import jax.numpy as jnp
from jax import lax
from jax.experimental import pallas as pl
from jax.experimental.pallas import tpu as pltpu
from jax.sharding import PartitionSpec as P

STEPS = 3
SUBLANES = 8

fine_diffuse = 0.04
fine_growth = 0.05
coarse_ratio = 4.0

MESH = pl.DeviceIdType.MESH

PIECES = 4
LANES = 128
ROW_SHARES = 2
VMEM_BYTES = 40 << 20


def slots(planes):
    kinds = dict(
        start=2 + PIECES, start_edge=1 + PIECES, rate=1, rate_edge=2, rate_core=3, again=PIECES, again_edge=2 * PIECES,
        chain=2 * planes, chain_edge=2, defect=1, corrected=planes,
    )
    first, total = {}, 0
    for kind, number in kinds.items():
        first[kind] = total
        total += number
    return first, total


def kernel(
    nt, ns, planes, half, wide, slot_of,
    initial, guess, rate_in, corrected_out, defect_out,
    start, rate, again, before, first, second, relaxed, coarse, offset, defect, after, reach,
    send, recv, local,
):
    tm, space = lax.axis_index("tm"), lax.axis_index("space")
    pair, side = lax.div(space, 2), lax.rem(space, 2)
    pairs = ns // 2
    mate = space + 1 - 2 * side
    block = 2 * planes
    length = block + 2 * STEPS
    rows = half + 2 * wide
    has_low, has_high = pair > 0, pair < pairs - 1
    has_next, has_previous = tm < nt - 1, tm > 0
    own = pl.ds(STEPS, block)

    for ref in (start, rate, again, before):
        zero_plane = jnp.zeros((STEPS,) + ref.shape[1:], jnp.float32)
        zero_rows = jnp.zeros((block, wide, ref.shape[2]), jnp.float32)
        ref[0:STEPS] = zero_plane
        ref[STEPS + block : length] = zero_plane
        ref[STEPS : STEPS + block, 0:wide] = zero_rows
        ref[STEPS : STEPS + block, wide + half : rows] = zero_rows

    barrier = pltpu.get_barrier_semaphore()
    count = jnp.int32(0)
    for step in (-1, 0, 1):
        for place in ("own", "mate", "low", "high"):
            if step == 0 and place == "own":
                continue
            there = {"own": space, "mate": mate, "low": space - 2, "high": space + 2}[place]
            tests = []
            if step:
                tests.append(has_next if step > 0 else has_previous)
            if place in ("low", "high"):
                tests.append(has_low if place == "low" else has_high)
            target = {"tm": tm + step, "space": there}
            if tests:
                valid = functools.reduce(jnp.logical_and, tests)

                @pl.when(valid)
                def _(target=target):
                    pl.semaphore_signal(barrier, inc=1, device_id=target, device_id_type=MESH)

                count = count + valid.astype(jnp.int32)
            else:
                pl.semaphore_signal(barrier, inc=1, device_id=target, device_id_type=MESH)
                count = count + 1
    for here, there in ((tm == 0, nt - 1), (tm == nt - 1, 0)):

        @pl.when(here)
        def _(there=there):
            pl.semaphore_signal(
                barrier, inc=1, device_id={"tm": there, "space": mate}, device_id_type=MESH
            )

        count = count + here.astype(jnp.int32)
    pl.semaphore_wait(barrier, count)

    def remote(src, dst, slot, to_tm, to_space):
        return pltpu.make_async_remote_copy(
            src_ref=src,
            dst_ref=dst,
            send_sem=send.at[slot],
            recv_sem=recv.at[slot],
            device_id={"tm": to_tm, "space": to_space},
            device_id_type=MESH,
        )

    def cut(ref, target):
        return ref.at[:, pl.ds(pl.multiple_of(target * (half - wide), SUBLANES), half + wide), :]

    def spot(ref, target, begin, size):
        at = pl.multiple_of(wide * (1 - target), SUBLANES)
        return ref.at[pl.ds(begin, size), pl.ds(at, half + wide), :]

    slab = STEPS + planes * side
    other = STEPS + planes * (1 - side)

    core = lax.rem(tm, 2)
    twin = tm + 1 - 2 * core
    lanes = start.shape[2] // 2

    def lane_half(ref, which):
        return ref.at[:, :, pl.ds(pl.multiple_of(which * lanes, lanes), lanes)]

    groups = (half + wide) // SUBLANES
    bounds = [groups * piece // PIECES * SUBLANES for piece in range(PIECES + 1)]

    def piece_of(ref, begin, size, piece, target=side):
        at = pl.multiple_of(wide * (1 - target) + bounds[piece], SUBLANES)
        return ref.at[pl.ds(begin, size), pl.ds(at, bounds[piece + 1] - bounds[piece]), :]

    def cut_piece(ref, target, piece):
        at = pl.multiple_of(target * (half - wide) + bounds[piece], SUBLANES)
        return ref.at[:, pl.ds(at, bounds[piece + 1] - bounds[piece]), :]

    rate_own = pltpu.make_async_copy(cut(rate_in, side), spot(rate, side, slab, planes), local.at[0])
    rate_mate = remote(
        lane_half(cut(rate_in, 1 - side), core),
        lane_half(spot(rate, 1 - side, slab, planes), core),
        slot_of["rate"],
        tm,
        mate,
    )
    initial_own = pltpu.make_async_copy(cut(initial, side), spot(start, side, slab, planes), local.at[1])
    guess_own = remote(
        cut(guess, side), spot(start, side, slab, planes), slot_of["start"], tm + 1, space
    )

    def to_mate(ref, to_tm):
        return [
            remote(
                cut_piece(ref, 1 - side, piece),
                piece_of(start, slab, planes, piece, 1 - side),
                slot_of["start"] + 1 + piece,
                to_tm,
                mate,
            )
            for piece in range(PIECES)
        ]

    guess_mate = to_mate(guess, tm + 1)
    initial_mate = to_mate(initial, 0)
    is_last = tm == nt - 1

    rate_mate.start()
    rate_own.start()

    @pl.when(has_next)
    def _():
        guess_own.start()
        for copy in guess_mate:
            copy.start()

    @pl.when(is_last)
    def _():
        for copy in initial_mate:
            copy.start()

    @pl.when(tm == 0)
    def _():
        initial_own.start()

    for ref in (first, second):
        @pl.when(jnp.logical_not(has_low))
        def _(ref=ref):
            ref[0:STEPS] = jnp.zeros((STEPS,) + ref.shape[1:], jnp.float32)

        @pl.when(jnp.logical_not(has_high))
        def _(ref=ref):
            ref[STEPS + block : length] = jnp.zeros((STEPS,) + ref.shape[1:], jnp.float32)

    row = lax.broadcasted_iota(jnp.int32, reach.shape, 0)
    outside = jnp.logical_or(
        jnp.logical_and(side == 0, row < wide), jnp.logical_and(side == 1, row >= wide + half)
    )
    reach[...] = jnp.where(outside, 0.0, fine_diffuse)

    low_place, high_place = STEPS + block, 0

    def edge_pieces(piece):
        slot = slot_of["start_edge"] + 1 + piece
        low = remote(
            piece_of(start, STEPS, STEPS, piece), piece_of(start, low_place, STEPS, piece),
            slot, tm, space - 2,
        )
        high = remote(
            piece_of(start, block, STEPS, piece), piece_of(start, high_place, STEPS, piece),
            slot, tm, space + 2,
        )
        return low, high

    start_edges = [edge_pieces(piece) for piece in range(PIECES)]
    start_low = remote(
        spot(start, side, STEPS, STEPS), spot(start, side, low_place, STEPS),
        slot_of["start_edge"], tm, space - 2,
    )
    start_high = remote(
        spot(start, side, block, STEPS), spot(start, side, high_place, STEPS),
        slot_of["start_edge"], tm, space + 2,
    )
    reach_rate = STEPS - 1
    rate_low_spot = lane_half(spot(rate, side, low_place, reach_rate), core)
    rate_high_spot = lane_half(spot(rate, side, high_place + 1, reach_rate), core)
    rate_low = remote(
        lane_half(spot(rate, side, STEPS, reach_rate), core), rate_low_spot,
        slot_of["rate_edge"], tm, space - 2,
    )
    rate_high = remote(
        lane_half(spot(rate, side, STEPS + block - reach_rate, reach_rate), core), rate_high_spot,
        slot_of["rate_edge"] + 1, tm, space + 2,
    )
    rate_other_spot = lane_half(spot(rate, side, other, planes), core)
    twin_mate = remote(rate_other_spot, rate_other_spot, slot_of["rate_core"], twin, space)
    twin_low = remote(rate_low_spot, rate_low_spot, slot_of["rate_core"] + 1, twin, space)
    twin_high = remote(rate_high_spot, rate_high_spot, slot_of["rate_core"] + 2, twin, space)

    own_low = jnp.logical_and(side == 0, has_low)
    own_high = jnp.logical_and(side == 1, has_high)
    other_low = jnp.logical_and(side == 1, has_low)
    other_high = jnp.logical_and(side == 0, has_high)

    rate_own.wait()
    pl.when(own_low)(rate_low.start)
    pl.when(own_high)(rate_high.start)

    @pl.when(tm == 0)
    def _():
        initial_own.wait()

    @pl.when(has_previous)
    def _():
        guess_own.wait_recv()

    pl.when(own_low)(start_low.start)
    pl.when(own_high)(start_high.start)

    rate_mate.wait_recv()
    pl.when(other_low)(rate_low.start)
    pl.when(other_high)(rate_high.start)
    twin_mate.start()

    for piece in range(PIECES):
        guess_mate[piece].wait_recv()
        pl.when(other_low)(start_edges[piece][0].start)
        pl.when(other_high)(start_edges[piece][1].start)

    @pl.when(has_high)
    def _():
        rate_low.wait_recv()
        twin_low.start()

    @pl.when(has_low)
    def _():
        rate_high.wait_recv()
        twin_high.start()

    twin_mate.wait_recv()
    pl.when(has_high)(twin_low.wait_recv)
    pl.when(has_low)(twin_high.wait_recv)

    @pl.when(jnp.logical_and(side == 0, has_high))
    def _():
        start_low.wait_recv()

    @pl.when(jnp.logical_and(side == 1, has_low))
    def _():
        start_high.wait_recv()

    @pl.when(jnp.logical_and(side == 1, has_high))
    def _():
        for low, high in start_edges:
            low.wait_recv()

    @pl.when(jnp.logical_and(side == 0, has_low))
    def _():
        for low, high in start_edges:
            high.wait_recv()

    keep = pltpu.make_async_copy(start, again, local.at[1])

    @pl.when(tm == 0)
    def _():
        keep.start()

    width = start.shape[2]
    lane = lax.broadcasted_iota(jnp.int32, reach.shape, 1)

    def change(ref, z):
        middle = ref[z]
        beside = ref[z + 1] + ref[z - 1]
        beside = beside + pltpu.roll(middle, 1, 0) + pltpu.roll(middle, rows - 1, 0)
        beside = beside + jnp.where(lane == 0, 0.0, pltpu.roll(middle, 1, 1))
        beside = beside + jnp.where(lane == width - 1, 0.0, pltpu.roll(middle, width - 1, 1))
        growth = rate[z] * (fine_growth - fine_growth * (middle * middle))
        return middle, reach[...] * beside + middle * (growth - 6.0 * fine_diffuse)

    def span(step):
        low = jnp.where(has_low, step, max(step, STEPS))
        high = jnp.where(has_high, length - step, min(length - step, STEPS + block))
        return low, high

    def fine(src, dst, step):
        def plane(z, carry):
            middle, delta = change(src, z)
            dst[z] = middle + delta
            return carry

        lax.fori_loop(*span(step), plane, 0)

    fine(start, first, 1)
    fine(first, second, 2)
    fine(second, relaxed, 3)

    given, given_low, given_high = [], [], []
    for piece in range(PIECES):
        slot = slot_of["again_edge"] + 2 * piece
        given.append(
            remote(
                piece_of(relaxed, STEPS, block, piece),
                piece_of(again, STEPS, block, piece),
                slot_of["again"] + piece,
                tm + 1,
                space,
            )
        )
        given_low.append(
            remote(
                piece_of(again, STEPS, STEPS, piece),
                piece_of(again, STEPS + block, STEPS, piece),
                slot,
                tm,
                space - 2,
            )
        )
        given_high.append(
            remote(
                piece_of(again, block, STEPS, piece),
                piece_of(again, 0, STEPS, piece),
                slot + 1,
                tm,
                space + 2,
            )
        )

    @pl.when(has_next)
    def _():
        for piece in range(PIECES):
            given[piece].start()

    @pl.when(tm == 0)
    def _():
        keep.wait()

    @pl.when(has_previous)
    def _():
        for piece in range(PIECES):
            given[piece].wait_recv()
            pl.when(has_low)(given_low[piece].start)
            pl.when(has_high)(given_high[piece].start)
        for piece in range(PIECES):
            pl.when(has_high)(given_low[piece].wait_recv)
            pl.when(has_low)(given_high[piece].wait_recv)

    def first_plane(z, carry):
        middle, delta = change(again, z)
        first[z] = middle + delta
        coarse[z] = middle + coarse_ratio * delta
        return carry

    lax.fori_loop(*span(1), first_plane, 0)
    fine(first, second, 2)

    order = []
    for depth in range(planes):
        order += [STEPS + depth, STEPS + block - 1 - depth]

    def row_span(z):
        at = pl.multiple_of(wide * (1 - side), SUBLANES)
        return (pl.ds(z, 1), pl.ds(at, half + wide), slice(None))

    passed = {
        z: remote(
            after.at[row_span(z)], before.at[row_span(z)], slot_of["chain"] + z - STEPS, tm + 1, space
        )
        for z in order
    }
    low_edge, high_edge = STEPS, STEPS + block - 1
    passed_low = remote(
        before.at[row_span(low_edge)], before.at[row_span(high_edge + 1)],
        slot_of["chain_edge"], tm, space - 2,
    )
    passed_high = remote(
        before.at[row_span(high_edge)], before.at[row_span(low_edge - 1)],
        slot_of["chain_edge"] + 1, tm, space + 2,
    )

    mine = pl.ds(pl.multiple_of(side * half, SUBLANES), half)
    middle_rows = pl.ds(wide, half)
    defect_stay = pltpu.make_async_copy(
        defect.at[pl.ds(slab, planes), middle_rows, :], defect_out.at[:, mine, :], local.at[2]
    )
    defect_go = remote(
        defect.at[pl.ds(other, planes), middle_rows, :], defect_out.at[:, mine, :],
        slot_of["defect"], tm, mate,
    )
    stay, go = {}, {}
    for z in order:
        place = (z - STEPS) % planes
        src = after.at[pl.ds(z, 1), middle_rows, :]
        dst = corrected_out.at[pl.ds(place, 1), mine, :]
        stay[z] = pltpu.make_async_copy(src, dst, local.at[3 + place])
        go[z] = remote(src, dst, slot_of["corrected"] + place, tm, mate)

    def at_home(z):
        return side == (z - STEPS) // planes

    def hand_in(z):
        pl.when(at_home(z))(stay[z].start)
        pl.when(jnp.logical_not(at_home(z)))(go[z].start)

    def last_plane(z):
        middle, delta = change(second, z)
        end = middle + delta
        defect[z] = end - relaxed[z]
        shift = end - coarse[z]
        offset[z] = shift
        after[z] = coarse[z] + shift

    def take_edges():
        passed[low_edge].wait_recv()
        pl.when(has_low)(passed_low.start)
        passed[high_edge].wait_recv()
        pl.when(has_high)(passed_high.start)

    pl.when(tm == 2)(take_edges)
    opens = jnp.logical_and(tm == 1, has_next)
    for index, z in enumerate(order):
        last_plane(z)
        if index:
            pl.when(opens)(passed[order[index - 1]].start)
    pl.when(opens)(passed[order[-1]].start)
    defect_go.start()
    defect_stay.start()

    later = tm > 1

    @pl.when(jnp.logical_not(later))
    def _():
        for z in order:
            hand_in(z)

    @pl.when(later)
    def _():
        pl.when(tm > 2)(take_edges)
        queue = order[2:]
        waiting = set(queue)

        def leave(z):
            pl.when(has_next)(passed[z].start)
            hand_in(z)

        for index, z in enumerate(order):
            while waiting & {z - 1, z, z + 1}:
                come = queue.pop(0)
                waiting.remove(come)
                passed[come].wait_recv()
            if z == low_edge:
                pl.when(has_low)(passed_high.wait_recv)
            if z == high_edge:
                pl.when(has_high)(passed_low.wait_recv)
            middle, delta = change(before, z)
            after[z] = middle + coarse_ratio * delta + offset[z]
            if index:
                leave(order[index - 1])
        leave(order[-1])
        pl.when(has_low)(passed_low.wait_send)
        pl.when(has_high)(passed_high.wait_send)

    onward = jnp.logical_and(tm > 0, has_next)

    @pl.when(is_last)
    def _():
        for copy in initial_mate:
            copy.wait_send()

    @pl.when(has_next)
    def _():
        guess_own.wait_send()
        for copy in guess_mate:
            copy.wait_send()

    rate_mate.wait_send()
    twin_mate.wait_send()
    pl.when(has_high)(twin_low.wait_send)
    pl.when(has_low)(twin_high.wait_send)
    pl.when(has_low)(rate_low.wait_send)
    pl.when(has_high)(rate_high.wait_send)
    pl.when(own_low)(start_low.wait_send)
    pl.when(own_high)(start_high.wait_send)

    @pl.when(other_low)
    def _():
        for low, high in start_edges:
            low.wait_send()

    @pl.when(other_high)
    def _():
        for low, high in start_edges:
            high.wait_send()

    @pl.when(has_next)
    def _():
        for piece in range(PIECES):
            given[piece].wait_send()

    @pl.when(has_previous)
    def _():
        for piece in range(PIECES):
            pl.when(has_low)(given_low[piece].wait_send)
            pl.when(has_high)(given_high[piece].wait_send)

    @pl.when(onward)
    def _():
        for z in order:
            passed[z].wait_send()

    defect_stay.wait()
    defect_go.wait()
    for z in order:
        pl.when(at_home(z))(stay[z].wait)
        pl.when(at_home(z))(go[z].wait_recv)
        pl.when(jnp.logical_not(at_home(z)))(go[z].wait_send)


def quarter_slots(nt, shares):
    kinds = dict(
        start=nt * shares, rate=shares, low_start=nt * shares, high_start=nt * shares,
        low_rate=shares, high_rate=shares,
        low_again=nt, high_again=nt, low_first=1, high_first=1, low_offset=nt, high_offset=nt,
        corrected=nt, defect=nt,
    )
    first, total = {}, 0
    for kind, number in kinds.items():
        first[kind] = total
        total += number
    return first, total


def quarter_kernel(
    nt, ns, planes, inner, wide, recv_of,
    initial, guess, rate_in, corrected_out, defect_out,
    start, again, rate, first, second, coarse, chain, offset, defect, end,
    send, recv,
):
    tm, space = lax.axis_index("tm"), lax.axis_index("space")
    y, core = lax.div(tm, 2), lax.rem(tm, 2)
    pair, x = lax.div(space, 2), lax.rem(space, 2)
    levels, pairs = nt // 2, ns // 2
    length = planes + 2 * STEPS
    outer, most = inner + 2 * wide, inner + 3 * wide
    less = most - wide
    across = initial.shape[1]
    tiles = start.shape[2]
    shares = ROW_SHARES * tiles
    low_own, high_own = STEPS, STEPS + planes
    slab = 2 * pair + core
    has_low, has_high = slab > 0, slab < ns - 1
    edge = y == levels - 1
    inside = jnp.logical_not(edge)
    first_row, last_row = jnp.logical_and(edge, x == 0), jnp.logical_and(edge, x == 1)
    low_to = {"tm": tm + 1 - 2 * core, "space": space - 2 * (1 - core)}
    high_to = {"tm": tm + 1 - 2 * core, "space": space + 2 * core}

    def begin_of(to_y, to_x):
        own_begin = outer + inner * (2 * to_y + to_x)
        begin = jnp.where(to_y == levels - 1, to_x * (across - most), own_begin - wide)
        return pl.multiple_of(begin, SUBLANES)

    my_begin = begin_of(y, x)
    my_part = jnp.where(edge, x * (nt - 1), 1 + 2 * y + x)
    inset = pl.multiple_of(jnp.where(first_row, 0, wide), SUBLANES)
    body = pl.ds(wide, most)

    edge_zero = jnp.zeros((length, tiles, wide, LANES), jnp.float32)
    plane_zero = jnp.zeros((STEPS,) + start.shape[2:], jnp.float32)

    def clear_rows(ref, k):
        @pl.when(first_row)
        def _():
            ref[k, :, :, 0:wide] = edge_zero

        @pl.when(last_row)
        def _():
            ref[k, :, :, wide + most : 2 * wide + most] = edge_zero

    def clear_planes(ref, k):
        @pl.when(jnp.logical_not(has_low))
        def _():
            ref[k, 0:low_own] = plane_zero

        @pl.when(jnp.logical_not(has_high))
        def _():
            ref[k, high_own:length] = plane_zero

    barrier = pltpu.get_barrier_semaphore()
    for dy in range(levels):
        for dx in range(2):
            for dc in range(2):
                if dy or dx or dc:
                    there = {
                        "tm": 2 * lax.rem(y + dy, levels) + lax.rem(core + dc, 2),
                        "space": 2 * pair + lax.rem(x + dx, 2),
                    }
                    pl.semaphore_signal(barrier, inc=1, device_id=there, device_id_type=MESH)
    count = jnp.int32(2 * nt - 1)
    for far, there in (
        (jnp.logical_and(core == 0, has_low), low_to),
        (jnp.logical_and(core == 1, has_high), high_to),
    ):

        @pl.when(far)
        def _(there=there):
            pl.semaphore_signal(barrier, inc=1, device_id=there, device_id_type=MESH)

        count = count + far.astype(jnp.int32)

    for k in range(nt):
        clear_rows(start, k)
        clear_planes(start, k)
    for k in range(nt - 1):
        clear_rows(again, k)
        clear_planes(again, k)
        clear_rows(chain, k)
    clear_rows(first, 0)
    clear_rows(second, 0)
    clear_planes(rate, 0)
    clear_planes(chain, 1)
    for j in range(2, nt - 1):
        clear_planes(offset, j)

    pl.semaphore_wait(barrier, count)

    sends = []
    send_count = [0]

    def launch(make, slot, there, condition, wider):
        number = send_count[0]
        send_count[0] += 1
        for rows, fits in ((most, wider), (less, jnp.logical_not(wider))):
            src, dst = make(rows)
            copy = pltpu.make_async_remote_copy(
                src_ref=src, dst_ref=dst, send_sem=send.at[number], recv_sem=recv.at[slot],
                device_id=there, device_id_type=MESH,
            )
            sends.append((copy, jnp.logical_and(condition, fits)))
            pl.when(jnp.logical_and(condition, fits))(copy.start)

    def local(make, slot, condition):
        for rows, fits in ((most, edge), (less, inside)):
            src, dst = make(rows)
            pl.when(jnp.logical_and(condition, fits))(pltpu.make_async_copy(src, dst, recv.at[slot]).start)

    def arrive(dst_of, slot, condition=True):
        for rows, fits in ((most, edge), (less, inside)):
            dst = dst_of(rows)
            pl.when(jnp.logical_and(condition, fits))(pltpu.make_async_copy(dst, dst, recv.at[slot]).wait)

    own = pl.ds(low_own, planes)
    home = core == x
    away = jnp.logical_not(home)

    cut = -(-most // (ROW_SHARES * SUBLANES)) * SUBLANES

    def piece(rows, share_at):
        down, tile = divmod(share_at, tiles)
        return tile, cut * down, min(cut * (down + 1), rows) - cut * down

    def source(ref, begin, rows, share_at):
        tile, at, size = piece(rows, share_at)
        return ref.at[:, pl.ds(pl.multiple_of(begin + at, SUBLANES), size), pl.ds(tile * LANES, LANES)]

    def place(ref, k, rows, share_at, zs=own):
        tile, at, size = piece(rows, share_at)
        return ref.at[k, zs, tile, pl.ds(wide + at, size), :]

    def filling(src, begin, ref, k, share_at):
        return lambda rows: (source(src, begin, rows, share_at), place(ref, k, rows, share_at))

    for ref, src, kind in ((start, initial, "start"), (rate, rate_in, "rate")):
        for share_at in range(shares):
            local(filling(src, my_begin, ref, 0, share_at), recv_of[kind] + share_at, home)

    there_begin = begin_of(y, 1 - x)
    for share_at in range(shares):
        launch(
            filling(initial, there_begin, start, 0, share_at), recv_of["start"] + share_at,
            {"tm": 2 * y + x, "space": space + 1 - 2 * x}, core == share_at % 2, edge,
        )
    for to_y in range(levels):
        for share_at in range(shares):
            launch(
                filling(rate_in, begin_of(to_y, 1 - x), rate, 0, share_at), recv_of["rate"] + share_at,
                {"tm": 2 * to_y + x, "space": space + 1 - 2 * x},
                jnp.logical_and(y == levels - 1, core == share_at % 2), jnp.bool_(to_y == levels - 1),
            )

    def give_guess(turn):
        gives = jnp.logical_and(tm < nt - 1, core == turn)
        for share_at in range(shares):
            slot = recv_of["start"] + (tm + 1) * shares + share_at
            for dy in range(levels):
                for dx in (1, 0):
                    to_y, to_x = lax.rem(y + dy, levels), lax.rem(x + dx, 2)
                    make = filling(guess, begin_of(to_y, to_x), start, tm + 1, share_at)
                    there = {"tm": 2 * to_y + x, "space": 2 * pair + to_x}
                    if dy or dx:
                        launch(make, slot, there, gives, to_y == levels - 1)
                    else:
                        launch(make, slot, there, jnp.logical_and(gives, away), edge)
                        local(make, slot, jnp.logical_and(gives, home))

    give_guess(0)

    reaches = [jnp.where(inside_of, fine_diffuse, 0.0) for inside_of in (has_low, True, has_high)]
    reaches[1] = fine_diffuse

    def share(view, depth, high_slot, low_slot):
        def low(rows):
            return view(pl.ds(low_own, depth), rows), view(pl.ds(high_own, depth), rows)

        def high(rows):
            return view(pl.ds(high_own - depth, depth), rows), view(pl.ds(low_own - depth, depth), rows)

        launch(low, high_slot, low_to, has_low, edge)
        launch(high, low_slot, high_to, has_high, edge)

    def shared(view, depth, high_slot, low_slot):
        arrive(lambda rows: view(pl.ds(high_own, depth), rows), high_slot, has_high)
        arrive(lambda rows: view(pl.ds(low_own - depth, depth), rows), low_slot, has_low)

    def start_view(k, share_at):
        return lambda zs, rows: place(start, k, rows, share_at, zs)

    def relay_start(k):
        for share_at in range(shares):
            at = k * shares + share_at
            arrive(lambda rows: place(start, k, rows, share_at), recv_of["start"] + at)
            share(start_view(k, share_at), STEPS, recv_of["high_start"] + at, recv_of["low_start"] + at)

    def start_ready(k):
        for share_at in range(shares):
            at = k * shares + share_at
            shared(start_view(k, share_at), STEPS, recv_of["high_start"] + at, recv_of["low_start"] + at)

    def rate_view(share_at):
        return lambda zs, rows: place(rate, 0, rows, share_at, zs)

    def relay_rate():
        for at in range(shares):
            arrive(lambda rows: place(rate, 0, rows, at), recv_of["rate"] + at)
            share(rate_view(at), STEPS - 1, recv_of["high_rate"] + at, recv_of["low_rate"] + at)

    def rate_ready():
        for at in range(shares):
            shared(rate_view(at), STEPS - 1, recv_of["high_rate"] + at, recv_of["low_rate"] + at)

    def body_view(ref, k):
        return lambda zs, rows: ref.at[k, zs, :, pl.ds(wide, rows), :]

    tall = next(number for number in (32, 16, 8) if most % number == 0)
    lane = lax.broadcasted_iota(jnp.int32, (tall, LANES), 1)

    def march(src, k, low, high, emit):
        def block(number, carry):
            at = pl.multiple_of(wide + number * tall, SUBLANES)
            here = pl.ds(at, tall)

            def load(z):
                return [src[k, z, tile, here, :] for tile in range(tiles)]

            under, middle = load(low - 1), load(low)
            for z in range(low, high):
                over = load(z + 1)
                zone = 0 if z < low_own else 1 if z < high_own else 2
                after = [pltpu.roll(part_of, 1, 1) for part_of in middle]
                ahead = [pltpu.roll(part_of, LANES - 1, 1) for part_of in middle]
                for tile in range(tiles):
                    value = middle[tile]
                    left = after[tile - 1] if tile else 0.0
                    right = ahead[tile + 1] if tile + 1 < tiles else 0.0
                    beside = over[tile] + under[tile]
                    beside = beside + src[k, z, tile, pl.ds(at - 1, tall), :] + src[k, z, tile, pl.ds(at + 1, tall), :]
                    beside = beside + jnp.where(lane == 0, left, after[tile])
                    beside = beside + jnp.where(lane == LANES - 1, right, ahead[tile])
                    growth = rate[0, z, tile, here, :] * (fine_growth - fine_growth * (value * value))
                    stepped = reaches[zone] * beside + value * (growth + (1.0 - 6.0 * fine_diffuse))
                    emit((z, tile, here), value, stepped)
                under, middle = middle, over
            return carry

        lax.fori_loop(0, most // tall, block, 0)

    def rough_of(value, stepped):
        return value + coarse_ratio * (stepped - value)

    def put(ref, k, spot, value):
        z, tile, here = spot
        ref[k, z, tile, here, :] = value

    def get(ref, k, spot):
        z, tile, here = spot
        return ref[k, z, tile, here, :]

    def fine(src, source_k, dst, halo, rough=False):
        def emit(spot, value, stepped):
            put(dst, 0, spot, stepped)
            if rough and low_own <= spot[0] < high_own:
                put(coarse, 0, spot, rough_of(value, stepped))

        march(src, source_k, low_own - halo, high_own + halo, emit)

    def own_begin(number):
        return outer + inner * (number - 1) if number else 0

    def hand_in(ref, k, out, kind, j):
        begin = pl.multiple_of(my_begin + inset, SUBLANES)
        slot = recv_of[kind] + my_part

        def make(rows):
            size = outer if rows == most else inner
            src = ref.at[k, own, :, pl.ds(pl.multiple_of(wide + inset, SUBLANES), size), :]
            return src, out.at[:, :, pl.ds(begin, size), :]

        stays = jnp.logical_and(tm == j, home)
        launch(make, slot, {"tm": j, "space": 2 * pair + core}, jnp.logical_not(stays), edge)
        local(make, slot, stays)

    def relax(k):
        fine(start, k, first, STEPS - 1, rough=k == 0)
        fine(first, 0, second, STEPS - 2)

        def emit(spot, value, stepped):
            if k == nt - 1:
                put(defect, k, spot, get(end, 0, spot) - stepped)
                return
            put(again, k, spot, stepped)
            if k == 0:
                put(defect, 0, spot, stepped - stepped)
                base = get(coarse, 0, spot)
                put(chain, 0, spot, base + (stepped - base))

        march(second, 0, low_own, high_own, emit)

    def send_again(k):
        share(body_view(again, k), STEPS, recv_of["high_again"] + k, recv_of["low_again"] + k)

    def finish(k):
        shared(body_view(again, k), STEPS, recv_of["high_again"] + k, recv_of["low_again"] + k)
        fine(again, k, first, STEPS - 1, rough=True)
        fine(first, 0, second, STEPS - 2)

        def emit(spot, value, stepped):
            if k + 1 < nt - 1:
                put(defect, k + 1, spot, stepped - get(again, k + 1, spot))
            else:
                put(end, 0, spot, stepped)
            base = get(coarse, 0, spot)
            if k:
                put(offset, k + 1, spot, stepped - base)
            else:
                put(chain, 1, spot, base + (stepped - base))

        march(second, 0, low_own, high_own, emit)

    def lift_between(j, low, high):
        def emit(spot, value, stepped):
            put(chain, j, spot, rough_of(value, stepped) + get(offset, j, spot))

        march(chain, j - 1, low, high, emit)

    def edges_of(j):
        slots = recv_of["high_offset"] + j, recv_of["low_offset"] + j
        return body_view(offset, j), nt - 1 - j, *slots

    def lift_around(j):
        halo = nt - 1 - j
        if halo:
            shared(*edges_of(j))
            lift_between(j, low_own - halo, low_own)
            lift_between(j, high_own, high_own + halo)

    relay_start(0)
    relay_rate()
    give_guess(1)
    relay_start(1)
    start_ready(0)
    rate_ready()
    relax(0)
    send_again(0)
    hand_in(chain, 0, corrected_out, "corrected", 0)
    hand_in(defect, 0, defect_out, "defect", 0)
    relay_start(2)
    start_ready(1)
    relax(1)
    send_again(1)
    finish(0)
    first_edges = body_view(chain, 1), nt - 2, recv_of["high_first"], recv_of["low_first"]
    share(*first_edges)
    hand_in(chain, 1, corrected_out, "corrected", 1)
    hand_in(defect, 1, defect_out, "defect", 1)
    for j in range(2, nt):
        if j < nt - 1:
            start_ready(j)
            relax(j)
            send_again(j)
        finish(j - 1)
        if j < nt - 1:
            share(*edges_of(j))
            relay_start(j + 1)
            hand_in(defect, j, defect_out, "defect", j)
        if j == 2:
            shared(*first_edges)
        else:
            lift_around(j - 1)
        lift_between(j, low_own, high_own)
        hand_in(chain, j, corrected_out, "corrected", j)
    start_ready(nt - 1)
    relax(nt - 1)
    hand_in(defect, nt - 1, defect_out, "defect", nt - 1)

    for copy, condition in sends:
        pl.when(condition)(copy.wait_send)
    for out, kind in ((corrected_out, "corrected"), (defect_out, "defect")):
        for number in range(nt):
            size = inner if 0 < number < nt - 1 else outer
            dst = out.at[:, :, pl.ds(own_begin(number), size), :]
            pltpu.make_async_copy(dst, dst, recv.at[recv_of[kind] + number]).wait()


def settle_kernel(corrected, defect, corrected_out, defect_out, local):
    copies = []
    for src, dst in ((corrected, corrected_out), (defect, defect_out)):
        for tile in range(src.shape[1]):
            to = dst.at[0, :, :, pl.ds(tile * LANES, LANES)]
            copies.append(pltpu.make_async_copy(src.at[:, tile], to, local.at[len(copies)]))
    for copy in copies:
        copy.start()
    for copy in copies:
        copy.wait()


def settle(corrected, defect):
    planes, tiles, across, lanes = corrected.shape
    shape = jax.ShapeDtypeStruct((1, planes, across, tiles * lanes), jnp.float32)
    return pl.pallas_call(
        settle_kernel,
        out_shape=(shape, shape),
        in_specs=[pl.BlockSpec(memory_space=pl.ANY)] * 2,
        out_specs=[pl.BlockSpec(memory_space=pl.ANY)] * 2,
        scratch_shapes=[pltpu.SemaphoreType.DMA((2 * tiles,))],
        compiler_params=pltpu.CompilerParams(vmem_limit_bytes=1 << 20),
    )(corrected, defect)


def quarter_device(nt, ns, initial, coarse_guess, react_rate):
    planes, across, width = initial.shape
    wide, inner = quarter_rows(nt, across)
    length = planes + 2 * STEPS
    tall = inner + 5 * wide
    tiles = width // LANES
    shares = ROW_SHARES * tiles
    recv_of, recv_total = quarter_slots(nt, shares)

    def field(number):
        return pltpu.VMEM((number, length, tiles, tall, LANES), jnp.float32)

    shape = jax.ShapeDtypeStruct((planes, tiles, across, LANES), jnp.float32)
    corrected, defect = pl.pallas_call(
        functools.partial(quarter_kernel, nt, ns, planes, inner, wide, recv_of),
        out_shape=(shape, shape),
        in_specs=[pl.BlockSpec(memory_space=pltpu.HBM)] * 3,
        out_specs=[pl.BlockSpec(memory_space=pl.ANY)] * 2,
        scratch_shapes=[
            field(nt), field(nt), field(1), field(1), field(1), field(1), field(nt), field(nt), field(nt), field(1),
            pltpu.SemaphoreType.DMA((shares * (4 * nt + nt // 2 + 3) + 6 * nt - 6,)),
            pltpu.SemaphoreType.DMA((recv_total,)),
        ],
        compiler_params=pltpu.CompilerParams(collective_id=0, has_side_effects=True, vmem_limit_bytes=VMEM_BYTES),
    )(*(pltpu.with_memory_space_constraint(ref, pltpu.HBM) for ref in (initial, coarse_guess[0], react_rate)))
    return settle(corrected, defect)


def quarter_rows(nt, across):
    wide = -(-(2 * STEPS + max(nt - 2, 0)) // SUBLANES) * SUBLANES
    return wide, (across - 4 * wide) // nt


def takes_quarters(nt, planes, across, width):
    wide, inner = quarter_rows(nt, across)
    fits = inner > 0 and (across - 4 * wide) % (nt * SUBLANES) == 0 and nt - 2 <= planes
    return nt % 2 == 0 and nt > 2 and planes >= STEPS and width % LANES == 0 and fits


def on_device(nt, ns, initial, coarse_guess, react_rate):
    planes, across, width = initial.shape
    if takes_quarters(nt, planes, across, width):
        return quarter_device(nt, ns, initial, coarse_guess, react_rate)
    half = across // 2
    wide = -(-(2 * STEPS + max(nt - 2, 0)) // SUBLANES) * SUBLANES
    length = 2 * planes + 2 * STEPS
    field = pltpu.VMEM((length, half + 2 * wide, width), jnp.float32)
    slot_of, total = slots(planes)
    shape = jax.ShapeDtypeStruct(initial.shape, jnp.float32)
    corrected, defect = pl.pallas_call(
        functools.partial(kernel, nt, ns, planes, half, wide, slot_of),
        out_shape=(shape, shape),
        in_specs=[pl.BlockSpec(memory_space=pl.ANY)] * 3,
        out_specs=[pl.BlockSpec(memory_space=pl.ANY)] * 2,
        scratch_shapes=[field] * 11
        + [
            pltpu.VMEM((half + 2 * wide, width), jnp.float32),
            pltpu.SemaphoreType.DMA((total,)),
            pltpu.SemaphoreType.DMA((total,)),
            pltpu.SemaphoreType.DMA((3 + planes,)),
        ],
        compiler_params=pltpu.CompilerParams(collective_id=0, has_side_effects=True),
    )(initial, coarse_guess[0], react_rate)
    return corrected[None], defect[None]


def solution(mesh):
    in_specs = (P("space", None, None), P("tm", "space", None, None), P("space", None, None))
    out_specs = (P("tm", "space", None, None), P("tm", "space", None, None))
    return jax.shard_map(
        functools.partial(on_device, mesh.shape["tm"], mesh.shape["space"]),
        mesh=mesh, in_specs=in_specs, out_specs=out_specs, check_vma=False,
    )
```

```python
import functools

import jax
import jax.numpy as jnp
from jax import lax
from jax.experimental import pallas as pl
from jax.experimental.pallas import tpu as pltpu
from jax.sharding import PartitionSpec as P

STEPS = 3
SUBLANES = 8

fine_diffuse = 0.04
fine_growth = 0.05
coarse_ratio = 4.0

MESH = pl.DeviceIdType.MESH

PIECES = 4
LANES = 128
ROW_SHARES = 1
VMEM_BYTES = 40 << 20


def slots(planes):
    kinds = dict(
        start=2 + PIECES, start_edge=1 + PIECES, rate=1, rate_edge=2, rate_core=3, again=PIECES, again_edge=2 * PIECES,
        chain=2 * planes, chain_edge=2, defect=1, corrected=planes,
    )
    first, total = {}, 0
    for kind, number in kinds.items():
        first[kind] = total
        total += number
    return first, total


def kernel(
    nt, ns, planes, half, wide, slot_of,
    initial, guess, rate_in, corrected_out, defect_out,
    start, rate, again, before, first, second, relaxed, coarse, offset, defect, after, reach,
    send, recv, local,
):
    tm, space = lax.axis_index("tm"), lax.axis_index("space")
    pair, side = lax.div(space, 2), lax.rem(space, 2)
    pairs = ns // 2
    mate = space + 1 - 2 * side
    block = 2 * planes
    length = block + 2 * STEPS
    rows = half + 2 * wide
    has_low, has_high = pair > 0, pair < pairs - 1
    has_next, has_previous = tm < nt - 1, tm > 0
    own = pl.ds(STEPS, block)

    for ref in (start, rate, again, before):
        zero_plane = jnp.zeros((STEPS,) + ref.shape[1:], jnp.float32)
        zero_rows = jnp.zeros((block, wide, ref.shape[2]), jnp.float32)
        ref[0:STEPS] = zero_plane
        ref[STEPS + block : length] = zero_plane
        ref[STEPS : STEPS + block, 0:wide] = zero_rows
        ref[STEPS : STEPS + block, wide + half : rows] = zero_rows

    barrier = pltpu.get_barrier_semaphore()
    count = jnp.int32(0)
    for step in (-1, 0, 1):
        for place in ("own", "mate", "low", "high"):
            if step == 0 and place == "own":
                continue
            there = {"own": space, "mate": mate, "low": space - 2, "high": space + 2}[place]
            tests = []
            if step:
                tests.append(has_next if step > 0 else has_previous)
            if place in ("low", "high"):
                tests.append(has_low if place == "low" else has_high)
            target = {"tm": tm + step, "space": there}
            if tests:
                valid = functools.reduce(jnp.logical_and, tests)

                @pl.when(valid)
                def _(target=target):
                    pl.semaphore_signal(barrier, inc=1, device_id=target, device_id_type=MESH)

                count = count + valid.astype(jnp.int32)
            else:
                pl.semaphore_signal(barrier, inc=1, device_id=target, device_id_type=MESH)
                count = count + 1
    for here, there in ((tm == 0, nt - 1), (tm == nt - 1, 0)):

        @pl.when(here)
        def _(there=there):
            pl.semaphore_signal(
                barrier, inc=1, device_id={"tm": there, "space": mate}, device_id_type=MESH
            )

        count = count + here.astype(jnp.int32)
    pl.semaphore_wait(barrier, count)

    def remote(src, dst, slot, to_tm, to_space):
        return pltpu.make_async_remote_copy(
            src_ref=src,
            dst_ref=dst,
            send_sem=send.at[slot],
            recv_sem=recv.at[slot],
            device_id={"tm": to_tm, "space": to_space},
            device_id_type=MESH,
        )

    def cut(ref, target):
        return ref.at[:, pl.ds(pl.multiple_of(target * (half - wide), SUBLANES), half + wide), :]

    def spot(ref, target, begin, size):
        at = pl.multiple_of(wide * (1 - target), SUBLANES)
        return ref.at[pl.ds(begin, size), pl.ds(at, half + wide), :]

    slab = STEPS + planes * side
    other = STEPS + planes * (1 - side)

    core = lax.rem(tm, 2)
    twin = tm + 1 - 2 * core
    lanes = start.shape[2] // 2

    def lane_half(ref, which):
        return ref.at[:, :, pl.ds(pl.multiple_of(which * lanes, lanes), lanes)]

    groups = (half + wide) // SUBLANES
    bounds = [groups * piece // PIECES * SUBLANES for piece in range(PIECES + 1)]

    def piece_of(ref, begin, size, piece, target=side):
        at = pl.multiple_of(wide * (1 - target) + bounds[piece], SUBLANES)
        return ref.at[pl.ds(begin, size), pl.ds(at, bounds[piece + 1] - bounds[piece]), :]

    def cut_piece(ref, target, piece):
        at = pl.multiple_of(target * (half - wide) + bounds[piece], SUBLANES)
        return ref.at[:, pl.ds(at, bounds[piece + 1] - bounds[piece]), :]

    rate_own = pltpu.make_async_copy(cut(rate_in, side), spot(rate, side, slab, planes), local.at[0])
    rate_mate = remote(
        lane_half(cut(rate_in, 1 - side), core),
        lane_half(spot(rate, 1 - side, slab, planes), core),
        slot_of["rate"],
        tm,
        mate,
    )
    initial_own = pltpu.make_async_copy(cut(initial, side), spot(start, side, slab, planes), local.at[1])
    guess_own = remote(
        cut(guess, side), spot(start, side, slab, planes), slot_of["start"], tm + 1, space
    )

    def to_mate(ref, to_tm):
        return [
            remote(
                cut_piece(ref, 1 - side, piece),
                piece_of(start, slab, planes, piece, 1 - side),
                slot_of["start"] + 1 + piece,
                to_tm,
                mate,
            )
            for piece in range(PIECES)
        ]

    guess_mate = to_mate(guess, tm + 1)
    initial_mate = to_mate(initial, 0)
    is_last = tm == nt - 1

    rate_mate.start()
    rate_own.start()

    @pl.when(has_next)
    def _():
        guess_own.start()
        for copy in guess_mate:
            copy.start()

    @pl.when(is_last)
    def _():
        for copy in initial_mate:
            copy.start()

    @pl.when(tm == 0)
    def _():
        initial_own.start()

    for ref in (first, second):
        @pl.when(jnp.logical_not(has_low))
        def _(ref=ref):
            ref[0:STEPS] = jnp.zeros((STEPS,) + ref.shape[1:], jnp.float32)

        @pl.when(jnp.logical_not(has_high))
        def _(ref=ref):
            ref[STEPS + block : length] = jnp.zeros((STEPS,) + ref.shape[1:], jnp.float32)

    row = lax.broadcasted_iota(jnp.int32, reach.shape, 0)
    outside = jnp.logical_or(
        jnp.logical_and(side == 0, row < wide), jnp.logical_and(side == 1, row >= wide + half)
    )
    reach[...] = jnp.where(outside, 0.0, fine_diffuse)

    low_place, high_place = STEPS + block, 0

    def edge_pieces(piece):
        slot = slot_of["start_edge"] + 1 + piece
        low = remote(
            piece_of(start, STEPS, STEPS, piece), piece_of(start, low_place, STEPS, piece),
            slot, tm, space - 2,
        )
        high = remote(
            piece_of(start, block, STEPS, piece), piece_of(start, high_place, STEPS, piece),
            slot, tm, space + 2,
        )
        return low, high

    start_edges = [edge_pieces(piece) for piece in range(PIECES)]
    start_low = remote(
        spot(start, side, STEPS, STEPS), spot(start, side, low_place, STEPS),
        slot_of["start_edge"], tm, space - 2,
    )
    start_high = remote(
        spot(start, side, block, STEPS), spot(start, side, high_place, STEPS),
        slot_of["start_edge"], tm, space + 2,
    )
    reach_rate = STEPS - 1
    rate_low_spot = lane_half(spot(rate, side, low_place, reach_rate), core)
    rate_high_spot = lane_half(spot(rate, side, high_place + 1, reach_rate), core)
    rate_low = remote(
        lane_half(spot(rate, side, STEPS, reach_rate), core), rate_low_spot,
        slot_of["rate_edge"], tm, space - 2,
    )
    rate_high = remote(
        lane_half(spot(rate, side, STEPS + block - reach_rate, reach_rate), core), rate_high_spot,
        slot_of["rate_edge"] + 1, tm, space + 2,
    )
    rate_other_spot = lane_half(spot(rate, side, other, planes), core)
    twin_mate = remote(rate_other_spot, rate_other_spot, slot_of["rate_core"], twin, space)
    twin_low = remote(rate_low_spot, rate_low_spot, slot_of["rate_core"] + 1, twin, space)
    twin_high = remote(rate_high_spot, rate_high_spot, slot_of["rate_core"] + 2, twin, space)

    own_low = jnp.logical_and(side == 0, has_low)
    own_high = jnp.logical_and(side == 1, has_high)
    other_low = jnp.logical_and(side == 1, has_low)
    other_high = jnp.logical_and(side == 0, has_high)

    rate_own.wait()
    pl.when(own_low)(rate_low.start)
    pl.when(own_high)(rate_high.start)

    @pl.when(tm == 0)
    def _():
        initial_own.wait()

    @pl.when(has_previous)
    def _():
        guess_own.wait_recv()

    pl.when(own_low)(start_low.start)
    pl.when(own_high)(start_high.start)

    rate_mate.wait_recv()
    pl.when(other_low)(rate_low.start)
    pl.when(other_high)(rate_high.start)
    twin_mate.start()

    for piece in range(PIECES):
        guess_mate[piece].wait_recv()
        pl.when(other_low)(start_edges[piece][0].start)
        pl.when(other_high)(start_edges[piece][1].start)

    @pl.when(has_high)
    def _():
        rate_low.wait_recv()
        twin_low.start()

    @pl.when(has_low)
    def _():
        rate_high.wait_recv()
        twin_high.start()

    twin_mate.wait_recv()
    pl.when(has_high)(twin_low.wait_recv)
    pl.when(has_low)(twin_high.wait_recv)

    @pl.when(jnp.logical_and(side == 0, has_high))
    def _():
        start_low.wait_recv()

    @pl.when(jnp.logical_and(side == 1, has_low))
    def _():
        start_high.wait_recv()

    @pl.when(jnp.logical_and(side == 1, has_high))
    def _():
        for low, high in start_edges:
            low.wait_recv()

    @pl.when(jnp.logical_and(side == 0, has_low))
    def _():
        for low, high in start_edges:
            high.wait_recv()

    keep = pltpu.make_async_copy(start, again, local.at[1])

    @pl.when(tm == 0)
    def _():
        keep.start()

    width = start.shape[2]
    lane = lax.broadcasted_iota(jnp.int32, reach.shape, 1)

    def change(ref, z):
        middle = ref[z]
        beside = ref[z + 1] + ref[z - 1]
        beside = beside + pltpu.roll(middle, 1, 0) + pltpu.roll(middle, rows - 1, 0)
        beside = beside + jnp.where(lane == 0, 0.0, pltpu.roll(middle, 1, 1))
        beside = beside + jnp.where(lane == width - 1, 0.0, pltpu.roll(middle, width - 1, 1))
        growth = rate[z] * (fine_growth - fine_growth * (middle * middle))
        return middle, reach[...] * beside + middle * (growth - 6.0 * fine_diffuse)

    def span(step):
        low = jnp.where(has_low, step, max(step, STEPS))
        high = jnp.where(has_high, length - step, min(length - step, STEPS + block))
        return low, high

    def fine(src, dst, step):
        def plane(z, carry):
            middle, delta = change(src, z)
            dst[z] = middle + delta
            return carry

        lax.fori_loop(*span(step), plane, 0)

    fine(start, first, 1)
    fine(first, second, 2)
    fine(second, relaxed, 3)

    given, given_low, given_high = [], [], []
    for piece in range(PIECES):
        slot = slot_of["again_edge"] + 2 * piece
        given.append(
            remote(
                piece_of(relaxed, STEPS, block, piece),
                piece_of(again, STEPS, block, piece),
                slot_of["again"] + piece,
                tm + 1,
                space,
            )
        )
        given_low.append(
            remote(
                piece_of(again, STEPS, STEPS, piece),
                piece_of(again, STEPS + block, STEPS, piece),
                slot,
                tm,
                space - 2,
            )
        )
        given_high.append(
            remote(
                piece_of(again, block, STEPS, piece),
                piece_of(again, 0, STEPS, piece),
                slot + 1,
                tm,
                space + 2,
            )
        )

    @pl.when(has_next)
    def _():
        for piece in range(PIECES):
            given[piece].start()

    @pl.when(tm == 0)
    def _():
        keep.wait()

    @pl.when(has_previous)
    def _():
        for piece in range(PIECES):
            given[piece].wait_recv()
            pl.when(has_low)(given_low[piece].start)
            pl.when(has_high)(given_high[piece].start)
        for piece in range(PIECES):
            pl.when(has_high)(given_low[piece].wait_recv)
            pl.when(has_low)(given_high[piece].wait_recv)

    def first_plane(z, carry):
        middle, delta = change(again, z)
        first[z] = middle + delta
        coarse[z] = middle + coarse_ratio * delta
        return carry

    lax.fori_loop(*span(1), first_plane, 0)
    fine(first, second, 2)

    order = []
    for depth in range(planes):
        order += [STEPS + depth, STEPS + block - 1 - depth]

    def row_span(z):
        at = pl.multiple_of(wide * (1 - side), SUBLANES)
        return (pl.ds(z, 1), pl.ds(at, half + wide), slice(None))

    passed = {
        z: remote(
            after.at[row_span(z)], before.at[row_span(z)], slot_of["chain"] + z - STEPS, tm + 1, space
        )
        for z in order
    }
    low_edge, high_edge = STEPS, STEPS + block - 1
    passed_low = remote(
        before.at[row_span(low_edge)], before.at[row_span(high_edge + 1)],
        slot_of["chain_edge"], tm, space - 2,
    )
    passed_high = remote(
        before.at[row_span(high_edge)], before.at[row_span(low_edge - 1)],
        slot_of["chain_edge"] + 1, tm, space + 2,
    )

    mine = pl.ds(pl.multiple_of(side * half, SUBLANES), half)
    middle_rows = pl.ds(wide, half)
    defect_stay = pltpu.make_async_copy(
        defect.at[pl.ds(slab, planes), middle_rows, :], defect_out.at[:, mine, :], local.at[2]
    )
    defect_go = remote(
        defect.at[pl.ds(other, planes), middle_rows, :], defect_out.at[:, mine, :],
        slot_of["defect"], tm, mate,
    )
    stay, go = {}, {}
    for z in order:
        place = (z - STEPS) % planes
        src = after.at[pl.ds(z, 1), middle_rows, :]
        dst = corrected_out.at[pl.ds(place, 1), mine, :]
        stay[z] = pltpu.make_async_copy(src, dst, local.at[3 + place])
        go[z] = remote(src, dst, slot_of["corrected"] + place, tm, mate)

    def at_home(z):
        return side == (z - STEPS) // planes

    def hand_in(z):
        pl.when(at_home(z))(stay[z].start)
        pl.when(jnp.logical_not(at_home(z)))(go[z].start)

    def last_plane(z):
        middle, delta = change(second, z)
        end = middle + delta
        defect[z] = end - relaxed[z]
        shift = end - coarse[z]
        offset[z] = shift
        after[z] = coarse[z] + shift

    def take_edges():
        passed[low_edge].wait_recv()
        pl.when(has_low)(passed_low.start)
        passed[high_edge].wait_recv()
        pl.when(has_high)(passed_high.start)

    pl.when(tm == 2)(take_edges)
    opens = jnp.logical_and(tm == 1, has_next)
    for index, z in enumerate(order):
        last_plane(z)
        if index:
            pl.when(opens)(passed[order[index - 1]].start)
    pl.when(opens)(passed[order[-1]].start)
    defect_go.start()
    defect_stay.start()

    later = tm > 1

    @pl.when(jnp.logical_not(later))
    def _():
        for z in order:
            hand_in(z)

    @pl.when(later)
    def _():
        pl.when(tm > 2)(take_edges)
        queue = order[2:]
        waiting = set(queue)

        def leave(z):
            pl.when(has_next)(passed[z].start)
            hand_in(z)

        for index, z in enumerate(order):
            while waiting & {z - 1, z, z + 1}:
                come = queue.pop(0)
                waiting.remove(come)
                passed[come].wait_recv()
            if z == low_edge:
                pl.when(has_low)(passed_high.wait_recv)
            if z == high_edge:
                pl.when(has_high)(passed_low.wait_recv)
            middle, delta = change(before, z)
            after[z] = middle + coarse_ratio * delta + offset[z]
            if index:
                leave(order[index - 1])
        leave(order[-1])
        pl.when(has_low)(passed_low.wait_send)
        pl.when(has_high)(passed_high.wait_send)

    onward = jnp.logical_and(tm > 0, has_next)

    @pl.when(is_last)
    def _():
        for copy in initial_mate:
            copy.wait_send()

    @pl.when(has_next)
    def _():
        guess_own.wait_send()
        for copy in guess_mate:
            copy.wait_send()

    rate_mate.wait_send()
    twin_mate.wait_send()
    pl.when(has_high)(twin_low.wait_send)
    pl.when(has_low)(twin_high.wait_send)
    pl.when(has_low)(rate_low.wait_send)
    pl.when(has_high)(rate_high.wait_send)
    pl.when(own_low)(start_low.wait_send)
    pl.when(own_high)(start_high.wait_send)

    @pl.when(other_low)
    def _():
        for low, high in start_edges:
            low.wait_send()

    @pl.when(other_high)
    def _():
        for low, high in start_edges:
            high.wait_send()

    @pl.when(has_next)
    def _():
        for piece in range(PIECES):
            given[piece].wait_send()

    @pl.when(has_previous)
    def _():
        for piece in range(PIECES):
            pl.when(has_low)(given_low[piece].wait_send)
            pl.when(has_high)(given_high[piece].wait_send)

    @pl.when(onward)
    def _():
        for z in order:
            passed[z].wait_send()

    defect_stay.wait()
    defect_go.wait()
    for z in order:
        pl.when(at_home(z))(stay[z].wait)
        pl.when(at_home(z))(go[z].wait_recv)
        pl.when(jnp.logical_not(at_home(z)))(go[z].wait_send)


def quarter_slots(nt, shares):
    kinds = dict(
        start=nt * shares, rate=shares, low_start=nt * shares, high_start=nt * shares,
        low_rate=shares, high_rate=shares,
        low_again=nt, high_again=nt, low_first=1, high_first=1, low_offset=nt, high_offset=nt,
        corrected=nt, defect=nt,
    )
    first, total = {}, 0
    for kind, number in kinds.items():
        first[kind] = total
        total += number
    return first, total


def quarter_kernel(
    nt, ns, planes, inner, wide, recv_of,
    initial, guess, rate_in, corrected_out, defect_out,
    start, again, rate, first, second, coarse, chain, offset, defect, end,
    send, recv,
):
    tm, space = lax.axis_index("tm"), lax.axis_index("space")
    y, core = lax.div(tm, 2), lax.rem(tm, 2)
    pair, x = lax.div(space, 2), lax.rem(space, 2)
    levels, pairs = nt // 2, ns // 2
    length = planes + 2 * STEPS
    outer, most = inner + 2 * wide, inner + 3 * wide
    less = most - wide
    across = initial.shape[1]
    tiles = start.shape[2]
    shares = ROW_SHARES * tiles
    low_own, high_own = STEPS, STEPS + planes
    slab = 2 * pair + core
    has_low, has_high = slab > 0, slab < ns - 1
    edge = y == levels - 1
    inside = jnp.logical_not(edge)
    first_row, last_row = jnp.logical_and(edge, x == 0), jnp.logical_and(edge, x == 1)
    low_to = {"tm": tm + 1 - 2 * core, "space": space - 2 * (1 - core)}
    high_to = {"tm": tm + 1 - 2 * core, "space": space + 2 * core}

    def begin_of(to_y, to_x):
        own_begin = outer + inner * (2 * to_y + to_x)
        begin = jnp.where(to_y == levels - 1, to_x * (across - most), own_begin - wide)
        return pl.multiple_of(begin, SUBLANES)

    my_begin = begin_of(y, x)
    my_part = jnp.where(edge, x * (nt - 1), 1 + 2 * y + x)
    inset = pl.multiple_of(jnp.where(first_row, 0, wide), SUBLANES)
    body = pl.ds(wide, most)

    edge_zero = jnp.zeros((length, tiles, wide, LANES), jnp.float32)
    plane_zero = jnp.zeros((STEPS,) + start.shape[2:], jnp.float32)

    def clear_rows(ref, k):
        @pl.when(first_row)
        def _():
            ref[k, :, :, 0:wide] = edge_zero

        @pl.when(last_row)
        def _():
            ref[k, :, :, wide + most : 2 * wide + most] = edge_zero

    def clear_planes(ref, k):
        @pl.when(jnp.logical_not(has_low))
        def _():
            ref[k, 0:low_own] = plane_zero

        @pl.when(jnp.logical_not(has_high))
        def _():
            ref[k, high_own:length] = plane_zero

    barrier = pltpu.get_barrier_semaphore()
    for dy in range(levels):
        for dx in range(2):
            for dc in range(2):
                if dy or dx or dc:
                    there = {
                        "tm": 2 * lax.rem(y + dy, levels) + lax.rem(core + dc, 2),
                        "space": 2 * pair + lax.rem(x + dx, 2),
                    }
                    pl.semaphore_signal(barrier, inc=1, device_id=there, device_id_type=MESH)
    count = jnp.int32(2 * nt - 1)
    for far, there in (
        (jnp.logical_and(core == 0, has_low), low_to),
        (jnp.logical_and(core == 1, has_high), high_to),
    ):

        @pl.when(far)
        def _(there=there):
            pl.semaphore_signal(barrier, inc=1, device_id=there, device_id_type=MESH)

        count = count + far.astype(jnp.int32)

    for k in range(nt):
        clear_rows(start, k)
        clear_planes(start, k)
    for k in range(nt - 1):
        clear_rows(again, k)
        clear_planes(again, k)
        clear_rows(chain, k)
    clear_rows(first, 0)
    clear_rows(second, 0)
    clear_planes(rate, 0)
    clear_planes(chain, 1)
    for j in range(2, nt - 1):
        clear_planes(offset, j)

    pl.semaphore_wait(barrier, count)

    sends = []
    send_count = [0]

    def launch(make, slot, there, condition, wider):
        number = send_count[0]
        send_count[0] += 1
        for rows, fits in ((most, wider), (less, jnp.logical_not(wider))):
            src, dst = make(rows)
            copy = pltpu.make_async_remote_copy(
                src_ref=src, dst_ref=dst, send_sem=send.at[number], recv_sem=recv.at[slot],
                device_id=there, device_id_type=MESH,
            )
            sends.append((copy, jnp.logical_and(condition, fits)))
            pl.when(jnp.logical_and(condition, fits))(copy.start)

    def local(make, slot, condition):
        for rows, fits in ((most, edge), (less, inside)):
            src, dst = make(rows)
            pl.when(jnp.logical_and(condition, fits))(pltpu.make_async_copy(src, dst, recv.at[slot]).start)

    def arrive(dst_of, slot, condition=True):
        for rows, fits in ((most, edge), (less, inside)):
            dst = dst_of(rows)
            pl.when(jnp.logical_and(condition, fits))(pltpu.make_async_copy(dst, dst, recv.at[slot]).wait)

    own = pl.ds(low_own, planes)
    home = core == x
    away = jnp.logical_not(home)

    cut = -(-most // (ROW_SHARES * SUBLANES)) * SUBLANES

    def piece(rows, share_at):
        down, tile = divmod(share_at, tiles)
        return tile, cut * down, min(cut * (down + 1), rows) - cut * down

    def source(ref, begin, rows, share_at):
        tile, at, size = piece(rows, share_at)
        return ref.at[:, pl.ds(pl.multiple_of(begin + at, SUBLANES), size), pl.ds(tile * LANES, LANES)]

    def place(ref, k, rows, share_at, zs=own):
        tile, at, size = piece(rows, share_at)
        return ref.at[k, zs, tile, pl.ds(wide + at, size), :]

    def filling(src, begin, ref, k, share_at):
        return lambda rows: (source(src, begin, rows, share_at), place(ref, k, rows, share_at))

    for ref, src, kind in ((start, initial, "start"), (rate, rate_in, "rate")):
        for share_at in range(shares):
            local(filling(src, my_begin, ref, 0, share_at), recv_of[kind] + share_at, home)

    there_begin = begin_of(y, 1 - x)
    for share_at in range(shares):
        launch(
            filling(initial, there_begin, start, 0, share_at), recv_of["start"] + share_at,
            {"tm": 2 * y + x, "space": space + 1 - 2 * x}, core == share_at % 2, edge,
        )
    for to_y in range(levels):
        for share_at in range(shares):
            launch(
                filling(rate_in, begin_of(to_y, 1 - x), rate, 0, share_at), recv_of["rate"] + share_at,
                {"tm": 2 * to_y + x, "space": space + 1 - 2 * x},
                jnp.logical_and(y == levels - 1, core == share_at % 2), jnp.bool_(to_y == levels - 1),
            )

    def give_guess(turn):
        gives = jnp.logical_and(tm < nt - 1, core == turn)
        for share_at in range(shares):
            slot = recv_of["start"] + (tm + 1) * shares + share_at
            for dy in range(levels):
                for dx in (1, 0):
                    to_y, to_x = lax.rem(y + dy, levels), lax.rem(x + dx, 2)
                    make = filling(guess, begin_of(to_y, to_x), start, tm + 1, share_at)
                    there = {"tm": 2 * to_y + x, "space": 2 * pair + to_x}
                    if dy or dx:
                        launch(make, slot, there, gives, to_y == levels - 1)
                    else:
                        launch(make, slot, there, jnp.logical_and(gives, away), edge)
                        local(make, slot, jnp.logical_and(gives, home))

    give_guess(0)

    reaches = [jnp.where(inside_of, fine_diffuse, 0.0) for inside_of in (has_low, True, has_high)]
    reaches[1] = fine_diffuse

    def share(view, depth, high_slot, low_slot):
        def low(rows):
            return view(pl.ds(low_own, depth), rows), view(pl.ds(high_own, depth), rows)

        def high(rows):
            return view(pl.ds(high_own - depth, depth), rows), view(pl.ds(low_own - depth, depth), rows)

        launch(low, high_slot, low_to, has_low, edge)
        launch(high, low_slot, high_to, has_high, edge)

    def shared(view, depth, high_slot, low_slot):
        arrive(lambda rows: view(pl.ds(high_own, depth), rows), high_slot, has_high)
        arrive(lambda rows: view(pl.ds(low_own - depth, depth), rows), low_slot, has_low)

    def start_view(k, share_at):
        return lambda zs, rows: place(start, k, rows, share_at, zs)

    def relay_start(k):
        for share_at in range(shares):
            at = k * shares + share_at
            arrive(lambda rows: place(start, k, rows, share_at), recv_of["start"] + at)
            share(start_view(k, share_at), STEPS, recv_of["high_start"] + at, recv_of["low_start"] + at)

    def start_ready(k):
        for share_at in range(shares):
            at = k * shares + share_at
            shared(start_view(k, share_at), STEPS, recv_of["high_start"] + at, recv_of["low_start"] + at)

    def rate_view(share_at):
        return lambda zs, rows: place(rate, 0, rows, share_at, zs)

    def relay_rate():
        for at in range(shares):
            arrive(lambda rows: place(rate, 0, rows, at), recv_of["rate"] + at)
            share(rate_view(at), STEPS - 1, recv_of["high_rate"] + at, recv_of["low_rate"] + at)

    def rate_ready():
        for at in range(shares):
            shared(rate_view(at), STEPS - 1, recv_of["high_rate"] + at, recv_of["low_rate"] + at)

    def body_view(ref, k):
        return lambda zs, rows: ref.at[k, zs, :, pl.ds(wide, rows), :]

    tall = next(number for number in (32, 16, 8) if most % number == 0)
    lane = lax.broadcasted_iota(jnp.int32, (tall, LANES), 1)

    def march(src, k, low, high, emit):
        def block(number, carry):
            at = pl.multiple_of(wide + number * tall, SUBLANES)
            here = pl.ds(at, tall)

            def load(z):
                return [src[k, z, tile, here, :] for tile in range(tiles)]

            under, middle = load(low - 1), load(low)
            for z in range(low, high):
                over = load(z + 1)
                zone = 0 if z < low_own else 1 if z < high_own else 2
                after = [pltpu.roll(part_of, 1, 1) for part_of in middle]
                ahead = [pltpu.roll(part_of, LANES - 1, 1) for part_of in middle]
                for tile in range(tiles):
                    value = middle[tile]
                    left = after[tile - 1] if tile else 0.0
                    right = ahead[tile + 1] if tile + 1 < tiles else 0.0
                    beside = over[tile] + under[tile]
                    beside = beside + src[k, z, tile, pl.ds(at - 1, tall), :] + src[k, z, tile, pl.ds(at + 1, tall), :]
                    beside = beside + jnp.where(lane == 0, left, after[tile])
                    beside = beside + jnp.where(lane == LANES - 1, right, ahead[tile])
                    growth = rate[0, z, tile, here, :] * (fine_growth - fine_growth * (value * value))
                    stepped = reaches[zone] * beside + value * (growth + (1.0 - 6.0 * fine_diffuse))
                    emit((z, tile, here), value, stepped)
                under, middle = middle, over
            return carry

        lax.fori_loop(0, most // tall, block, 0)

    def rough_of(value, stepped):
        return value + coarse_ratio * (stepped - value)

    def put(ref, k, spot, value):
        z, tile, here = spot
        ref[k, z, tile, here, :] = value

    def get(ref, k, spot):
        z, tile, here = spot
        return ref[k, z, tile, here, :]

    def fine(src, source_k, dst, halo, rough=False):
        def emit(spot, value, stepped):
            put(dst, 0, spot, stepped)
            if rough and low_own <= spot[0] < high_own:
                put(coarse, 0, spot, rough_of(value, stepped))

        march(src, source_k, low_own - halo, high_own + halo, emit)

    def own_begin(number):
        return outer + inner * (number - 1) if number else 0

    def hand_in(ref, k, out, kind, j):
        begin = pl.multiple_of(my_begin + inset, SUBLANES)
        slot = recv_of[kind] + my_part

        def make(rows):
            size = outer if rows == most else inner
            src = ref.at[k, own, :, pl.ds(pl.multiple_of(wide + inset, SUBLANES), size), :]
            return src, out.at[:, :, pl.ds(begin, size), :]

        stays = jnp.logical_and(tm == j, home)
        launch(make, slot, {"tm": j, "space": 2 * pair + core}, jnp.logical_not(stays), edge)
        local(make, slot, stays)

    def relax(k):
        fine(start, k, first, STEPS - 1, rough=k == 0)
        fine(first, 0, second, STEPS - 2)

        def emit(spot, value, stepped):
            if k == nt - 1:
                put(defect, k, spot, get(end, 0, spot) - stepped)
                return
            put(again, k, spot, stepped)
            if k == 0:
                put(defect, 0, spot, stepped - stepped)
                base = get(coarse, 0, spot)
                put(chain, 0, spot, base + (stepped - base))

        march(second, 0, low_own, high_own, emit)

    def send_again(k):
        share(body_view(again, k), STEPS, recv_of["high_again"] + k, recv_of["low_again"] + k)

    def finish(k):
        shared(body_view(again, k), STEPS, recv_of["high_again"] + k, recv_of["low_again"] + k)
        fine(again, k, first, STEPS - 1, rough=True)
        fine(first, 0, second, STEPS - 2)

        def emit(spot, value, stepped):
            if k + 1 < nt - 1:
                put(defect, k + 1, spot, stepped - get(again, k + 1, spot))
            else:
                put(end, 0, spot, stepped)
            base = get(coarse, 0, spot)
            if k:
                put(offset, k + 1, spot, stepped - base)
            else:
                put(chain, 1, spot, base + (stepped - base))

        march(second, 0, low_own, high_own, emit)

    def lift_between(j, low, high):
        def emit(spot, value, stepped):
            put(chain, j, spot, rough_of(value, stepped) + get(offset, j, spot))

        march(chain, j - 1, low, high, emit)

    def edges_of(j):
        slots = recv_of["high_offset"] + j, recv_of["low_offset"] + j
        return body_view(offset, j), nt - 1 - j, *slots

    def lift_around(j):
        halo = nt - 1 - j
        if halo:
            shared(*edges_of(j))
            lift_between(j, low_own - halo, low_own)
            lift_between(j, high_own, high_own + halo)

    relay_start(0)
    relay_rate()
    give_guess(1)
    relay_start(1)
    start_ready(0)
    rate_ready()
    relax(0)
    send_again(0)
    hand_in(chain, 0, corrected_out, "corrected", 0)
    hand_in(defect, 0, defect_out, "defect", 0)
    relay_start(2)
    start_ready(1)
    relax(1)
    send_again(1)
    finish(0)
    first_edges = body_view(chain, 1), nt - 2, recv_of["high_first"], recv_of["low_first"]
    share(*first_edges)
    hand_in(chain, 1, corrected_out, "corrected", 1)
    hand_in(defect, 1, defect_out, "defect", 1)
    for j in range(2, nt):
        if j < nt - 1:
            start_ready(j)
            relax(j)
            send_again(j)
        finish(j - 1)
        if j < nt - 1:
            share(*edges_of(j))
            relay_start(j + 1)
            hand_in(defect, j, defect_out, "defect", j)
        if j == 2:
            shared(*first_edges)
        else:
            lift_around(j - 1)
        lift_between(j, low_own, high_own)
        hand_in(chain, j, corrected_out, "corrected", j)
    start_ready(nt - 1)
    relax(nt - 1)
    hand_in(defect, nt - 1, defect_out, "defect", nt - 1)

    for copy, condition in sends:
        pl.when(condition)(copy.wait_send)
    for out, kind in ((corrected_out, "corrected"), (defect_out, "defect")):
        for number in range(nt):
            size = inner if 0 < number < nt - 1 else outer
            dst = out.at[:, :, pl.ds(own_begin(number), size), :]
            pltpu.make_async_copy(dst, dst, recv.at[recv_of[kind] + number]).wait()


def settle_kernel(corrected, defect, corrected_out, defect_out, local):
    copies = []
    for src, dst in ((corrected, corrected_out), (defect, defect_out)):
        for tile in range(src.shape[1]):
            to = dst.at[0, :, :, pl.ds(tile * LANES, LANES)]
            copies.append(pltpu.make_async_copy(src.at[:, tile], to, local.at[len(copies)]))
    for copy in copies:
        copy.start()
    for copy in copies:
        copy.wait()


def settle(corrected, defect):
    planes, tiles, across, lanes = corrected.shape
    shape = jax.ShapeDtypeStruct((1, planes, across, tiles * lanes), jnp.float32)
    return pl.pallas_call(
        settle_kernel,
        out_shape=(shape, shape),
        in_specs=[pl.BlockSpec(memory_space=pl.ANY)] * 2,
        out_specs=[pl.BlockSpec(memory_space=pl.ANY)] * 2,
        scratch_shapes=[pltpu.SemaphoreType.DMA((2 * tiles,))],
        compiler_params=pltpu.CompilerParams(vmem_limit_bytes=1 << 20),
    )(corrected, defect)


def quarter_device(nt, ns, initial, coarse_guess, react_rate):
    planes, across, width = initial.shape
    wide, inner = quarter_rows(nt, across)
    length = planes + 2 * STEPS
    tall = inner + 5 * wide
    tiles = width // LANES
    shares = ROW_SHARES * tiles
    recv_of, recv_total = quarter_slots(nt, shares)

    def field(number):
        return pltpu.VMEM((number, length, tiles, tall, LANES), jnp.float32)

    shape = jax.ShapeDtypeStruct((planes, tiles, across, LANES), jnp.float32)
    corrected, defect = pl.pallas_call(
        functools.partial(quarter_kernel, nt, ns, planes, inner, wide, recv_of),
        out_shape=(shape, shape),
        in_specs=[pl.BlockSpec(memory_space=pltpu.HBM)] * 3,
        out_specs=[pl.BlockSpec(memory_space=pl.ANY)] * 2,
        scratch_shapes=[
            field(nt), field(nt), field(1), field(1), field(1), field(1), field(nt), field(nt), field(nt), field(1),
            pltpu.SemaphoreType.DMA((shares * (4 * nt + nt // 2 + 3) + 6 * nt - 6,)),
            pltpu.SemaphoreType.DMA((recv_total,)),
        ],
        compiler_params=pltpu.CompilerParams(collective_id=0, has_side_effects=True, vmem_limit_bytes=VMEM_BYTES),
    )(*(pltpu.with_memory_space_constraint(ref, pltpu.HBM) for ref in (initial, coarse_guess[0], react_rate)))
    return settle(corrected, defect)


def quarter_rows(nt, across):
    wide = -(-(2 * STEPS + max(nt - 2, 0)) // SUBLANES) * SUBLANES
    return wide, (across - 4 * wide) // nt


def takes_quarters(nt, planes, across, width):
    wide, inner = quarter_rows(nt, across)
    fits = inner > 0 and (across - 4 * wide) % (nt * SUBLANES) == 0 and nt - 2 <= planes
    return nt % 2 == 0 and nt > 2 and planes >= STEPS and width % LANES == 0 and fits


def on_device(nt, ns, initial, coarse_guess, react_rate):
    planes, across, width = initial.shape
    if takes_quarters(nt, planes, across, width):
        return quarter_device(nt, ns, initial, coarse_guess, react_rate)
    half = across // 2
    wide = -(-(2 * STEPS + max(nt - 2, 0)) // SUBLANES) * SUBLANES
    length = 2 * planes + 2 * STEPS
    field = pltpu.VMEM((length, half + 2 * wide, width), jnp.float32)
    slot_of, total = slots(planes)
    shape = jax.ShapeDtypeStruct(initial.shape, jnp.float32)
    corrected, defect = pl.pallas_call(
        functools.partial(kernel, nt, ns, planes, half, wide, slot_of),
        out_shape=(shape, shape),
        in_specs=[pl.BlockSpec(memory_space=pl.ANY)] * 3,
        out_specs=[pl.BlockSpec(memory_space=pl.ANY)] * 2,
        scratch_shapes=[field] * 11
        + [
            pltpu.VMEM((half + 2 * wide, width), jnp.float32),
            pltpu.SemaphoreType.DMA((total,)),
            pltpu.SemaphoreType.DMA((total,)),
            pltpu.SemaphoreType.DMA((3 + planes,)),
        ],
        compiler_params=pltpu.CompilerParams(collective_id=0, has_side_effects=True),
    )(initial, coarse_guess[0], react_rate)
    return corrected[None], defect[None]


def solution(mesh):
    in_specs = (P("space", None, None), P("tm", "space", None, None), P("space", None, None))
    out_specs = (P("tm", "space", None, None), P("tm", "space", None, None))
    return jax.shard_map(
        functools.partial(on_device, mesh.shape["tm"], mesh.shape["space"]),
        mesh=mesh, in_specs=in_specs, out_specs=out_specs, check_vma=False,
    )
```

```python
import functools

import jax
import jax.numpy as jnp
from jax import lax
from jax.experimental import pallas as pl
from jax.experimental.pallas import tpu as pltpu
from jax.sharding import PartitionSpec as P

STEPS = 3
SUBLANES = 8

fine_diffuse = 0.04
fine_growth = 0.05
coarse_ratio = 4.0

MESH = pl.DeviceIdType.MESH

PIECES = 4
LANES = 128
CORES = 2
VMEM_BYTES = 40 << 20


def slots(planes):
    kinds = dict(
        start=2 + PIECES, start_edge=1 + PIECES, rate=1, rate_edge=2, rate_core=3, again=PIECES, again_edge=2 * PIECES,
        chain=2 * planes, chain_edge=2, defect=1, corrected=planes,
    )
    first, total = {}, 0
    for kind, number in kinds.items():
        first[kind] = total
        total += number
    return first, total


def kernel(
    nt, ns, planes, half, wide, slot_of,
    initial, guess, rate_in, corrected_out, defect_out,
    start, rate, again, before, first, second, relaxed, coarse, offset, defect, after, reach,
    send, recv, local,
):
    tm, space = lax.axis_index("tm"), lax.axis_index("space")
    pair, side = lax.div(space, 2), lax.rem(space, 2)
    pairs = ns // 2
    mate = space + 1 - 2 * side
    block = 2 * planes
    length = block + 2 * STEPS
    rows = half + 2 * wide
    has_low, has_high = pair > 0, pair < pairs - 1
    has_next, has_previous = tm < nt - 1, tm > 0
    own = pl.ds(STEPS, block)

    for ref in (start, rate, again, before):
        zero_plane = jnp.zeros((STEPS,) + ref.shape[1:], jnp.float32)
        zero_rows = jnp.zeros((block, wide, ref.shape[2]), jnp.float32)
        ref[0:STEPS] = zero_plane
        ref[STEPS + block : length] = zero_plane
        ref[STEPS : STEPS + block, 0:wide] = zero_rows
        ref[STEPS : STEPS + block, wide + half : rows] = zero_rows

    barrier = pltpu.get_barrier_semaphore()
    count = jnp.int32(0)
    for step in (-1, 0, 1):
        for place in ("own", "mate", "low", "high"):
            if step == 0 and place == "own":
                continue
            there = {"own": space, "mate": mate, "low": space - 2, "high": space + 2}[place]
            tests = []
            if step:
                tests.append(has_next if step > 0 else has_previous)
            if place in ("low", "high"):
                tests.append(has_low if place == "low" else has_high)
            target = {"tm": tm + step, "space": there}
            if tests:
                valid = functools.reduce(jnp.logical_and, tests)

                @pl.when(valid)
                def _(target=target):
                    pl.semaphore_signal(barrier, inc=1, device_id=target, device_id_type=MESH)

                count = count + valid.astype(jnp.int32)
            else:
                pl.semaphore_signal(barrier, inc=1, device_id=target, device_id_type=MESH)
                count = count + 1
    for here, there in ((tm == 0, nt - 1), (tm == nt - 1, 0)):

        @pl.when(here)
        def _(there=there):
            pl.semaphore_signal(
                barrier, inc=1, device_id={"tm": there, "space": mate}, device_id_type=MESH
            )

        count = count + here.astype(jnp.int32)
    pl.semaphore_wait(barrier, count)

    def remote(src, dst, slot, to_tm, to_space):
        return pltpu.make_async_remote_copy(
            src_ref=src,
            dst_ref=dst,
            send_sem=send.at[slot],
            recv_sem=recv.at[slot],
            device_id={"tm": to_tm, "space": to_space},
            device_id_type=MESH,
        )

    def cut(ref, target):
        return ref.at[:, pl.ds(pl.multiple_of(target * (half - wide), SUBLANES), half + wide), :]

    def spot(ref, target, begin, size):
        at = pl.multiple_of(wide * (1 - target), SUBLANES)
        return ref.at[pl.ds(begin, size), pl.ds(at, half + wide), :]

    slab = STEPS + planes * side
    other = STEPS + planes * (1 - side)

    core = lax.rem(tm, 2)
    twin = tm + 1 - 2 * core
    lanes = start.shape[2] // 2

    def lane_half(ref, which):
        return ref.at[:, :, pl.ds(pl.multiple_of(which * lanes, lanes), lanes)]

    groups = (half + wide) // SUBLANES
    bounds = [groups * piece // PIECES * SUBLANES for piece in range(PIECES + 1)]

    def piece_of(ref, begin, size, piece, target=side):
        at = pl.multiple_of(wide * (1 - target) + bounds[piece], SUBLANES)
        return ref.at[pl.ds(begin, size), pl.ds(at, bounds[piece + 1] - bounds[piece]), :]

    def cut_piece(ref, target, piece):
        at = pl.multiple_of(target * (half - wide) + bounds[piece], SUBLANES)
        return ref.at[:, pl.ds(at, bounds[piece + 1] - bounds[piece]), :]

    rate_own = pltpu.make_async_copy(cut(rate_in, side), spot(rate, side, slab, planes), local.at[0])
    rate_mate = remote(
        lane_half(cut(rate_in, 1 - side), core),
        lane_half(spot(rate, 1 - side, slab, planes), core),
        slot_of["rate"],
        tm,
        mate,
    )
    initial_own = pltpu.make_async_copy(cut(initial, side), spot(start, side, slab, planes), local.at[1])
    guess_own = remote(
        cut(guess, side), spot(start, side, slab, planes), slot_of["start"], tm + 1, space
    )

    def to_mate(ref, to_tm):
        return [
            remote(
                cut_piece(ref, 1 - side, piece),
                piece_of(start, slab, planes, piece, 1 - side),
                slot_of["start"] + 1 + piece,
                to_tm,
                mate,
            )
            for piece in range(PIECES)
        ]

    guess_mate = to_mate(guess, tm + 1)
    initial_mate = to_mate(initial, 0)
    is_last = tm == nt - 1

    rate_mate.start()
    rate_own.start()

    @pl.when(has_next)
    def _():
        guess_own.start()
        for copy in guess_mate:
            copy.start()

    @pl.when(is_last)
    def _():
        for copy in initial_mate:
            copy.start()

    @pl.when(tm == 0)
    def _():
        initial_own.start()

    for ref in (first, second):
        @pl.when(jnp.logical_not(has_low))
        def _(ref=ref):
            ref[0:STEPS] = jnp.zeros((STEPS,) + ref.shape[1:], jnp.float32)

        @pl.when(jnp.logical_not(has_high))
        def _(ref=ref):
            ref[STEPS + block : length] = jnp.zeros((STEPS,) + ref.shape[1:], jnp.float32)

    row = lax.broadcasted_iota(jnp.int32, reach.shape, 0)
    outside = jnp.logical_or(
        jnp.logical_and(side == 0, row < wide), jnp.logical_and(side == 1, row >= wide + half)
    )
    reach[...] = jnp.where(outside, 0.0, fine_diffuse)

    low_place, high_place = STEPS + block, 0

    def edge_pieces(piece):
        slot = slot_of["start_edge"] + 1 + piece
        low = remote(
            piece_of(start, STEPS, STEPS, piece), piece_of(start, low_place, STEPS, piece),
            slot, tm, space - 2,
        )
        high = remote(
            piece_of(start, block, STEPS, piece), piece_of(start, high_place, STEPS, piece),
            slot, tm, space + 2,
        )
        return low, high

    start_edges = [edge_pieces(piece) for piece in range(PIECES)]
    start_low = remote(
        spot(start, side, STEPS, STEPS), spot(start, side, low_place, STEPS),
        slot_of["start_edge"], tm, space - 2,
    )
    start_high = remote(
        spot(start, side, block, STEPS), spot(start, side, high_place, STEPS),
        slot_of["start_edge"], tm, space + 2,
    )
    reach_rate = STEPS - 1
    rate_low_spot = lane_half(spot(rate, side, low_place, reach_rate), core)
    rate_high_spot = lane_half(spot(rate, side, high_place + 1, reach_rate), core)
    rate_low = remote(
        lane_half(spot(rate, side, STEPS, reach_rate), core), rate_low_spot,
        slot_of["rate_edge"], tm, space - 2,
    )
    rate_high = remote(
        lane_half(spot(rate, side, STEPS + block - reach_rate, reach_rate), core), rate_high_spot,
        slot_of["rate_edge"] + 1, tm, space + 2,
    )
    rate_other_spot = lane_half(spot(rate, side, other, planes), core)
    twin_mate = remote(rate_other_spot, rate_other_spot, slot_of["rate_core"], twin, space)
    twin_low = remote(rate_low_spot, rate_low_spot, slot_of["rate_core"] + 1, twin, space)
    twin_high = remote(rate_high_spot, rate_high_spot, slot_of["rate_core"] + 2, twin, space)

    own_low = jnp.logical_and(side == 0, has_low)
    own_high = jnp.logical_and(side == 1, has_high)
    other_low = jnp.logical_and(side == 1, has_low)
    other_high = jnp.logical_and(side == 0, has_high)

    rate_own.wait()
    pl.when(own_low)(rate_low.start)
    pl.when(own_high)(rate_high.start)

    @pl.when(tm == 0)
    def _():
        initial_own.wait()

    @pl.when(has_previous)
    def _():
        guess_own.wait_recv()

    pl.when(own_low)(start_low.start)
    pl.when(own_high)(start_high.start)

    rate_mate.wait_recv()
    pl.when(other_low)(rate_low.start)
    pl.when(other_high)(rate_high.start)
    twin_mate.start()

    for piece in range(PIECES):
        guess_mate[piece].wait_recv()
        pl.when(other_low)(start_edges[piece][0].start)
        pl.when(other_high)(start_edges[piece][1].start)

    @pl.when(has_high)
    def _():
        rate_low.wait_recv()
        twin_low.start()

    @pl.when(has_low)
    def _():
        rate_high.wait_recv()
        twin_high.start()

    twin_mate.wait_recv()
    pl.when(has_high)(twin_low.wait_recv)
    pl.when(has_low)(twin_high.wait_recv)

    @pl.when(jnp.logical_and(side == 0, has_high))
    def _():
        start_low.wait_recv()

    @pl.when(jnp.logical_and(side == 1, has_low))
    def _():
        start_high.wait_recv()

    @pl.when(jnp.logical_and(side == 1, has_high))
    def _():
        for low, high in start_edges:
            low.wait_recv()

    @pl.when(jnp.logical_and(side == 0, has_low))
    def _():
        for low, high in start_edges:
            high.wait_recv()

    keep = pltpu.make_async_copy(start, again, local.at[1])

    @pl.when(tm == 0)
    def _():
        keep.start()

    width = start.shape[2]
    lane = lax.broadcasted_iota(jnp.int32, reach.shape, 1)

    def change(ref, z):
        middle = ref[z]
        beside = ref[z + 1] + ref[z - 1]
        beside = beside + pltpu.roll(middle, 1, 0) + pltpu.roll(middle, rows - 1, 0)
        beside = beside + jnp.where(lane == 0, 0.0, pltpu.roll(middle, 1, 1))
        beside = beside + jnp.where(lane == width - 1, 0.0, pltpu.roll(middle, width - 1, 1))
        growth = rate[z] * (fine_growth - fine_growth * (middle * middle))
        return middle, reach[...] * beside + middle * (growth - 6.0 * fine_diffuse)

    def span(step):
        low = jnp.where(has_low, step, max(step, STEPS))
        high = jnp.where(has_high, length - step, min(length - step, STEPS + block))
        return low, high

    def fine(src, dst, step):
        def plane(z, carry):
            middle, delta = change(src, z)
            dst[z] = middle + delta
            return carry

        lax.fori_loop(*span(step), plane, 0)

    fine(start, first, 1)
    fine(first, second, 2)
    fine(second, relaxed, 3)

    given, given_low, given_high = [], [], []
    for piece in range(PIECES):
        slot = slot_of["again_edge"] + 2 * piece
        given.append(
            remote(
                piece_of(relaxed, STEPS, block, piece),
                piece_of(again, STEPS, block, piece),
                slot_of["again"] + piece,
                tm + 1,
                space,
            )
        )
        given_low.append(
            remote(
                piece_of(again, STEPS, STEPS, piece),
                piece_of(again, STEPS + block, STEPS, piece),
                slot,
                tm,
                space - 2,
            )
        )
        given_high.append(
            remote(
                piece_of(again, block, STEPS, piece),
                piece_of(again, 0, STEPS, piece),
                slot + 1,
                tm,
                space + 2,
            )
        )

    @pl.when(has_next)
    def _():
        for piece in range(PIECES):
            given[piece].start()

    @pl.when(tm == 0)
    def _():
        keep.wait()

    @pl.when(has_previous)
    def _():
        for piece in range(PIECES):
            given[piece].wait_recv()
            pl.when(has_low)(given_low[piece].start)
            pl.when(has_high)(given_high[piece].start)
        for piece in range(PIECES):
            pl.when(has_high)(given_low[piece].wait_recv)
            pl.when(has_low)(given_high[piece].wait_recv)

    def first_plane(z, carry):
        middle, delta = change(again, z)
        first[z] = middle + delta
        coarse[z] = middle + coarse_ratio * delta
        return carry

    lax.fori_loop(*span(1), first_plane, 0)
    fine(first, second, 2)

    order = []
    for depth in range(planes):
        order += [STEPS + depth, STEPS + block - 1 - depth]

    def row_span(z):
        at = pl.multiple_of(wide * (1 - side), SUBLANES)
        return (pl.ds(z, 1), pl.ds(at, half + wide), slice(None))

    passed = {
        z: remote(
            after.at[row_span(z)], before.at[row_span(z)], slot_of["chain"] + z - STEPS, tm + 1, space
        )
        for z in order
    }
    low_edge, high_edge = STEPS, STEPS + block - 1
    passed_low = remote(
        before.at[row_span(low_edge)], before.at[row_span(high_edge + 1)],
        slot_of["chain_edge"], tm, space - 2,
    )
    passed_high = remote(
        before.at[row_span(high_edge)], before.at[row_span(low_edge - 1)],
        slot_of["chain_edge"] + 1, tm, space + 2,
    )

    mine = pl.ds(pl.multiple_of(side * half, SUBLANES), half)
    middle_rows = pl.ds(wide, half)
    defect_stay = pltpu.make_async_copy(
        defect.at[pl.ds(slab, planes), middle_rows, :], defect_out.at[:, mine, :], local.at[2]
    )
    defect_go = remote(
        defect.at[pl.ds(other, planes), middle_rows, :], defect_out.at[:, mine, :],
        slot_of["defect"], tm, mate,
    )
    stay, go = {}, {}
    for z in order:
        place = (z - STEPS) % planes
        src = after.at[pl.ds(z, 1), middle_rows, :]
        dst = corrected_out.at[pl.ds(place, 1), mine, :]
        stay[z] = pltpu.make_async_copy(src, dst, local.at[3 + place])
        go[z] = remote(src, dst, slot_of["corrected"] + place, tm, mate)

    def at_home(z):
        return side == (z - STEPS) // planes

    def hand_in(z):
        pl.when(at_home(z))(stay[z].start)
        pl.when(jnp.logical_not(at_home(z)))(go[z].start)

    def last_plane(z):
        middle, delta = change(second, z)
        end = middle + delta
        defect[z] = end - relaxed[z]
        shift = end - coarse[z]
        offset[z] = shift
        after[z] = coarse[z] + shift

    def take_edges():
        passed[low_edge].wait_recv()
        pl.when(has_low)(passed_low.start)
        passed[high_edge].wait_recv()
        pl.when(has_high)(passed_high.start)

    pl.when(tm == 2)(take_edges)
    opens = jnp.logical_and(tm == 1, has_next)
    for index, z in enumerate(order):
        last_plane(z)
        if index:
            pl.when(opens)(passed[order[index - 1]].start)
    pl.when(opens)(passed[order[-1]].start)
    defect_go.start()
    defect_stay.start()

    later = tm > 1

    @pl.when(jnp.logical_not(later))
    def _():
        for z in order:
            hand_in(z)

    @pl.when(later)
    def _():
        pl.when(tm > 2)(take_edges)
        queue = order[2:]
        waiting = set(queue)

        def leave(z):
            pl.when(has_next)(passed[z].start)
            hand_in(z)

        for index, z in enumerate(order):
            while waiting & {z - 1, z, z + 1}:
                come = queue.pop(0)
                waiting.remove(come)
                passed[come].wait_recv()
            if z == low_edge:
                pl.when(has_low)(passed_high.wait_recv)
            if z == high_edge:
                pl.when(has_high)(passed_low.wait_recv)
            middle, delta = change(before, z)
            after[z] = middle + coarse_ratio * delta + offset[z]
            if index:
                leave(order[index - 1])
        leave(order[-1])
        pl.when(has_low)(passed_low.wait_send)
        pl.when(has_high)(passed_high.wait_send)

    onward = jnp.logical_and(tm > 0, has_next)

    @pl.when(is_last)
    def _():
        for copy in initial_mate:
            copy.wait_send()

    @pl.when(has_next)
    def _():
        guess_own.wait_send()
        for copy in guess_mate:
            copy.wait_send()

    rate_mate.wait_send()
    twin_mate.wait_send()
    pl.when(has_high)(twin_low.wait_send)
    pl.when(has_low)(twin_high.wait_send)
    pl.when(has_low)(rate_low.wait_send)
    pl.when(has_high)(rate_high.wait_send)
    pl.when(own_low)(start_low.wait_send)
    pl.when(own_high)(start_high.wait_send)

    @pl.when(other_low)
    def _():
        for low, high in start_edges:
            low.wait_send()

    @pl.when(other_high)
    def _():
        for low, high in start_edges:
            high.wait_send()

    @pl.when(has_next)
    def _():
        for piece in range(PIECES):
            given[piece].wait_send()

    @pl.when(has_previous)
    def _():
        for piece in range(PIECES):
            pl.when(has_low)(given_low[piece].wait_send)
            pl.when(has_high)(given_high[piece].wait_send)

    @pl.when(onward)
    def _():
        for z in order:
            passed[z].wait_send()

    defect_stay.wait()
    defect_go.wait()
    for z in order:
        pl.when(at_home(z))(stay[z].wait)
        pl.when(at_home(z))(go[z].wait_recv)
        pl.when(jnp.logical_not(at_home(z)))(go[z].wait_send)


def quarter_slots(nt, tiles):
    kinds = dict(
        initial=CORES * tiles, rate=CORES * tiles, guess=nt * tiles, low_start=nt * tiles, high_start=nt * tiles,
        low_rate=tiles, high_rate=tiles, low_again=nt, high_again=nt, low_first=1, high_first=1,
        low_offset=nt, high_offset=nt, corrected=nt, defect=nt,
    )
    first, total = {}, 0
    for kind, number in kinds.items():
        first[kind] = total
        total += number
    return first, total


def quarter_kernel(
    nt, ns, planes, inner, wide, recv_of,
    initial, guess, rate_in, corrected_out, defect_out,
    start, again, rate, first, second, coarse, chain, offset, defect, end,
    send, recv,
):
    tm, space = lax.axis_index("tm"), lax.axis_index("space")
    y, core = lax.div(tm, 2), lax.rem(tm, 2)
    pair, x = lax.div(space, 2), lax.rem(space, 2)
    levels, pairs = nt // 2, ns // 2
    length = planes + 2 * STEPS
    outer, most = inner + 2 * wide, inner + 3 * wide
    less = most - wide
    across = initial.shape[1]
    tiles = start.shape[2]
    low_own, high_own = STEPS, STEPS + planes
    slab = 2 * pair + core
    has_low, has_high = slab > 0, slab < ns - 1
    edge = y == levels - 1
    inside = jnp.logical_not(edge)
    first_row, last_row = jnp.logical_and(edge, x == 0), jnp.logical_and(edge, x == 1)
    low_to = {"tm": tm + 1 - 2 * core, "space": space - 2 * (1 - core)}
    high_to = {"tm": tm + 1 - 2 * core, "space": space + 2 * core}

    def begin_of(to_y, to_x):
        own_begin = outer + inner * (2 * to_y + to_x)
        begin = jnp.where(to_y == levels - 1, to_x * (across - most), own_begin - wide)
        return pl.multiple_of(begin, SUBLANES)

    my_begin = begin_of(y, x)
    my_part = jnp.where(edge, x * (nt - 1), 1 + 2 * y + x)
    inset = pl.multiple_of(jnp.where(first_row, 0, wide), SUBLANES)
    body = pl.ds(wide, most)

    edge_zero = jnp.zeros((length, tiles, wide, LANES), jnp.float32)
    plane_zero = jnp.zeros((STEPS,) + start.shape[2:], jnp.float32)

    def clear_rows(ref, k):
        @pl.when(first_row)
        def _():
            ref[k, :, :, 0:wide] = edge_zero

        @pl.when(last_row)
        def _():
            ref[k, :, :, wide + most : 2 * wide + most] = edge_zero

    def clear_planes(ref, k):
        @pl.when(jnp.logical_not(has_low))
        def _():
            ref[k, 0:low_own] = plane_zero

        @pl.when(jnp.logical_not(has_high))
        def _():
            ref[k, high_own:length] = plane_zero

    barrier = pltpu.get_barrier_semaphore()
    for dy in range(levels):
        for dx in range(2):
            for dc in range(2):
                if dy or dx or dc:
                    there = {
                        "tm": 2 * lax.rem(y + dy, levels) + lax.rem(core + dc, 2),
                        "space": 2 * pair + lax.rem(x + dx, 2),
                    }
                    pl.semaphore_signal(barrier, inc=1, device_id=there, device_id_type=MESH)
    count = jnp.int32(2 * nt - 1)
    for far, there in (
        (jnp.logical_and(core == 0, has_low), low_to),
        (jnp.logical_and(core == 1, has_high), high_to),
    ):

        @pl.when(far)
        def _(there=there):
            pl.semaphore_signal(barrier, inc=1, device_id=there, device_id_type=MESH)

        count = count + far.astype(jnp.int32)

    for k in range(nt):
        clear_rows(start, k)
        clear_planes(start, k)
    for k in range(nt - 1):
        clear_rows(again, k)
        clear_planes(again, k)
        clear_rows(chain, k)
    clear_rows(first, 0)
    clear_rows(second, 0)
    clear_planes(rate, 0)
    clear_planes(chain, 1)
    for j in range(2, nt - 1):
        clear_planes(offset, j)

    pl.semaphore_wait(barrier, count)

    sends = []
    send_count = [0]

    def launch(make, slot, there, condition, wider):
        number = send_count[0]
        send_count[0] += 1
        for rows, fits in ((most, wider), (less, jnp.logical_not(wider))):
            src, dst = make(rows)
            copy = pltpu.make_async_remote_copy(
                src_ref=src, dst_ref=dst, send_sem=send.at[number], recv_sem=recv.at[slot],
                device_id=there, device_id_type=MESH,
            )
            sends.append((copy, jnp.logical_and(condition, fits)))
            pl.when(jnp.logical_and(condition, fits))(copy.start)

    def local(make, slot, condition):
        for rows, fits in ((most, edge), (less, inside)):
            src, dst = make(rows)
            pl.when(jnp.logical_and(condition, fits))(pltpu.make_async_copy(src, dst, recv.at[slot]).start)

    def arrive(dst_of, slot, condition=True):
        for rows, fits in ((most, edge), (less, inside)):
            dst = dst_of(rows)
            pl.when(jnp.logical_and(condition, fits))(pltpu.make_async_copy(dst, dst, recv.at[slot]).wait)

    own = pl.ds(low_own, planes)
    home = core == x
    away = jnp.logical_not(home)

    cut = -(-most // (CORES * SUBLANES)) * SUBLANES

    def filling(src, begin, ref, k, tile, turn=None):
        def make(rows):
            at, size = (0, rows) if turn is None else (cut * turn, min(cut * (turn + 1), rows) - cut * turn)
            from_rows = pl.ds(pl.multiple_of(begin + at, SUBLANES), size)
            return src.at[:, from_rows, pl.ds(tile * LANES, LANES)], ref.at[k, own, tile, pl.ds(wide + at, size), :]

        return make

    def arrive_filling(ref, k, tile, slot, turn=None):
        arrive(lambda rows: filling(initial, 0, ref, k, tile, turn)(rows)[1], slot)

    for ref, src, kind in ((start, initial, "initial"), (rate, rate_in, "rate")):
        for tile in range(tiles):
            for turn in range(CORES):
                local(filling(src, my_begin, ref, 0, tile, turn), recv_of[kind] + CORES * tile + turn, home)

    def give_split(src, ref, kind, to_y, condition, wider):
        begin = begin_of(to_y, 1 - x)
        for tile in range(tiles):
            for turn in range(CORES):
                launch(
                    filling(src, begin, ref, 0, tile, turn), recv_of[kind] + CORES * tile + turn,
                    {"tm": 2 * to_y + x, "space": space + 1 - 2 * x}, jnp.logical_and(condition, core == turn), wider,
                )

    give_split(initial, start, "initial", y, jnp.bool_(True), edge)
    for to_y in range(levels):
        give_split(rate_in, rate, "rate", to_y, edge, jnp.bool_(to_y == levels - 1))

    def give_guess(turn):
        gives = jnp.logical_and(tm < nt - 1, core == turn)
        for tile in range(tiles):
            slot = recv_of["guess"] + (tm + 1) * tiles + tile
            for dy in range(levels):
                for dx in (1, 0):
                    to_y, to_x = lax.rem(y + dy, levels), lax.rem(x + dx, 2)
                    make = filling(guess, begin_of(to_y, to_x), start, tm + 1, tile)
                    there = {"tm": 2 * to_y + x, "space": 2 * pair + to_x}
                    if dy or dx:
                        launch(make, slot, there, gives, to_y == levels - 1)
                    else:
                        launch(make, slot, there, jnp.logical_and(gives, away), edge)
                        local(make, slot, jnp.logical_and(gives, home))

    give_guess(0)

    reaches = [jnp.where(inside_of, fine_diffuse, 0.0) for inside_of in (has_low, True, has_high)]
    reaches[1] = fine_diffuse

    def share(view, depth, high_slot, low_slot):
        def low(rows):
            return view(pl.ds(low_own, depth), rows), view(pl.ds(high_own, depth), rows)

        def high(rows):
            return view(pl.ds(high_own - depth, depth), rows), view(pl.ds(low_own - depth, depth), rows)

        launch(low, high_slot, low_to, has_low, edge)
        launch(high, low_slot, high_to, has_high, edge)

    def shared(view, depth, high_slot, low_slot):
        arrive(lambda rows: view(pl.ds(high_own, depth), rows), high_slot, has_high)
        arrive(lambda rows: view(pl.ds(low_own - depth, depth), rows), low_slot, has_low)

    def tile_view(ref, k, tile):
        return lambda zs, rows: ref.at[k, zs, tile, pl.ds(wide, rows), :]

    def relay_start(k):
        for tile in range(tiles):
            if k:
                arrive_filling(start, k, tile, recv_of["guess"] + k * tiles + tile)
            else:
                for turn in range(CORES):
                    arrive_filling(start, 0, tile, recv_of["initial"] + CORES * tile + turn, turn)
            at = k * tiles + tile
            share(tile_view(start, k, tile), STEPS, recv_of["high_start"] + at, recv_of["low_start"] + at)

    def start_ready(k):
        for tile in range(tiles):
            at = k * tiles + tile
            shared(tile_view(start, k, tile), STEPS, recv_of["high_start"] + at, recv_of["low_start"] + at)

    def relay_rate():
        for tile in range(tiles):
            for turn in range(CORES):
                arrive_filling(rate, 0, tile, recv_of["rate"] + CORES * tile + turn, turn)
            share(tile_view(rate, 0, tile), STEPS - 1, recv_of["high_rate"] + tile, recv_of["low_rate"] + tile)

    def rate_ready():
        for tile in range(tiles):
            shared(tile_view(rate, 0, tile), STEPS - 1, recv_of["high_rate"] + tile, recv_of["low_rate"] + tile)

    def body_view(ref, k):
        return lambda zs, rows: ref.at[k, zs, :, pl.ds(wide, rows), :]

    tall = next(number for number in (32, 16, 8) if most % number == 0)
    lane = lax.broadcasted_iota(jnp.int32, (tall, LANES), 1)

    def march(src, k, low, high, emit):
        def block(number, carry):
            at = pl.multiple_of(wide + number * tall, SUBLANES)
            here = pl.ds(at, tall)

            def load(z):
                return [src[k, z, tile, here, :] for tile in range(tiles)]

            under, middle = load(low - 1), load(low)
            for z in range(low, high):
                over = load(z + 1)
                zone = 0 if z < low_own else 1 if z < high_own else 2
                after = [pltpu.roll(part_of, 1, 1) for part_of in middle]
                ahead = [pltpu.roll(part_of, LANES - 1, 1) for part_of in middle]
                for tile in range(tiles):
                    value = middle[tile]
                    left = after[tile - 1] if tile else 0.0
                    right = ahead[tile + 1] if tile + 1 < tiles else 0.0
                    beside = over[tile] + under[tile]
                    beside = beside + src[k, z, tile, pl.ds(at - 1, tall), :] + src[k, z, tile, pl.ds(at + 1, tall), :]
                    beside = beside + jnp.where(lane == 0, left, after[tile])
                    beside = beside + jnp.where(lane == LANES - 1, right, ahead[tile])
                    growth = rate[0, z, tile, here, :] * (fine_growth - fine_growth * (value * value))
                    stepped = reaches[zone] * beside + value * (growth + (1.0 - 6.0 * fine_diffuse))
                    emit((z, tile, here), value, stepped)
                under, middle = middle, over
            return carry

        lax.fori_loop(0, most // tall, block, 0)

    def rough_of(value, stepped):
        return value + coarse_ratio * (stepped - value)

    def put(ref, k, spot, value):
        z, tile, here = spot
        ref[k, z, tile, here, :] = value

    def get(ref, k, spot):
        z, tile, here = spot
        return ref[k, z, tile, here, :]

    def fine(src, source_k, dst, halo, rough=False):
        def emit(spot, value, stepped):
            put(dst, 0, spot, stepped)
            if rough and low_own <= spot[0] < high_own:
                put(coarse, 0, spot, rough_of(value, stepped))

        march(src, source_k, low_own - halo, high_own + halo, emit)

    def own_begin(number):
        return outer + inner * (number - 1) if number else 0

    def hand_in(ref, k, out, kind, j):
        begin = pl.multiple_of(my_begin + inset, SUBLANES)
        slot = recv_of[kind] + my_part

        def make(rows):
            size = outer if rows == most else inner
            src = ref.at[k, own, :, pl.ds(pl.multiple_of(wide + inset, SUBLANES), size), :]
            return src, out.at[:, :, pl.ds(begin, size), :]

        stays = jnp.logical_and(tm == j, home)
        launch(make, slot, {"tm": j, "space": 2 * pair + core}, jnp.logical_not(stays), edge)
        local(make, slot, stays)

    def relax(k):
        fine(start, k, first, STEPS - 1, rough=k == 0)
        fine(first, 0, second, STEPS - 2)

        def emit(spot, value, stepped):
            if k == nt - 1:
                put(defect, k, spot, get(end, 0, spot) - stepped)
                return
            put(again, k, spot, stepped)
            if k == 0:
                put(defect, 0, spot, stepped - stepped)
                base = get(coarse, 0, spot)
                put(chain, 0, spot, base + (stepped - base))

        march(second, 0, low_own, high_own, emit)

    def send_again(k):
        share(body_view(again, k), STEPS, recv_of["high_again"] + k, recv_of["low_again"] + k)

    def finish(k):
        shared(body_view(again, k), STEPS, recv_of["high_again"] + k, recv_of["low_again"] + k)
        fine(again, k, first, STEPS - 1, rough=True)
        fine(first, 0, second, STEPS - 2)

        def emit(spot, value, stepped):
            if k + 1 < nt - 1:
                put(defect, k + 1, spot, stepped - get(again, k + 1, spot))
            else:
                put(end, 0, spot, stepped)
            base = get(coarse, 0, spot)
            if k:
                put(offset, k + 1, spot, stepped - base)
            else:
                put(chain, 1, spot, base + (stepped - base))

        march(second, 0, low_own, high_own, emit)

    def lift_between(j, low, high):
        def emit(spot, value, stepped):
            put(chain, j, spot, rough_of(value, stepped) + get(offset, j, spot))

        march(chain, j - 1, low, high, emit)

    def edges_of(j):
        slots = recv_of["high_offset"] + j, recv_of["low_offset"] + j
        return body_view(offset, j), nt - 1 - j, *slots

    def lift_around(j):
        halo = nt - 1 - j
        if halo:
            shared(*edges_of(j))
            lift_between(j, low_own - halo, low_own)
            lift_between(j, high_own, high_own + halo)

    relay_start(0)
    relay_rate()
    give_guess(1)
    relay_start(1)
    start_ready(0)
    rate_ready()
    relax(0)
    send_again(0)
    hand_in(chain, 0, corrected_out, "corrected", 0)
    hand_in(defect, 0, defect_out, "defect", 0)
    relay_start(2)
    start_ready(1)
    relax(1)
    send_again(1)
    finish(0)
    first_edges = body_view(chain, 1), nt - 2, recv_of["high_first"], recv_of["low_first"]
    share(*first_edges)
    hand_in(chain, 1, corrected_out, "corrected", 1)
    hand_in(defect, 1, defect_out, "defect", 1)
    for j in range(2, nt):
        if j < nt - 1:
            start_ready(j)
            relax(j)
            send_again(j)
        finish(j - 1)
        if j < nt - 1:
            share(*edges_of(j))
            relay_start(j + 1)
            hand_in(defect, j, defect_out, "defect", j)
        if j == 2:
            shared(*first_edges)
        else:
            lift_around(j - 1)
        lift_between(j, low_own, high_own)
        hand_in(chain, j, corrected_out, "corrected", j)
    start_ready(nt - 1)
    relax(nt - 1)
    hand_in(defect, nt - 1, defect_out, "defect", nt - 1)

    for copy, condition in sends:
        pl.when(condition)(copy.wait_send)
    for out, kind in ((corrected_out, "corrected"), (defect_out, "defect")):
        for number in range(nt):
            size = inner if 0 < number < nt - 1 else outer
            dst = out.at[:, :, pl.ds(own_begin(number), size), :]
            pltpu.make_async_copy(dst, dst, recv.at[recv_of[kind] + number]).wait()


def settle_kernel(corrected, defect, corrected_out, defect_out, local):
    copies = []
    for src, dst in ((corrected, corrected_out), (defect, defect_out)):
        for tile in range(src.shape[1]):
            to = dst.at[0, :, :, pl.ds(tile * LANES, LANES)]
            copies.append(pltpu.make_async_copy(src.at[:, tile], to, local.at[len(copies)]))
    for copy in copies:
        copy.start()
    for copy in copies:
        copy.wait()


def settle(corrected, defect):
    planes, tiles, across, lanes = corrected.shape
    shape = jax.ShapeDtypeStruct((1, planes, across, tiles * lanes), jnp.float32)
    return pl.pallas_call(
        settle_kernel,
        out_shape=(shape, shape),
        in_specs=[pl.BlockSpec(memory_space=pl.ANY)] * 2,
        out_specs=[pl.BlockSpec(memory_space=pl.ANY)] * 2,
        scratch_shapes=[pltpu.SemaphoreType.DMA((2 * tiles,))],
        compiler_params=pltpu.CompilerParams(vmem_limit_bytes=1 << 20),
    )(corrected, defect)


def quarter_device(nt, ns, initial, coarse_guess, react_rate):
    planes, across, width = initial.shape
    wide, inner = quarter_rows(nt, across)
    length = planes + 2 * STEPS
    tall = inner + 5 * wide
    tiles = width // LANES
    recv_of, recv_total = quarter_slots(nt, tiles)

    def field(number):
        return pltpu.VMEM((number, length, tiles, tall, LANES), jnp.float32)

    shape = jax.ShapeDtypeStruct((planes, tiles, across, LANES), jnp.float32)
    corrected, defect = pl.pallas_call(
        functools.partial(quarter_kernel, nt, ns, planes, inner, wide, recv_of),
        out_shape=(shape, shape),
        in_specs=[pl.BlockSpec(memory_space=pltpu.HBM)] * 3,
        out_specs=[pl.BlockSpec(memory_space=pl.ANY)] * 2,
        scratch_shapes=[
            field(nt), field(nt), field(1), field(1), field(1), field(1), field(nt), field(nt), field(nt), field(1),
            pltpu.SemaphoreType.DMA((tiles * (CORES * (1 + nt // 2) + 4 * nt + 2) + 6 * nt - 6,)),
            pltpu.SemaphoreType.DMA((recv_total,)),
        ],
        compiler_params=pltpu.CompilerParams(collective_id=0, has_side_effects=True, vmem_limit_bytes=VMEM_BYTES),
    )(*(pltpu.with_memory_space_constraint(ref, pltpu.HBM) for ref in (initial, coarse_guess[0], react_rate)))
    return settle(corrected, defect)


def quarter_rows(nt, across):
    wide = -(-(2 * STEPS + max(nt - 2, 0)) // SUBLANES) * SUBLANES
    return wide, (across - 4 * wide) // nt


def takes_quarters(nt, planes, across, width):
    wide, inner = quarter_rows(nt, across)
    fits = inner > 0 and (across - 4 * wide) % (nt * SUBLANES) == 0 and nt - 2 <= planes
    return nt % 2 == 0 and nt > 2 and planes >= STEPS and width % LANES == 0 and fits


def on_device(nt, ns, initial, coarse_guess, react_rate):
    planes, across, width = initial.shape
    if takes_quarters(nt, planes, across, width):
        return quarter_device(nt, ns, initial, coarse_guess, react_rate)
    half = across // 2
    wide = -(-(2 * STEPS + max(nt - 2, 0)) // SUBLANES) * SUBLANES
    length = 2 * planes + 2 * STEPS
    field = pltpu.VMEM((length, half + 2 * wide, width), jnp.float32)
    slot_of, total = slots(planes)
    shape = jax.ShapeDtypeStruct(initial.shape, jnp.float32)
    corrected, defect = pl.pallas_call(
        functools.partial(kernel, nt, ns, planes, half, wide, slot_of),
        out_shape=(shape, shape),
        in_specs=[pl.BlockSpec(memory_space=pl.ANY)] * 3,
        out_specs=[pl.BlockSpec(memory_space=pl.ANY)] * 2,
        scratch_shapes=[field] * 11
        + [
            pltpu.VMEM((half + 2 * wide, width), jnp.float32),
            pltpu.SemaphoreType.DMA((total,)),
            pltpu.SemaphoreType.DMA((total,)),
            pltpu.SemaphoreType.DMA((3 + planes,)),
        ],
        compiler_params=pltpu.CompilerParams(collective_id=0, has_side_effects=True),
    )(initial, coarse_guess[0], react_rate)
    return corrected[None], defect[None]


def solution(mesh):
    in_specs = (P("space", None, None), P("tm", "space", None, None), P("space", None, None))
    out_specs = (P("tm", "space", None, None), P("tm", "space", None, None))
    return jax.shard_map(
        functools.partial(on_device, mesh.shape["tm"], mesh.shape["space"]),
        mesh=mesh, in_specs=in_specs, out_specs=out_specs, check_vma=False,
    )
```

```python
import functools

import jax
import jax.numpy as jnp
from jax import lax
from jax.experimental import pallas as pl
from jax.experimental.pallas import tpu as pltpu
from jax.sharding import PartitionSpec as P

STEPS = 3
SUBLANES = 8

fine_diffuse = 0.04
fine_growth = 0.05
coarse_ratio = 4.0

MESH = pl.DeviceIdType.MESH

PIECES = 4
LANES = 128
CORES = 2
VMEM_BYTES = 40 << 20


def slots(planes):
    kinds = dict(
        start=2 + PIECES, start_edge=1 + PIECES, rate=1, rate_edge=2, rate_core=3, again=PIECES, again_edge=2 * PIECES,
        chain=2 * planes, chain_edge=2, defect=1, corrected=planes,
    )
    first, total = {}, 0
    for kind, number in kinds.items():
        first[kind] = total
        total += number
    return first, total


def kernel(
    nt, ns, planes, half, wide, slot_of,
    initial, guess, rate_in, corrected_out, defect_out,
    start, rate, again, before, first, second, relaxed, coarse, offset, defect, after, reach,
    send, recv, local,
):
    tm, space = lax.axis_index("tm"), lax.axis_index("space")
    pair, side = lax.div(space, 2), lax.rem(space, 2)
    pairs = ns // 2
    mate = space + 1 - 2 * side
    block = 2 * planes
    length = block + 2 * STEPS
    rows = half + 2 * wide
    has_low, has_high = pair > 0, pair < pairs - 1
    has_next, has_previous = tm < nt - 1, tm > 0
    own = pl.ds(STEPS, block)

    for ref in (start, rate, again, before):
        zero_plane = jnp.zeros((STEPS,) + ref.shape[1:], jnp.float32)
        zero_rows = jnp.zeros((block, wide, ref.shape[2]), jnp.float32)
        ref[0:STEPS] = zero_plane
        ref[STEPS + block : length] = zero_plane
        ref[STEPS : STEPS + block, 0:wide] = zero_rows
        ref[STEPS : STEPS + block, wide + half : rows] = zero_rows

    barrier = pltpu.get_barrier_semaphore()
    count = jnp.int32(0)
    for step in (-1, 0, 1):
        for place in ("own", "mate", "low", "high"):
            if step == 0 and place == "own":
                continue
            there = {"own": space, "mate": mate, "low": space - 2, "high": space + 2}[place]
            tests = []
            if step:
                tests.append(has_next if step > 0 else has_previous)
            if place in ("low", "high"):
                tests.append(has_low if place == "low" else has_high)
            target = {"tm": tm + step, "space": there}
            if tests:
                valid = functools.reduce(jnp.logical_and, tests)

                @pl.when(valid)
                def _(target=target):
                    pl.semaphore_signal(barrier, inc=1, device_id=target, device_id_type=MESH)

                count = count + valid.astype(jnp.int32)
            else:
                pl.semaphore_signal(barrier, inc=1, device_id=target, device_id_type=MESH)
                count = count + 1
    for here, there in ((tm == 0, nt - 1), (tm == nt - 1, 0)):

        @pl.when(here)
        def _(there=there):
            pl.semaphore_signal(
                barrier, inc=1, device_id={"tm": there, "space": mate}, device_id_type=MESH
            )

        count = count + here.astype(jnp.int32)
    pl.semaphore_wait(barrier, count)

    def remote(src, dst, slot, to_tm, to_space):
        return pltpu.make_async_remote_copy(
            src_ref=src,
            dst_ref=dst,
            send_sem=send.at[slot],
            recv_sem=recv.at[slot],
            device_id={"tm": to_tm, "space": to_space},
            device_id_type=MESH,
        )

    def cut(ref, target):
        return ref.at[:, pl.ds(pl.multiple_of(target * (half - wide), SUBLANES), half + wide), :]

    def spot(ref, target, begin, size):
        at = pl.multiple_of(wide * (1 - target), SUBLANES)
        return ref.at[pl.ds(begin, size), pl.ds(at, half + wide), :]

    slab = STEPS + planes * side
    other = STEPS + planes * (1 - side)

    core = lax.rem(tm, 2)
    twin = tm + 1 - 2 * core
    lanes = start.shape[2] // 2

    def lane_half(ref, which):
        return ref.at[:, :, pl.ds(pl.multiple_of(which * lanes, lanes), lanes)]

    groups = (half + wide) // SUBLANES
    bounds = [groups * piece // PIECES * SUBLANES for piece in range(PIECES + 1)]

    def piece_of(ref, begin, size, piece, target=side):
        at = pl.multiple_of(wide * (1 - target) + bounds[piece], SUBLANES)
        return ref.at[pl.ds(begin, size), pl.ds(at, bounds[piece + 1] - bounds[piece]), :]

    def cut_piece(ref, target, piece):
        at = pl.multiple_of(target * (half - wide) + bounds[piece], SUBLANES)
        return ref.at[:, pl.ds(at, bounds[piece + 1] - bounds[piece]), :]

    rate_own = pltpu.make_async_copy(cut(rate_in, side), spot(rate, side, slab, planes), local.at[0])
    rate_mate = remote(
        lane_half(cut(rate_in, 1 - side), core),
        lane_half(spot(rate, 1 - side, slab, planes), core),
        slot_of["rate"],
        tm,
        mate,
    )
    initial_own = pltpu.make_async_copy(cut(initial, side), spot(start, side, slab, planes), local.at[1])
    guess_own = remote(
        cut(guess, side), spot(start, side, slab, planes), slot_of["start"], tm + 1, space
    )

    def to_mate(ref, to_tm):
        return [
            remote(
                cut_piece(ref, 1 - side, piece),
                piece_of(start, slab, planes, piece, 1 - side),
                slot_of["start"] + 1 + piece,
                to_tm,
                mate,
            )
            for piece in range(PIECES)
        ]

    guess_mate = to_mate(guess, tm + 1)
    initial_mate = to_mate(initial, 0)
    is_last = tm == nt - 1

    rate_mate.start()
    rate_own.start()

    @pl.when(has_next)
    def _():
        guess_own.start()
        for copy in guess_mate:
            copy.start()

    @pl.when(is_last)
    def _():
        for copy in initial_mate:
            copy.start()

    @pl.when(tm == 0)
    def _():
        initial_own.start()

    for ref in (first, second):
        @pl.when(jnp.logical_not(has_low))
        def _(ref=ref):
            ref[0:STEPS] = jnp.zeros((STEPS,) + ref.shape[1:], jnp.float32)

        @pl.when(jnp.logical_not(has_high))
        def _(ref=ref):
            ref[STEPS + block : length] = jnp.zeros((STEPS,) + ref.shape[1:], jnp.float32)

    row = lax.broadcasted_iota(jnp.int32, reach.shape, 0)
    outside = jnp.logical_or(
        jnp.logical_and(side == 0, row < wide), jnp.logical_and(side == 1, row >= wide + half)
    )
    reach[...] = jnp.where(outside, 0.0, fine_diffuse)

    low_place, high_place = STEPS + block, 0

    def edge_pieces(piece):
        slot = slot_of["start_edge"] + 1 + piece
        low = remote(
            piece_of(start, STEPS, STEPS, piece), piece_of(start, low_place, STEPS, piece),
            slot, tm, space - 2,
        )
        high = remote(
            piece_of(start, block, STEPS, piece), piece_of(start, high_place, STEPS, piece),
            slot, tm, space + 2,
        )
        return low, high

    start_edges = [edge_pieces(piece) for piece in range(PIECES)]
    start_low = remote(
        spot(start, side, STEPS, STEPS), spot(start, side, low_place, STEPS),
        slot_of["start_edge"], tm, space - 2,
    )
    start_high = remote(
        spot(start, side, block, STEPS), spot(start, side, high_place, STEPS),
        slot_of["start_edge"], tm, space + 2,
    )
    reach_rate = STEPS - 1
    rate_low_spot = lane_half(spot(rate, side, low_place, reach_rate), core)
    rate_high_spot = lane_half(spot(rate, side, high_place + 1, reach_rate), core)
    rate_low = remote(
        lane_half(spot(rate, side, STEPS, reach_rate), core), rate_low_spot,
        slot_of["rate_edge"], tm, space - 2,
    )
    rate_high = remote(
        lane_half(spot(rate, side, STEPS + block - reach_rate, reach_rate), core), rate_high_spot,
        slot_of["rate_edge"] + 1, tm, space + 2,
    )
    rate_other_spot = lane_half(spot(rate, side, other, planes), core)
    twin_mate = remote(rate_other_spot, rate_other_spot, slot_of["rate_core"], twin, space)
    twin_low = remote(rate_low_spot, rate_low_spot, slot_of["rate_core"] + 1, twin, space)
    twin_high = remote(rate_high_spot, rate_high_spot, slot_of["rate_core"] + 2, twin, space)

    own_low = jnp.logical_and(side == 0, has_low)
    own_high = jnp.logical_and(side == 1, has_high)
    other_low = jnp.logical_and(side == 1, has_low)
    other_high = jnp.logical_and(side == 0, has_high)

    rate_own.wait()
    pl.when(own_low)(rate_low.start)
    pl.when(own_high)(rate_high.start)

    @pl.when(tm == 0)
    def _():
        initial_own.wait()

    @pl.when(has_previous)
    def _():
        guess_own.wait_recv()

    pl.when(own_low)(start_low.start)
    pl.when(own_high)(start_high.start)

    rate_mate.wait_recv()
    pl.when(other_low)(rate_low.start)
    pl.when(other_high)(rate_high.start)
    twin_mate.start()

    for piece in range(PIECES):
        guess_mate[piece].wait_recv()
        pl.when(other_low)(start_edges[piece][0].start)
        pl.when(other_high)(start_edges[piece][1].start)

    @pl.when(has_high)
    def _():
        rate_low.wait_recv()
        twin_low.start()

    @pl.when(has_low)
    def _():
        rate_high.wait_recv()
        twin_high.start()

    twin_mate.wait_recv()
    pl.when(has_high)(twin_low.wait_recv)
    pl.when(has_low)(twin_high.wait_recv)

    @pl.when(jnp.logical_and(side == 0, has_high))
    def _():
        start_low.wait_recv()

    @pl.when(jnp.logical_and(side == 1, has_low))
    def _():
        start_high.wait_recv()

    @pl.when(jnp.logical_and(side == 1, has_high))
    def _():
        for low, high in start_edges:
            low.wait_recv()

    @pl.when(jnp.logical_and(side == 0, has_low))
    def _():
        for low, high in start_edges:
            high.wait_recv()

    keep = pltpu.make_async_copy(start, again, local.at[1])

    @pl.when(tm == 0)
    def _():
        keep.start()

    width = start.shape[2]
    lane = lax.broadcasted_iota(jnp.int32, reach.shape, 1)

    def change(ref, z):
        middle = ref[z]
        beside = ref[z + 1] + ref[z - 1]
        beside = beside + pltpu.roll(middle, 1, 0) + pltpu.roll(middle, rows - 1, 0)
        beside = beside + jnp.where(lane == 0, 0.0, pltpu.roll(middle, 1, 1))
        beside = beside + jnp.where(lane == width - 1, 0.0, pltpu.roll(middle, width - 1, 1))
        growth = rate[z] * (fine_growth - fine_growth * (middle * middle))
        return middle, reach[...] * beside + middle * (growth - 6.0 * fine_diffuse)

    def span(step):
        low = jnp.where(has_low, step, max(step, STEPS))
        high = jnp.where(has_high, length - step, min(length - step, STEPS + block))
        return low, high

    def fine(src, dst, step):
        def plane(z, carry):
            middle, delta = change(src, z)
            dst[z] = middle + delta
            return carry

        lax.fori_loop(*span(step), plane, 0)

    fine(start, first, 1)
    fine(first, second, 2)
    fine(second, relaxed, 3)

    given, given_low, given_high = [], [], []
    for piece in range(PIECES):
        slot = slot_of["again_edge"] + 2 * piece
        given.append(
            remote(
                piece_of(relaxed, STEPS, block, piece),
                piece_of(again, STEPS, block, piece),
                slot_of["again"] + piece,
                tm + 1,
                space,
            )
        )
        given_low.append(
            remote(
                piece_of(again, STEPS, STEPS, piece),
                piece_of(again, STEPS + block, STEPS, piece),
                slot,
                tm,
                space - 2,
            )
        )
        given_high.append(
            remote(
                piece_of(again, block, STEPS, piece),
                piece_of(again, 0, STEPS, piece),
                slot + 1,
                tm,
                space + 2,
            )
        )

    @pl.when(has_next)
    def _():
        for piece in range(PIECES):
            given[piece].start()

    @pl.when(tm == 0)
    def _():
        keep.wait()

    @pl.when(has_previous)
    def _():
        for piece in range(PIECES):
            given[piece].wait_recv()
            pl.when(has_low)(given_low[piece].start)
            pl.when(has_high)(given_high[piece].start)
        for piece in range(PIECES):
            pl.when(has_high)(given_low[piece].wait_recv)
            pl.when(has_low)(given_high[piece].wait_recv)

    def first_plane(z, carry):
        middle, delta = change(again, z)
        first[z] = middle + delta
        coarse[z] = middle + coarse_ratio * delta
        return carry

    lax.fori_loop(*span(1), first_plane, 0)
    fine(first, second, 2)

    order = []
    for depth in range(planes):
        order += [STEPS + depth, STEPS + block - 1 - depth]

    def row_span(z):
        at = pl.multiple_of(wide * (1 - side), SUBLANES)
        return (pl.ds(z, 1), pl.ds(at, half + wide), slice(None))

    passed = {
        z: remote(
            after.at[row_span(z)], before.at[row_span(z)], slot_of["chain"] + z - STEPS, tm + 1, space
        )
        for z in order
    }
    low_edge, high_edge = STEPS, STEPS + block - 1
    passed_low = remote(
        before.at[row_span(low_edge)], before.at[row_span(high_edge + 1)],
        slot_of["chain_edge"], tm, space - 2,
    )
    passed_high = remote(
        before.at[row_span(high_edge)], before.at[row_span(low_edge - 1)],
        slot_of["chain_edge"] + 1, tm, space + 2,
    )

    mine = pl.ds(pl.multiple_of(side * half, SUBLANES), half)
    middle_rows = pl.ds(wide, half)
    defect_stay = pltpu.make_async_copy(
        defect.at[pl.ds(slab, planes), middle_rows, :], defect_out.at[:, mine, :], local.at[2]
    )
    defect_go = remote(
        defect.at[pl.ds(other, planes), middle_rows, :], defect_out.at[:, mine, :],
        slot_of["defect"], tm, mate,
    )
    stay, go = {}, {}
    for z in order:
        place = (z - STEPS) % planes
        src = after.at[pl.ds(z, 1), middle_rows, :]
        dst = corrected_out.at[pl.ds(place, 1), mine, :]
        stay[z] = pltpu.make_async_copy(src, dst, local.at[3 + place])
        go[z] = remote(src, dst, slot_of["corrected"] + place, tm, mate)

    def at_home(z):
        return side == (z - STEPS) // planes

    def hand_in(z):
        pl.when(at_home(z))(stay[z].start)
        pl.when(jnp.logical_not(at_home(z)))(go[z].start)

    def last_plane(z):
        middle, delta = change(second, z)
        end = middle + delta
        defect[z] = end - relaxed[z]
        shift = end - coarse[z]
        offset[z] = shift
        after[z] = coarse[z] + shift

    def take_edges():
        passed[low_edge].wait_recv()
        pl.when(has_low)(passed_low.start)
        passed[high_edge].wait_recv()
        pl.when(has_high)(passed_high.start)

    pl.when(tm == 2)(take_edges)
    opens = jnp.logical_and(tm == 1, has_next)
    for index, z in enumerate(order):
        last_plane(z)
        if index:
            pl.when(opens)(passed[order[index - 1]].start)
    pl.when(opens)(passed[order[-1]].start)
    defect_go.start()
    defect_stay.start()

    later = tm > 1

    @pl.when(jnp.logical_not(later))
    def _():
        for z in order:
            hand_in(z)

    @pl.when(later)
    def _():
        pl.when(tm > 2)(take_edges)
        queue = order[2:]
        waiting = set(queue)

        def leave(z):
            pl.when(has_next)(passed[z].start)
            hand_in(z)

        for index, z in enumerate(order):
            while waiting & {z - 1, z, z + 1}:
                come = queue.pop(0)
                waiting.remove(come)
                passed[come].wait_recv()
            if z == low_edge:
                pl.when(has_low)(passed_high.wait_recv)
            if z == high_edge:
                pl.when(has_high)(passed_low.wait_recv)
            middle, delta = change(before, z)
            after[z] = middle + coarse_ratio * delta + offset[z]
            if index:
                leave(order[index - 1])
        leave(order[-1])
        pl.when(has_low)(passed_low.wait_send)
        pl.when(has_high)(passed_high.wait_send)

    onward = jnp.logical_and(tm > 0, has_next)

    @pl.when(is_last)
    def _():
        for copy in initial_mate:
            copy.wait_send()

    @pl.when(has_next)
    def _():
        guess_own.wait_send()
        for copy in guess_mate:
            copy.wait_send()

    rate_mate.wait_send()
    twin_mate.wait_send()
    pl.when(has_high)(twin_low.wait_send)
    pl.when(has_low)(twin_high.wait_send)
    pl.when(has_low)(rate_low.wait_send)
    pl.when(has_high)(rate_high.wait_send)
    pl.when(own_low)(start_low.wait_send)
    pl.when(own_high)(start_high.wait_send)

    @pl.when(other_low)
    def _():
        for low, high in start_edges:
            low.wait_send()

    @pl.when(other_high)
    def _():
        for low, high in start_edges:
            high.wait_send()

    @pl.when(has_next)
    def _():
        for piece in range(PIECES):
            given[piece].wait_send()

    @pl.when(has_previous)
    def _():
        for piece in range(PIECES):
            pl.when(has_low)(given_low[piece].wait_send)
            pl.when(has_high)(given_high[piece].wait_send)

    @pl.when(onward)
    def _():
        for z in order:
            passed[z].wait_send()

    defect_stay.wait()
    defect_go.wait()
    for z in order:
        pl.when(at_home(z))(stay[z].wait)
        pl.when(at_home(z))(go[z].wait_recv)
        pl.when(jnp.logical_not(at_home(z)))(go[z].wait_send)


def quarter_slots(nt, tiles):
    kinds = dict(
        initial=CORES * tiles, rate=CORES * tiles, guess=nt * tiles, low_start=nt * tiles, high_start=nt * tiles,
        low_rate=tiles, high_rate=tiles, low_again=nt, high_again=nt, low_first=1, high_first=1,
        low_offset=nt, high_offset=nt, corrected=nt, defect=nt,
    )
    first, total = {}, 0
    for kind, number in kinds.items():
        first[kind] = total
        total += number
    return first, total


def quarter_kernel(
    nt, ns, planes, inner, wide, recv_of,
    initial, guess, rate_in, corrected_out, defect_out,
    start, again, rate, first, second, coarse, chain, offset, defect, end,
    send, recv,
):
    tm, space = lax.axis_index("tm"), lax.axis_index("space")
    y, core = lax.div(tm, 2), lax.rem(tm, 2)
    pair, x = lax.div(space, 2), lax.rem(space, 2)
    levels, pairs = nt // 2, ns // 2
    length = planes + 2 * STEPS
    outer, most = inner + 2 * wide, inner + 3 * wide
    less = most - wide
    across = initial.shape[1]
    tiles = start.shape[2]
    low_own, high_own = STEPS, STEPS + planes
    slab = 2 * pair + core
    has_low, has_high = slab > 0, slab < ns - 1
    edge = y == levels - 1
    inside = jnp.logical_not(edge)
    first_row, last_row = jnp.logical_and(edge, x == 0), jnp.logical_and(edge, x == 1)
    low_to = {"tm": tm + 1 - 2 * core, "space": space - 2 * (1 - core)}
    high_to = {"tm": tm + 1 - 2 * core, "space": space + 2 * core}

    def begin_of(to_y, to_x):
        own_begin = outer + inner * (2 * to_y + to_x)
        begin = jnp.where(to_y == levels - 1, to_x * (across - most), own_begin - wide)
        return pl.multiple_of(begin, SUBLANES)

    my_begin = begin_of(y, x)
    my_part = jnp.where(edge, x * (nt - 1), 1 + 2 * y + x)
    inset = pl.multiple_of(jnp.where(first_row, 0, wide), SUBLANES)
    body = pl.ds(wide, most)

    edge_zero = jnp.zeros((length, tiles, wide, LANES), jnp.float32)
    plane_zero = jnp.zeros((STEPS,) + start.shape[2:], jnp.float32)

    def clear_rows(ref, k):
        @pl.when(first_row)
        def _():
            ref[k, :, :, 0:wide] = edge_zero

        @pl.when(last_row)
        def _():
            ref[k, :, :, wide + most : 2 * wide + most] = edge_zero

    def clear_planes(ref, k):
        @pl.when(jnp.logical_not(has_low))
        def _():
            ref[k, 0:low_own] = plane_zero

        @pl.when(jnp.logical_not(has_high))
        def _():
            ref[k, high_own:length] = plane_zero

    barrier = pltpu.get_barrier_semaphore()
    for dy in range(levels):
        for dx in range(2):
            for dc in range(2):
                if dy or dx or dc:
                    there = {
                        "tm": 2 * lax.rem(y + dy, levels) + lax.rem(core + dc, 2),
                        "space": 2 * pair + lax.rem(x + dx, 2),
                    }
                    pl.semaphore_signal(barrier, inc=1, device_id=there, device_id_type=MESH)
    count = jnp.int32(2 * nt - 1)
    for far, there in (
        (jnp.logical_and(core == 0, has_low), low_to),
        (jnp.logical_and(core == 1, has_high), high_to),
    ):

        @pl.when(far)
        def _(there=there):
            pl.semaphore_signal(barrier, inc=1, device_id=there, device_id_type=MESH)

        count = count + far.astype(jnp.int32)

    for k in range(nt):
        clear_rows(start, k)
        clear_planes(start, k)
    for k in range(nt - 1):
        clear_rows(again, k)
        clear_planes(again, k)
        clear_rows(chain, k)
    clear_rows(first, 0)
    clear_rows(second, 0)
    clear_planes(rate, 0)
    clear_planes(chain, 1)
    for j in range(2, nt - 1):
        clear_planes(offset, j)

    pl.semaphore_wait(barrier, count)

    sends = []
    send_count = [0]

    def launch(make, slot, there, condition, wider):
        number = send_count[0]
        send_count[0] += 1
        for rows, fits in ((most, wider), (less, jnp.logical_not(wider))):
            src, dst = make(rows)
            copy = pltpu.make_async_remote_copy(
                src_ref=src, dst_ref=dst, send_sem=send.at[number], recv_sem=recv.at[slot],
                device_id=there, device_id_type=MESH,
            )
            sends.append((copy, jnp.logical_and(condition, fits)))
            pl.when(jnp.logical_and(condition, fits))(copy.start)

    def local(make, slot, condition):
        for rows, fits in ((most, edge), (less, inside)):
            src, dst = make(rows)
            pl.when(jnp.logical_and(condition, fits))(pltpu.make_async_copy(src, dst, recv.at[slot]).start)

    def arrive(dst_of, slot, condition=True):
        for rows, fits in ((most, edge), (less, inside)):
            dst = dst_of(rows)
            pl.when(jnp.logical_and(condition, fits))(pltpu.make_async_copy(dst, dst, recv.at[slot]).wait)

    own = pl.ds(low_own, planes)
    home = core == x
    away = jnp.logical_not(home)

    cut = -(-most // (CORES * SUBLANES)) * SUBLANES

    def filling(src, begin, ref, k, tile, turn=None):
        def make(rows):
            at, size = (0, rows) if turn is None else (cut * turn, min(cut * (turn + 1), rows) - cut * turn)
            from_rows = pl.ds(pl.multiple_of(begin + at, SUBLANES), size)
            return src.at[:, from_rows, pl.ds(tile * LANES, LANES)], ref.at[k, own, tile, pl.ds(wide + at, size), :]

        return make

    def arrive_filling(ref, k, tile, slot, turn=None):
        arrive(lambda rows: filling(initial, 0, ref, k, tile, turn)(rows)[1], slot)

    for ref, src, kind in ((start, initial, "initial"), (rate, rate_in, "rate")):
        for tile in range(tiles):
            for turn in range(CORES):
                local(filling(src, my_begin, ref, 0, tile, turn), recv_of[kind] + CORES * tile + turn, home)

    def give_split(src, ref, kind, to_y, condition, wider):
        begin = begin_of(to_y, 1 - x)
        for tile in range(tiles):
            for turn in range(CORES):
                launch(
                    filling(src, begin, ref, 0, tile, turn), recv_of[kind] + CORES * tile + turn,
                    {"tm": 2 * to_y + x, "space": space + 1 - 2 * x}, jnp.logical_and(condition, core == turn), wider,
                )

    give_split(initial, start, "initial", y, jnp.bool_(True), edge)
    for to_y in range(levels):
        give_split(rate_in, rate, "rate", to_y, edge, jnp.bool_(to_y == levels - 1))

    def give_guess(turn):
        gives = jnp.logical_and(tm < nt - 1, core == turn)
        for tile in range(tiles):
            slot = recv_of["guess"] + (tm + 1) * tiles + tile
            for dy in range(levels):
                for dx in (1, 0):
                    to_y, to_x = lax.rem(y + dy, levels), lax.rem(x + dx, 2)
                    make = filling(guess, begin_of(to_y, to_x), start, tm + 1, tile)
                    there = {"tm": 2 * to_y + x, "space": 2 * pair + to_x}
                    if dy or dx:
                        launch(make, slot, there, gives, to_y == levels - 1)
                    else:
                        launch(make, slot, there, jnp.logical_and(gives, away), edge)
                        local(make, slot, jnp.logical_and(gives, home))

    give_guess(0)

    reaches = [jnp.where(inside_of, fine_diffuse, 0.0) for inside_of in (has_low, True, has_high)]
    reaches[1] = fine_diffuse

    def share(view, depth, high_slot, low_slot):
        def low(rows):
            return view(pl.ds(low_own, depth), rows), view(pl.ds(high_own, depth), rows)

        def high(rows):
            return view(pl.ds(high_own - depth, depth), rows), view(pl.ds(low_own - depth, depth), rows)

        launch(low, high_slot, low_to, has_low, edge)
        launch(high, low_slot, high_to, has_high, edge)

    def shared(view, depth, high_slot, low_slot):
        arrive(lambda rows: view(pl.ds(high_own, depth), rows), high_slot, has_high)
        arrive(lambda rows: view(pl.ds(low_own - depth, depth), rows), low_slot, has_low)

    def tile_view(ref, k, tile):
        return lambda zs, rows: ref.at[k, zs, tile, pl.ds(wide, rows), :]

    def relay_start(k):
        for tile in range(tiles):
            if k:
                arrive_filling(start, k, tile, recv_of["guess"] + k * tiles + tile)
            else:
                for turn in range(CORES):
                    arrive_filling(start, 0, tile, recv_of["initial"] + CORES * tile + turn, turn)
            at = k * tiles + tile
            share(tile_view(start, k, tile), STEPS, recv_of["high_start"] + at, recv_of["low_start"] + at)

    def start_ready(k):
        for tile in range(tiles):
            at = k * tiles + tile
            shared(tile_view(start, k, tile), STEPS, recv_of["high_start"] + at, recv_of["low_start"] + at)

    def relay_rate():
        for tile in range(tiles):
            for turn in range(CORES):
                arrive_filling(rate, 0, tile, recv_of["rate"] + CORES * tile + turn, turn)
            share(tile_view(rate, 0, tile), STEPS - 1, recv_of["high_rate"] + tile, recv_of["low_rate"] + tile)

    def rate_ready():
        for tile in range(tiles):
            shared(tile_view(rate, 0, tile), STEPS - 1, recv_of["high_rate"] + tile, recv_of["low_rate"] + tile)

    def body_view(ref, k):
        return lambda zs, rows: ref.at[k, zs, :, pl.ds(wide, rows), :]

    tall = next(number for number in (64, 32, 16, 8) if most % number == 0)
    lane = lax.broadcasted_iota(jnp.int32, (tall, LANES), 1)

    def march(src, k, low, high, emit):
        def block(number, carry):
            at = pl.multiple_of(wide + number * tall, SUBLANES)
            here = pl.ds(at, tall)

            def load(z):
                return [src[k, z, tile, here, :] for tile in range(tiles)]

            under, middle = load(low - 1), load(low)
            for z in range(low, high):
                over = load(z + 1)
                zone = 0 if z < low_own else 1 if z < high_own else 2
                after = [pltpu.roll(part_of, 1, 1) for part_of in middle]
                ahead = [pltpu.roll(part_of, LANES - 1, 1) for part_of in middle]
                for tile in range(tiles):
                    value = middle[tile]
                    left = after[tile - 1] if tile else 0.0
                    right = ahead[tile + 1] if tile + 1 < tiles else 0.0
                    beside = over[tile] + under[tile]
                    beside = beside + src[k, z, tile, pl.ds(at - 1, tall), :] + src[k, z, tile, pl.ds(at + 1, tall), :]
                    beside = beside + jnp.where(lane == 0, left, after[tile])
                    beside = beside + jnp.where(lane == LANES - 1, right, ahead[tile])
                    growth = rate[0, z, tile, here, :] * (fine_growth - fine_growth * (value * value))
                    stepped = reaches[zone] * beside + value * (growth + (1.0 - 6.0 * fine_diffuse))
                    emit((z, tile, here), value, stepped)
                under, middle = middle, over
            return carry

        lax.fori_loop(0, most // tall, block, 0)

    def rough_of(value, stepped):
        return value + coarse_ratio * (stepped - value)

    def put(ref, k, spot, value):
        z, tile, here = spot
        ref[k, z, tile, here, :] = value

    def get(ref, k, spot):
        z, tile, here = spot
        return ref[k, z, tile, here, :]

    def fine(src, source_k, dst, halo, rough=False):
        def emit(spot, value, stepped):
            put(dst, 0, spot, stepped)
            if rough and low_own <= spot[0] < high_own:
                put(coarse, 0, spot, rough_of(value, stepped))

        march(src, source_k, low_own - halo, high_own + halo, emit)

    def own_begin(number):
        return outer + inner * (number - 1) if number else 0

    def hand_in(ref, k, out, kind, j):
        begin = pl.multiple_of(my_begin + inset, SUBLANES)
        slot = recv_of[kind] + my_part

        def make(rows):
            size = outer if rows == most else inner
            src = ref.at[k, own, :, pl.ds(pl.multiple_of(wide + inset, SUBLANES), size), :]
            return src, out.at[:, :, pl.ds(begin, size), :]

        stays = jnp.logical_and(tm == j, home)
        launch(make, slot, {"tm": j, "space": 2 * pair + core}, jnp.logical_not(stays), edge)
        local(make, slot, stays)

    def relax(k):
        fine(start, k, first, STEPS - 1, rough=k == 0)
        fine(first, 0, second, STEPS - 2)

        def emit(spot, value, stepped):
            if k == nt - 1:
                put(defect, k, spot, get(end, 0, spot) - stepped)
                return
            put(again, k, spot, stepped)
            if k == 0:
                put(defect, 0, spot, stepped - stepped)
                base = get(coarse, 0, spot)
                put(chain, 0, spot, base + (stepped - base))

        march(second, 0, low_own, high_own, emit)

    def send_again(k):
        share(body_view(again, k), STEPS, recv_of["high_again"] + k, recv_of["low_again"] + k)

    def finish(k):
        shared(body_view(again, k), STEPS, recv_of["high_again"] + k, recv_of["low_again"] + k)
        fine(again, k, first, STEPS - 1, rough=True)
        fine(first, 0, second, STEPS - 2)

        def emit(spot, value, stepped):
            if k + 1 < nt - 1:
                put(defect, k + 1, spot, stepped - get(again, k + 1, spot))
            else:
                put(end, 0, spot, stepped)
            base = get(coarse, 0, spot)
            if k:
                put(offset, k + 1, spot, stepped - base)
            else:
                put(chain, 1, spot, base + (stepped - base))

        march(second, 0, low_own, high_own, emit)

    def lift_between(j, low, high):
        def emit(spot, value, stepped):
            put(chain, j, spot, rough_of(value, stepped) + get(offset, j, spot))

        march(chain, j - 1, low, high, emit)

    def edges_of(j):
        slots = recv_of["high_offset"] + j, recv_of["low_offset"] + j
        return body_view(offset, j), nt - 1 - j, *slots

    def lift_around(j):
        halo = nt - 1 - j
        if halo:
            shared(*edges_of(j))
            lift_between(j, low_own - halo, low_own)
            lift_between(j, high_own, high_own + halo)

    relay_start(0)
    relay_rate()
    give_guess(1)
    relay_start(1)
    start_ready(0)
    rate_ready()
    relax(0)
    send_again(0)
    hand_in(chain, 0, corrected_out, "corrected", 0)
    hand_in(defect, 0, defect_out, "defect", 0)
    relay_start(2)
    start_ready(1)
    relax(1)
    send_again(1)
    finish(0)
    first_edges = body_view(chain, 1), nt - 2, recv_of["high_first"], recv_of["low_first"]
    share(*first_edges)
    hand_in(chain, 1, corrected_out, "corrected", 1)
    hand_in(defect, 1, defect_out, "defect", 1)
    for j in range(2, nt):
        if j < nt - 1:
            start_ready(j)
            relax(j)
            send_again(j)
        finish(j - 1)
        if j < nt - 1:
            share(*edges_of(j))
            relay_start(j + 1)
            hand_in(defect, j, defect_out, "defect", j)
        if j == 2:
            shared(*first_edges)
        else:
            lift_around(j - 1)
        lift_between(j, low_own, high_own)
        hand_in(chain, j, corrected_out, "corrected", j)
    start_ready(nt - 1)
    relax(nt - 1)
    hand_in(defect, nt - 1, defect_out, "defect", nt - 1)

    for copy, condition in sends:
        pl.when(condition)(copy.wait_send)
    for out, kind in ((corrected_out, "corrected"), (defect_out, "defect")):
        for number in range(nt):
            size = inner if 0 < number < nt - 1 else outer
            dst = out.at[:, :, pl.ds(own_begin(number), size), :]
            pltpu.make_async_copy(dst, dst, recv.at[recv_of[kind] + number]).wait()


def settle_kernel(corrected, defect, corrected_out, defect_out, local):
    copies = []
    for src, dst in ((corrected, corrected_out), (defect, defect_out)):
        for tile in range(src.shape[1]):
            to = dst.at[0, :, :, pl.ds(tile * LANES, LANES)]
            copies.append(pltpu.make_async_copy(src.at[:, tile], to, local.at[len(copies)]))
    for copy in copies:
        copy.start()
    for copy in copies:
        copy.wait()


def settle(corrected, defect):
    planes, tiles, across, lanes = corrected.shape
    shape = jax.ShapeDtypeStruct((1, planes, across, tiles * lanes), jnp.float32)
    return pl.pallas_call(
        settle_kernel,
        out_shape=(shape, shape),
        in_specs=[pl.BlockSpec(memory_space=pl.ANY)] * 2,
        out_specs=[pl.BlockSpec(memory_space=pl.ANY)] * 2,
        scratch_shapes=[pltpu.SemaphoreType.DMA((2 * tiles,))],
        compiler_params=pltpu.CompilerParams(vmem_limit_bytes=1 << 20),
    )(corrected, defect)


def quarter_device(nt, ns, initial, coarse_guess, react_rate):
    planes, across, width = initial.shape
    wide, inner = quarter_rows(nt, across)
    length = planes + 2 * STEPS
    tall = inner + 5 * wide
    tiles = width // LANES
    recv_of, recv_total = quarter_slots(nt, tiles)

    def field(number):
        return pltpu.VMEM((number, length, tiles, tall, LANES), jnp.float32)

    shape = jax.ShapeDtypeStruct((planes, tiles, across, LANES), jnp.float32)
    corrected, defect = pl.pallas_call(
        functools.partial(quarter_kernel, nt, ns, planes, inner, wide, recv_of),
        out_shape=(shape, shape),
        in_specs=[pl.BlockSpec(memory_space=pltpu.HBM)] * 3,
        out_specs=[pl.BlockSpec(memory_space=pl.ANY)] * 2,
        scratch_shapes=[
            field(nt), field(nt), field(1), field(1), field(1), field(1), field(nt), field(nt), field(nt), field(1),
            pltpu.SemaphoreType.DMA((tiles * (CORES * (1 + nt // 2) + 4 * nt + 2) + 6 * nt - 6,)),
            pltpu.SemaphoreType.DMA((recv_total,)),
        ],
        compiler_params=pltpu.CompilerParams(collective_id=0, has_side_effects=True, vmem_limit_bytes=VMEM_BYTES),
    )(*(pltpu.with_memory_space_constraint(ref, pltpu.HBM) for ref in (initial, coarse_guess[0], react_rate)))
    return settle(corrected, defect)


def quarter_rows(nt, across):
    wide = -(-(2 * STEPS + max(nt - 2, 0)) // SUBLANES) * SUBLANES
    return wide, (across - 4 * wide) // nt


def takes_quarters(nt, planes, across, width):
    wide, inner = quarter_rows(nt, across)
    fits = inner > 0 and (across - 4 * wide) % (nt * SUBLANES) == 0 and nt - 2 <= planes
    return nt % 2 == 0 and nt > 2 and planes >= STEPS and width % LANES == 0 and fits


def on_device(nt, ns, initial, coarse_guess, react_rate):
    planes, across, width = initial.shape
    if takes_quarters(nt, planes, across, width):
        return quarter_device(nt, ns, initial, coarse_guess, react_rate)
    half = across // 2
    wide = -(-(2 * STEPS + max(nt - 2, 0)) // SUBLANES) * SUBLANES
    length = 2 * planes + 2 * STEPS
    field = pltpu.VMEM((length, half + 2 * wide, width), jnp.float32)
    slot_of, total = slots(planes)
    shape = jax.ShapeDtypeStruct(initial.shape, jnp.float32)
    corrected, defect = pl.pallas_call(
        functools.partial(kernel, nt, ns, planes, half, wide, slot_of),
        out_shape=(shape, shape),
        in_specs=[pl.BlockSpec(memory_space=pl.ANY)] * 3,
        out_specs=[pl.BlockSpec(memory_space=pl.ANY)] * 2,
        scratch_shapes=[field] * 11
        + [
            pltpu.VMEM((half + 2 * wide, width), jnp.float32),
            pltpu.SemaphoreType.DMA((total,)),
            pltpu.SemaphoreType.DMA((total,)),
            pltpu.SemaphoreType.DMA((3 + planes,)),
        ],
        compiler_params=pltpu.CompilerParams(collective_id=0, has_side_effects=True),
    )(initial, coarse_guess[0], react_rate)
    return corrected[None], defect[None]


def solution(mesh):
    in_specs = (P("space", None, None), P("tm", "space", None, None), P("space", None, None))
    out_specs = (P("tm", "space", None, None), P("tm", "space", None, None))
    return jax.shard_map(
        functools.partial(on_device, mesh.shape["tm"], mesh.shape["space"]),
        mesh=mesh, in_specs=in_specs, out_specs=out_specs, check_vma=False,
    )
```

```python
import functools

import jax
import jax.numpy as jnp
from jax import lax
from jax.experimental import pallas as pl
from jax.experimental.pallas import tpu as pltpu
from jax.sharding import PartitionSpec as P

STEPS = 3
SUBLANES = 8

fine_diffuse = 0.04
fine_growth = 0.05
coarse_ratio = 4.0

MESH = pl.DeviceIdType.MESH

PIECES = 4
LANES = 128
CORES = 2
VMEM_BYTES = 40 << 20


def slots(planes):
    kinds = dict(
        start=2 + PIECES, start_edge=1 + PIECES, rate=1, rate_edge=2, rate_core=3, again=PIECES, again_edge=2 * PIECES,
        chain=2 * planes, chain_edge=2, defect=1, corrected=planes,
    )
    first, total = {}, 0
    for kind, number in kinds.items():
        first[kind] = total
        total += number
    return first, total


def kernel(
    nt, ns, planes, half, wide, slot_of,
    initial, guess, rate_in, corrected_out, defect_out,
    start, rate, again, before, first, second, relaxed, coarse, offset, defect, after, reach,
    send, recv, local,
):
    tm, space = lax.axis_index("tm"), lax.axis_index("space")
    pair, side = lax.div(space, 2), lax.rem(space, 2)
    pairs = ns // 2
    mate = space + 1 - 2 * side
    block = 2 * planes
    length = block + 2 * STEPS
    rows = half + 2 * wide
    has_low, has_high = pair > 0, pair < pairs - 1
    has_next, has_previous = tm < nt - 1, tm > 0
    own = pl.ds(STEPS, block)

    for ref in (start, rate, again, before):
        zero_plane = jnp.zeros((STEPS,) + ref.shape[1:], jnp.float32)
        zero_rows = jnp.zeros((block, wide, ref.shape[2]), jnp.float32)
        ref[0:STEPS] = zero_plane
        ref[STEPS + block : length] = zero_plane
        ref[STEPS : STEPS + block, 0:wide] = zero_rows
        ref[STEPS : STEPS + block, wide + half : rows] = zero_rows

    barrier = pltpu.get_barrier_semaphore()
    count = jnp.int32(0)
    for step in (-1, 0, 1):
        for place in ("own", "mate", "low", "high"):
            if step == 0 and place == "own":
                continue
            there = {"own": space, "mate": mate, "low": space - 2, "high": space + 2}[place]
            tests = []
            if step:
                tests.append(has_next if step > 0 else has_previous)
            if place in ("low", "high"):
                tests.append(has_low if place == "low" else has_high)
            target = {"tm": tm + step, "space": there}
            if tests:
                valid = functools.reduce(jnp.logical_and, tests)

                @pl.when(valid)
                def _(target=target):
                    pl.semaphore_signal(barrier, inc=1, device_id=target, device_id_type=MESH)

                count = count + valid.astype(jnp.int32)
            else:
                pl.semaphore_signal(barrier, inc=1, device_id=target, device_id_type=MESH)
                count = count + 1
    for here, there in ((tm == 0, nt - 1), (tm == nt - 1, 0)):

        @pl.when(here)
        def _(there=there):
            pl.semaphore_signal(
                barrier, inc=1, device_id={"tm": there, "space": mate}, device_id_type=MESH
            )

        count = count + here.astype(jnp.int32)
    pl.semaphore_wait(barrier, count)

    def remote(src, dst, slot, to_tm, to_space):
        return pltpu.make_async_remote_copy(
            src_ref=src,
            dst_ref=dst,
            send_sem=send.at[slot],
            recv_sem=recv.at[slot],
            device_id={"tm": to_tm, "space": to_space},
            device_id_type=MESH,
        )

    def cut(ref, target):
        return ref.at[:, pl.ds(pl.multiple_of(target * (half - wide), SUBLANES), half + wide), :]

    def spot(ref, target, begin, size):
        at = pl.multiple_of(wide * (1 - target), SUBLANES)
        return ref.at[pl.ds(begin, size), pl.ds(at, half + wide), :]

    slab = STEPS + planes * side
    other = STEPS + planes * (1 - side)

    core = lax.rem(tm, 2)
    twin = tm + 1 - 2 * core
    lanes = start.shape[2] // 2

    def lane_half(ref, which):
        return ref.at[:, :, pl.ds(pl.multiple_of(which * lanes, lanes), lanes)]

    groups = (half + wide) // SUBLANES
    bounds = [groups * piece // PIECES * SUBLANES for piece in range(PIECES + 1)]

    def piece_of(ref, begin, size, piece, target=side):
        at = pl.multiple_of(wide * (1 - target) + bounds[piece], SUBLANES)
        return ref.at[pl.ds(begin, size), pl.ds(at, bounds[piece + 1] - bounds[piece]), :]

    def cut_piece(ref, target, piece):
        at = pl.multiple_of(target * (half - wide) + bounds[piece], SUBLANES)
        return ref.at[:, pl.ds(at, bounds[piece + 1] - bounds[piece]), :]

    rate_own = pltpu.make_async_copy(cut(rate_in, side), spot(rate, side, slab, planes), local.at[0])
    rate_mate = remote(
        lane_half(cut(rate_in, 1 - side), core),
        lane_half(spot(rate, 1 - side, slab, planes), core),
        slot_of["rate"],
        tm,
        mate,
    )
    initial_own = pltpu.make_async_copy(cut(initial, side), spot(start, side, slab, planes), local.at[1])
    guess_own = remote(
        cut(guess, side), spot(start, side, slab, planes), slot_of["start"], tm + 1, space
    )

    def to_mate(ref, to_tm):
        return [
            remote(
                cut_piece(ref, 1 - side, piece),
                piece_of(start, slab, planes, piece, 1 - side),
                slot_of["start"] + 1 + piece,
                to_tm,
                mate,
            )
            for piece in range(PIECES)
        ]

    guess_mate = to_mate(guess, tm + 1)
    initial_mate = to_mate(initial, 0)
    is_last = tm == nt - 1

    rate_mate.start()
    rate_own.start()

    @pl.when(has_next)
    def _():
        guess_own.start()
        for copy in guess_mate:
            copy.start()

    @pl.when(is_last)
    def _():
        for copy in initial_mate:
            copy.start()

    @pl.when(tm == 0)
    def _():
        initial_own.start()

    for ref in (first, second):
        @pl.when(jnp.logical_not(has_low))
        def _(ref=ref):
            ref[0:STEPS] = jnp.zeros((STEPS,) + ref.shape[1:], jnp.float32)

        @pl.when(jnp.logical_not(has_high))
        def _(ref=ref):
            ref[STEPS + block : length] = jnp.zeros((STEPS,) + ref.shape[1:], jnp.float32)

    row = lax.broadcasted_iota(jnp.int32, reach.shape, 0)
    outside = jnp.logical_or(
        jnp.logical_and(side == 0, row < wide), jnp.logical_and(side == 1, row >= wide + half)
    )
    reach[...] = jnp.where(outside, 0.0, fine_diffuse)

    low_place, high_place = STEPS + block, 0

    def edge_pieces(piece):
        slot = slot_of["start_edge"] + 1 + piece
        low = remote(
            piece_of(start, STEPS, STEPS, piece), piece_of(start, low_place, STEPS, piece),
            slot, tm, space - 2,
        )
        high = remote(
            piece_of(start, block, STEPS, piece), piece_of(start, high_place, STEPS, piece),
            slot, tm, space + 2,
        )
        return low, high

    start_edges = [edge_pieces(piece) for piece in range(PIECES)]
    start_low = remote(
        spot(start, side, STEPS, STEPS), spot(start, side, low_place, STEPS),
        slot_of["start_edge"], tm, space - 2,
    )
    start_high = remote(
        spot(start, side, block, STEPS), spot(start, side, high_place, STEPS),
        slot_of["start_edge"], tm, space + 2,
    )
    reach_rate = STEPS - 1
    rate_low_spot = lane_half(spot(rate, side, low_place, reach_rate), core)
    rate_high_spot = lane_half(spot(rate, side, high_place + 1, reach_rate), core)
    rate_low = remote(
        lane_half(spot(rate, side, STEPS, reach_rate), core), rate_low_spot,
        slot_of["rate_edge"], tm, space - 2,
    )
    rate_high = remote(
        lane_half(spot(rate, side, STEPS + block - reach_rate, reach_rate), core), rate_high_spot,
        slot_of["rate_edge"] + 1, tm, space + 2,
    )
    rate_other_spot = lane_half(spot(rate, side, other, planes), core)
    twin_mate = remote(rate_other_spot, rate_other_spot, slot_of["rate_core"], twin, space)
    twin_low = remote(rate_low_spot, rate_low_spot, slot_of["rate_core"] + 1, twin, space)
    twin_high = remote(rate_high_spot, rate_high_spot, slot_of["rate_core"] + 2, twin, space)

    own_low = jnp.logical_and(side == 0, has_low)
    own_high = jnp.logical_and(side == 1, has_high)
    other_low = jnp.logical_and(side == 1, has_low)
    other_high = jnp.logical_and(side == 0, has_high)

    rate_own.wait()
    pl.when(own_low)(rate_low.start)
    pl.when(own_high)(rate_high.start)

    @pl.when(tm == 0)
    def _():
        initial_own.wait()

    @pl.when(has_previous)
    def _():
        guess_own.wait_recv()

    pl.when(own_low)(start_low.start)
    pl.when(own_high)(start_high.start)

    rate_mate.wait_recv()
    pl.when(other_low)(rate_low.start)
    pl.when(other_high)(rate_high.start)
    twin_mate.start()

    for piece in range(PIECES):
        guess_mate[piece].wait_recv()
        pl.when(other_low)(start_edges[piece][0].start)
        pl.when(other_high)(start_edges[piece][1].start)

    @pl.when(has_high)
    def _():
        rate_low.wait_recv()
        twin_low.start()

    @pl.when(has_low)
    def _():
        rate_high.wait_recv()
        twin_high.start()

    twin_mate.wait_recv()
    pl.when(has_high)(twin_low.wait_recv)
    pl.when(has_low)(twin_high.wait_recv)

    @pl.when(jnp.logical_and(side == 0, has_high))
    def _():
        start_low.wait_recv()

    @pl.when(jnp.logical_and(side == 1, has_low))
    def _():
        start_high.wait_recv()

    @pl.when(jnp.logical_and(side == 1, has_high))
    def _():
        for low, high in start_edges:
            low.wait_recv()

    @pl.when(jnp.logical_and(side == 0, has_low))
    def _():
        for low, high in start_edges:
            high.wait_recv()

    keep = pltpu.make_async_copy(start, again, local.at[1])

    @pl.when(tm == 0)
    def _():
        keep.start()

    width = start.shape[2]
    lane = lax.broadcasted_iota(jnp.int32, reach.shape, 1)

    def change(ref, z):
        middle = ref[z]
        beside = ref[z + 1] + ref[z - 1]
        beside = beside + pltpu.roll(middle, 1, 0) + pltpu.roll(middle, rows - 1, 0)
        beside = beside + jnp.where(lane == 0, 0.0, pltpu.roll(middle, 1, 1))
        beside = beside + jnp.where(lane == width - 1, 0.0, pltpu.roll(middle, width - 1, 1))
        growth = rate[z] * (fine_growth - fine_growth * (middle * middle))
        return middle, reach[...] * beside + middle * (growth - 6.0 * fine_diffuse)

    def span(step):
        low = jnp.where(has_low, step, max(step, STEPS))
        high = jnp.where(has_high, length - step, min(length - step, STEPS + block))
        return low, high

    def fine(src, dst, step):
        def plane(z, carry):
            middle, delta = change(src, z)
            dst[z] = middle + delta
            return carry

        lax.fori_loop(*span(step), plane, 0)

    fine(start, first, 1)
    fine(first, second, 2)
    fine(second, relaxed, 3)

    given, given_low, given_high = [], [], []
    for piece in range(PIECES):
        slot = slot_of["again_edge"] + 2 * piece
        given.append(
            remote(
                piece_of(relaxed, STEPS, block, piece),
                piece_of(again, STEPS, block, piece),
                slot_of["again"] + piece,
                tm + 1,
                space,
            )
        )
        given_low.append(
            remote(
                piece_of(again, STEPS, STEPS, piece),
                piece_of(again, STEPS + block, STEPS, piece),
                slot,
                tm,
                space - 2,
            )
        )
        given_high.append(
            remote(
                piece_of(again, block, STEPS, piece),
                piece_of(again, 0, STEPS, piece),
                slot + 1,
                tm,
                space + 2,
            )
        )

    @pl.when(has_next)
    def _():
        for piece in range(PIECES):
            given[piece].start()

    @pl.when(tm == 0)
    def _():
        keep.wait()

    @pl.when(has_previous)
    def _():
        for piece in range(PIECES):
            given[piece].wait_recv()
            pl.when(has_low)(given_low[piece].start)
            pl.when(has_high)(given_high[piece].start)
        for piece in range(PIECES):
            pl.when(has_high)(given_low[piece].wait_recv)
            pl.when(has_low)(given_high[piece].wait_recv)

    def first_plane(z, carry):
        middle, delta = change(again, z)
        first[z] = middle + delta
        coarse[z] = middle + coarse_ratio * delta
        return carry

    lax.fori_loop(*span(1), first_plane, 0)
    fine(first, second, 2)

    order = []
    for depth in range(planes):
        order += [STEPS + depth, STEPS + block - 1 - depth]

    def row_span(z):
        at = pl.multiple_of(wide * (1 - side), SUBLANES)
        return (pl.ds(z, 1), pl.ds(at, half + wide), slice(None))

    passed = {
        z: remote(
            after.at[row_span(z)], before.at[row_span(z)], slot_of["chain"] + z - STEPS, tm + 1, space
        )
        for z in order
    }
    low_edge, high_edge = STEPS, STEPS + block - 1
    passed_low = remote(
        before.at[row_span(low_edge)], before.at[row_span(high_edge + 1)],
        slot_of["chain_edge"], tm, space - 2,
    )
    passed_high = remote(
        before.at[row_span(high_edge)], before.at[row_span(low_edge - 1)],
        slot_of["chain_edge"] + 1, tm, space + 2,
    )

    mine = pl.ds(pl.multiple_of(side * half, SUBLANES), half)
    middle_rows = pl.ds(wide, half)
    defect_stay = pltpu.make_async_copy(
        defect.at[pl.ds(slab, planes), middle_rows, :], defect_out.at[:, mine, :], local.at[2]
    )
    defect_go = remote(
        defect.at[pl.ds(other, planes), middle_rows, :], defect_out.at[:, mine, :],
        slot_of["defect"], tm, mate,
    )
    stay, go = {}, {}
    for z in order:
        place = (z - STEPS) % planes
        src = after.at[pl.ds(z, 1), middle_rows, :]
        dst = corrected_out.at[pl.ds(place, 1), mine, :]
        stay[z] = pltpu.make_async_copy(src, dst, local.at[3 + place])
        go[z] = remote(src, dst, slot_of["corrected"] + place, tm, mate)

    def at_home(z):
        return side == (z - STEPS) // planes

    def hand_in(z):
        pl.when(at_home(z))(stay[z].start)
        pl.when(jnp.logical_not(at_home(z)))(go[z].start)

    def last_plane(z):
        middle, delta = change(second, z)
        end = middle + delta
        defect[z] = end - relaxed[z]
        shift = end - coarse[z]
        offset[z] = shift
        after[z] = coarse[z] + shift

    def take_edges():
        passed[low_edge].wait_recv()
        pl.when(has_low)(passed_low.start)
        passed[high_edge].wait_recv()
        pl.when(has_high)(passed_high.start)

    pl.when(tm == 2)(take_edges)
    opens = jnp.logical_and(tm == 1, has_next)
    for index, z in enumerate(order):
        last_plane(z)
        if index:
            pl.when(opens)(passed[order[index - 1]].start)
    pl.when(opens)(passed[order[-1]].start)
    defect_go.start()
    defect_stay.start()

    later = tm > 1

    @pl.when(jnp.logical_not(later))
    def _():
        for z in order:
            hand_in(z)

    @pl.when(later)
    def _():
        pl.when(tm > 2)(take_edges)
        queue = order[2:]
        waiting = set(queue)

        def leave(z):
            pl.when(has_next)(passed[z].start)
            hand_in(z)

        for index, z in enumerate(order):
            while waiting & {z - 1, z, z + 1}:
                come = queue.pop(0)
                waiting.remove(come)
                passed[come].wait_recv()
            if z == low_edge:
                pl.when(has_low)(passed_high.wait_recv)
            if z == high_edge:
                pl.when(has_high)(passed_low.wait_recv)
            middle, delta = change(before, z)
            after[z] = middle + coarse_ratio * delta + offset[z]
            if index:
                leave(order[index - 1])
        leave(order[-1])
        pl.when(has_low)(passed_low.wait_send)
        pl.when(has_high)(passed_high.wait_send)

    onward = jnp.logical_and(tm > 0, has_next)

    @pl.when(is_last)
    def _():
        for copy in initial_mate:
            copy.wait_send()

    @pl.when(has_next)
    def _():
        guess_own.wait_send()
        for copy in guess_mate:
            copy.wait_send()

    rate_mate.wait_send()
    twin_mate.wait_send()
    pl.when(has_high)(twin_low.wait_send)
    pl.when(has_low)(twin_high.wait_send)
    pl.when(has_low)(rate_low.wait_send)
    pl.when(has_high)(rate_high.wait_send)
    pl.when(own_low)(start_low.wait_send)
    pl.when(own_high)(start_high.wait_send)

    @pl.when(other_low)
    def _():
        for low, high in start_edges:
            low.wait_send()

    @pl.when(other_high)
    def _():
        for low, high in start_edges:
            high.wait_send()

    @pl.when(has_next)
    def _():
        for piece in range(PIECES):
            given[piece].wait_send()

    @pl.when(has_previous)
    def _():
        for piece in range(PIECES):
            pl.when(has_low)(given_low[piece].wait_send)
            pl.when(has_high)(given_high[piece].wait_send)

    @pl.when(onward)
    def _():
        for z in order:
            passed[z].wait_send()

    defect_stay.wait()
    defect_go.wait()
    for z in order:
        pl.when(at_home(z))(stay[z].wait)
        pl.when(at_home(z))(go[z].wait_recv)
        pl.when(jnp.logical_not(at_home(z)))(go[z].wait_send)


def quarter_slots(nt, tiles):
    kinds = dict(
        initial=CORES * tiles, rate=CORES * tiles, guess=nt * tiles, low_start=nt * tiles, high_start=nt * tiles,
        low_rate=tiles, high_rate=tiles, low_again=nt, high_again=nt, low_first=1, high_first=1,
        low_offset=nt, high_offset=nt, corrected=nt, defect=nt,
    )
    first, total = {}, 0
    for kind, number in kinds.items():
        first[kind] = total
        total += number
    return first, total


def quarter_kernel(
    nt, ns, planes, inner, wide, recv_of,
    initial, guess, rate_in, corrected_out, defect_out,
    start, again, rate, first, second, coarse, chain, offset, defect, end,
    send, recv,
):
    tm, space = lax.axis_index("tm"), lax.axis_index("space")
    y, core = lax.div(tm, 2), lax.rem(tm, 2)
    pair, x = lax.div(space, 2), lax.rem(space, 2)
    levels, pairs = nt // 2, ns // 2
    length = planes + 2 * STEPS
    outer, most = inner + 2 * wide, inner + 3 * wide
    less = most - wide
    across = initial.shape[1]
    tiles = start.shape[2]
    low_own, high_own = STEPS, STEPS + planes
    slab = 2 * pair + core
    has_low, has_high = slab > 0, slab < ns - 1
    edge = y == levels - 1
    inside = jnp.logical_not(edge)
    first_row, last_row = jnp.logical_and(edge, x == 0), jnp.logical_and(edge, x == 1)
    low_to = {"tm": tm + 1 - 2 * core, "space": space - 2 * (1 - core)}
    high_to = {"tm": tm + 1 - 2 * core, "space": space + 2 * core}

    def begin_of(to_y, to_x):
        own_begin = outer + inner * (2 * to_y + to_x)
        begin = jnp.where(to_y == levels - 1, to_x * (across - most), own_begin - wide)
        return pl.multiple_of(begin, SUBLANES)

    my_begin = begin_of(y, x)
    my_part = jnp.where(edge, x * (nt - 1), 1 + 2 * y + x)
    inset = pl.multiple_of(jnp.where(first_row, 0, wide), SUBLANES)
    body = pl.ds(wide, most)

    edge_zero = jnp.zeros((length, tiles, wide, LANES), jnp.float32)
    plane_zero = jnp.zeros((STEPS,) + start.shape[2:], jnp.float32)

    def clear_rows(ref, k):
        @pl.when(first_row)
        def _():
            ref[k, :, :, 0:wide] = edge_zero

        @pl.when(last_row)
        def _():
            ref[k, :, :, wide + most : 2 * wide + most] = edge_zero

    def clear_planes(ref, k):
        @pl.when(jnp.logical_not(has_low))
        def _():
            ref[k, 0:low_own] = plane_zero

        @pl.when(jnp.logical_not(has_high))
        def _():
            ref[k, high_own:length] = plane_zero

    barrier = pltpu.get_barrier_semaphore()
    for dy in range(levels):
        for dx in range(2):
            for dc in range(2):
                if dy or dx or dc:
                    there = {
                        "tm": 2 * lax.rem(y + dy, levels) + lax.rem(core + dc, 2),
                        "space": 2 * pair + lax.rem(x + dx, 2),
                    }
                    pl.semaphore_signal(barrier, inc=1, device_id=there, device_id_type=MESH)
    count = jnp.int32(2 * nt - 1)
    for far, there in (
        (jnp.logical_and(core == 0, has_low), low_to),
        (jnp.logical_and(core == 1, has_high), high_to),
    ):

        @pl.when(far)
        def _(there=there):
            pl.semaphore_signal(barrier, inc=1, device_id=there, device_id_type=MESH)

        count = count + far.astype(jnp.int32)

    for k in range(nt):
        clear_rows(start, k)
        clear_planes(start, k)
    for k in range(nt - 1):
        clear_rows(again, k)
        clear_planes(again, k)
        clear_rows(chain, k)
    clear_rows(first, 0)
    clear_rows(second, 0)
    clear_planes(rate, 0)
    clear_planes(chain, 1)
    for j in range(2, nt - 1):
        clear_planes(offset, j)

    pl.semaphore_wait(barrier, count)

    sends = []
    send_count = [0]

    def launch(make, slot, there, condition, wider):
        number = send_count[0]
        send_count[0] += 1
        for rows, fits in ((most, wider), (less, jnp.logical_not(wider))):
            src, dst = make(rows)
            copy = pltpu.make_async_remote_copy(
                src_ref=src, dst_ref=dst, send_sem=send.at[number], recv_sem=recv.at[slot],
                device_id=there, device_id_type=MESH,
            )
            sends.append((copy, jnp.logical_and(condition, fits)))
            pl.when(jnp.logical_and(condition, fits))(copy.start)

    def local(make, slot, condition):
        for rows, fits in ((most, edge), (less, inside)):
            src, dst = make(rows)
            pl.when(jnp.logical_and(condition, fits))(pltpu.make_async_copy(src, dst, recv.at[slot]).start)

    def arrive(dst_of, slot, condition=True):
        for rows, fits in ((most, edge), (less, inside)):
            dst = dst_of(rows)
            pl.when(jnp.logical_and(condition, fits))(pltpu.make_async_copy(dst, dst, recv.at[slot]).wait)

    own = pl.ds(low_own, planes)
    home = core == x
    away = jnp.logical_not(home)

    cut = -(-most // (CORES * SUBLANES)) * SUBLANES

    def filling(src, begin, ref, k, tile, turn=None):
        def make(rows):
            at, size = (0, rows) if turn is None else (cut * turn, min(cut * (turn + 1), rows) - cut * turn)
            from_rows = pl.ds(pl.multiple_of(begin + at, SUBLANES), size)
            return src.at[:, from_rows, pl.ds(tile * LANES, LANES)], ref.at[k, own, tile, pl.ds(wide + at, size), :]

        return make

    def arrive_filling(ref, k, tile, slot, turn=None):
        arrive(lambda rows: filling(initial, 0, ref, k, tile, turn)(rows)[1], slot)

    for ref, src, kind in ((start, initial, "initial"), (rate, rate_in, "rate")):
        for tile in range(tiles):
            for turn in range(CORES):
                local(filling(src, my_begin, ref, 0, tile, turn), recv_of[kind] + CORES * tile + turn, home)

    def give_split(src, ref, kind, to_y, condition, wider):
        begin = begin_of(to_y, 1 - x)
        for tile in range(tiles):
            for turn in range(CORES):
                launch(
                    filling(src, begin, ref, 0, tile, turn), recv_of[kind] + CORES * tile + turn,
                    {"tm": 2 * to_y + x, "space": space + 1 - 2 * x}, jnp.logical_and(condition, core == turn), wider,
                )

    give_split(initial, start, "initial", y, jnp.bool_(True), edge)
    for to_y in range(levels):
        give_split(rate_in, rate, "rate", to_y, edge, jnp.bool_(to_y == levels - 1))

    def give_guess(turn):
        gives = jnp.logical_and(tm < nt - 1, core == turn)
        number = jnp.minimum(tm + 1, nt - 1)
        for tile in range(tiles):
            slot = recv_of["guess"] + number * tiles + tile
            for dy in range(levels):
                for dx in (1, 0):
                    to_y, to_x = lax.rem(y + dy, levels), lax.rem(x + dx, 2)
                    make = filling(guess, begin_of(to_y, to_x), start, number, tile)
                    there = {"tm": 2 * to_y + x, "space": 2 * pair + to_x}
                    if dy or dx:
                        launch(make, slot, there, gives, to_y == levels - 1)
                    else:
                        launch(make, slot, there, jnp.logical_and(gives, away), edge)
                        local(make, slot, jnp.logical_and(gives, home))

    give_guess(0)

    reaches = [jnp.where(inside_of, fine_diffuse, 0.0) for inside_of in (has_low, True, has_high)]
    reaches[1] = fine_diffuse

    def share(view, depth, high_slot, low_slot):
        def low(rows):
            return view(pl.ds(low_own, depth), rows), view(pl.ds(high_own, depth), rows)

        def high(rows):
            return view(pl.ds(high_own - depth, depth), rows), view(pl.ds(low_own - depth, depth), rows)

        launch(low, high_slot, low_to, has_low, edge)
        launch(high, low_slot, high_to, has_high, edge)

    def shared(view, depth, high_slot, low_slot):
        arrive(lambda rows: view(pl.ds(high_own, depth), rows), high_slot, has_high)
        arrive(lambda rows: view(pl.ds(low_own - depth, depth), rows), low_slot, has_low)

    def tile_view(ref, k, tile):
        return lambda zs, rows: ref.at[k, zs, tile, pl.ds(wide, rows), :]

    def relay_start(k):
        for tile in range(tiles):
            if k:
                arrive_filling(start, k, tile, recv_of["guess"] + k * tiles + tile)
            else:
                for turn in range(CORES):
                    arrive_filling(start, 0, tile, recv_of["initial"] + CORES * tile + turn, turn)
            at = k * tiles + tile
            share(tile_view(start, k, tile), STEPS, recv_of["high_start"] + at, recv_of["low_start"] + at)

    def start_ready(k):
        for tile in range(tiles):
            at = k * tiles + tile
            shared(tile_view(start, k, tile), STEPS, recv_of["high_start"] + at, recv_of["low_start"] + at)

    def relay_rate():
        for tile in range(tiles):
            for turn in range(CORES):
                arrive_filling(rate, 0, tile, recv_of["rate"] + CORES * tile + turn, turn)
            share(tile_view(rate, 0, tile), STEPS - 1, recv_of["high_rate"] + tile, recv_of["low_rate"] + tile)

    def rate_ready():
        for tile in range(tiles):
            shared(tile_view(rate, 0, tile), STEPS - 1, recv_of["high_rate"] + tile, recv_of["low_rate"] + tile)

    def body_view(ref, k):
        return lambda zs, rows: ref.at[k, zs, :, pl.ds(wide, rows), :]

    tall = next(number for number in (64, 32, 16, 8) if most % number == 0)
    lane = lax.broadcasted_iota(jnp.int32, (tall, LANES), 1)

    def march(src, k, low, high, emit):
        def block(number, carry):
            at = pl.multiple_of(wide + number * tall, SUBLANES)
            here = pl.ds(at, tall)

            def load(z):
                return [src[k, z, tile, here, :] for tile in range(tiles)]

            under, middle = load(low - 1), load(low)
            for z in range(low, high):
                over = load(z + 1)
                zone = 0 if z < low_own else 1 if z < high_own else 2
                after = [pltpu.roll(part_of, 1, 1) for part_of in middle]
                ahead = [pltpu.roll(part_of, LANES - 1, 1) for part_of in middle]
                for tile in range(tiles):
                    value = middle[tile]
                    left = after[tile - 1] if tile else 0.0
                    right = ahead[tile + 1] if tile + 1 < tiles else 0.0
                    beside = over[tile] + under[tile]
                    beside = beside + src[k, z, tile, pl.ds(at - 1, tall), :] + src[k, z, tile, pl.ds(at + 1, tall), :]
                    beside = beside + jnp.where(lane == 0, left, after[tile])
                    beside = beside + jnp.where(lane == LANES - 1, right, ahead[tile])
                    growth = rate[0, z, tile, here, :] * (fine_growth - fine_growth * (value * value))
                    stepped = reaches[zone] * beside + value * (growth + (1.0 - 6.0 * fine_diffuse))
                    emit((z, tile, here), value, stepped)
                under, middle = middle, over
            return carry

        lax.fori_loop(0, most // tall, block, 0)

    def rough_of(value, stepped):
        return value + coarse_ratio * (stepped - value)

    def put(ref, k, spot, value):
        z, tile, here = spot
        ref[k, z, tile, here, :] = value

    def get(ref, k, spot):
        z, tile, here = spot
        return ref[k, z, tile, here, :]

    def fine(src, source_k, dst, halo, rough=False):
        def emit(spot, value, stepped):
            put(dst, 0, spot, stepped)
            if rough and low_own <= spot[0] < high_own:
                put(coarse, 0, spot, rough_of(value, stepped))

        march(src, source_k, low_own - halo, high_own + halo, emit)

    def own_begin(number):
        return outer + inner * (number - 1) if number else 0

    def hand_in(ref, k, out, kind, j):
        begin = pl.multiple_of(my_begin + inset, SUBLANES)
        slot = recv_of[kind] + my_part

        def make(rows):
            size = outer if rows == most else inner
            src = ref.at[k, own, :, pl.ds(pl.multiple_of(wide + inset, SUBLANES), size), :]
            return src, out.at[:, :, pl.ds(begin, size), :]

        stays = jnp.logical_and(tm == j, home)
        launch(make, slot, {"tm": j, "space": 2 * pair + core}, jnp.logical_not(stays), edge)
        local(make, slot, stays)

    def relax(k):
        fine(start, k, first, STEPS - 1, rough=k == 0)
        fine(first, 0, second, STEPS - 2)

        def emit(spot, value, stepped):
            if k == nt - 1:
                put(defect, k, spot, get(end, 0, spot) - stepped)
                return
            put(again, k, spot, stepped)
            if k == 0:
                put(defect, 0, spot, stepped - stepped)
                base = get(coarse, 0, spot)
                put(chain, 0, spot, base + (stepped - base))

        march(second, 0, low_own, high_own, emit)

    def send_again(k):
        share(body_view(again, k), STEPS, recv_of["high_again"] + k, recv_of["low_again"] + k)

    def finish(k):
        shared(body_view(again, k), STEPS, recv_of["high_again"] + k, recv_of["low_again"] + k)
        fine(again, k, first, STEPS - 1, rough=True)
        fine(first, 0, second, STEPS - 2)

        def emit(spot, value, stepped):
            if k + 1 < nt - 1:
                put(defect, k + 1, spot, stepped - get(again, k + 1, spot))
            else:
                put(end, 0, spot, stepped)
            base = get(coarse, 0, spot)
            if k:
                put(offset, k + 1, spot, stepped - base)
            else:
                put(chain, 1, spot, base + (stepped - base))

        march(second, 0, low_own, high_own, emit)

    def lift_between(j, low, high):
        def emit(spot, value, stepped):
            put(chain, j, spot, rough_of(value, stepped) + get(offset, j, spot))

        march(chain, j - 1, low, high, emit)

    def edges_of(j):
        slots = recv_of["high_offset"] + j, recv_of["low_offset"] + j
        return body_view(offset, j), nt - 1 - j, *slots

    def lift_around(j):
        halo = nt - 1 - j
        if halo:
            shared(*edges_of(j))
            lift_between(j, low_own - halo, low_own)
            lift_between(j, high_own, high_own + halo)

    relay_start(0)
    relay_rate()
    give_guess(1)
    relay_start(1)
    start_ready(0)
    rate_ready()
    relax(0)
    send_again(0)
    hand_in(chain, 0, corrected_out, "corrected", 0)
    hand_in(defect, 0, defect_out, "defect", 0)
    relay_start(2)
    start_ready(1)
    relax(1)
    send_again(1)
    finish(0)
    first_edges = body_view(chain, 1), nt - 2, recv_of["high_first"], recv_of["low_first"]
    share(*first_edges)
    hand_in(chain, 1, corrected_out, "corrected", 1)
    hand_in(defect, 1, defect_out, "defect", 1)
    for j in range(2, nt):
        if j < nt - 1:
            start_ready(j)
            relax(j)
            send_again(j)
        finish(j - 1)
        if j < nt - 1:
            share(*edges_of(j))
            relay_start(j + 1)
            hand_in(defect, j, defect_out, "defect", j)
        if j == 2:
            shared(*first_edges)
        else:
            lift_around(j - 1)
        lift_between(j, low_own, high_own)
        hand_in(chain, j, corrected_out, "corrected", j)
    start_ready(nt - 1)
    relax(nt - 1)
    hand_in(defect, nt - 1, defect_out, "defect", nt - 1)

    for copy, condition in sends:
        pl.when(condition)(copy.wait_send)
    for out, kind in ((corrected_out, "corrected"), (defect_out, "defect")):
        for number in range(nt):
            size = inner if 0 < number < nt - 1 else outer
            dst = out.at[:, :, pl.ds(own_begin(number), size), :]
            pltpu.make_async_copy(dst, dst, recv.at[recv_of[kind] + number]).wait()


def settle_kernel(corrected, defect, corrected_out, defect_out, local):
    copies = []
    for src, dst in ((corrected, corrected_out), (defect, defect_out)):
        for tile in range(src.shape[1]):
            to = dst.at[0, :, :, pl.ds(tile * LANES, LANES)]
            copies.append(pltpu.make_async_copy(src.at[:, tile], to, local.at[len(copies)]))
    for copy in copies:
        copy.start()
    for copy in copies:
        copy.wait()


def settle(corrected, defect):
    planes, tiles, across, lanes = corrected.shape
    shape = jax.ShapeDtypeStruct((1, planes, across, tiles * lanes), jnp.float32)
    return pl.pallas_call(
        settle_kernel,
        out_shape=(shape, shape),
        in_specs=[pl.BlockSpec(memory_space=pl.ANY)] * 2,
        out_specs=[pl.BlockSpec(memory_space=pl.ANY)] * 2,
        scratch_shapes=[pltpu.SemaphoreType.DMA((2 * tiles,))],
        compiler_params=pltpu.CompilerParams(vmem_limit_bytes=1 << 20),
    )(corrected, defect)


def quarter_device(nt, ns, initial, coarse_guess, react_rate):
    planes, across, width = initial.shape
    wide, inner = quarter_rows(nt, across)
    length = planes + 2 * STEPS
    tall = inner + 5 * wide
    tiles = width // LANES
    recv_of, recv_total = quarter_slots(nt, tiles)

    def field(number):
        return pltpu.VMEM((number, length, tiles, tall, LANES), jnp.float32)

    shape = jax.ShapeDtypeStruct((planes, tiles, across, LANES), jnp.float32)
    corrected, defect = pl.pallas_call(
        functools.partial(quarter_kernel, nt, ns, planes, inner, wide, recv_of),
        out_shape=(shape, shape),
        in_specs=[pl.BlockSpec(memory_space=pltpu.HBM)] * 3,
        out_specs=[pl.BlockSpec(memory_space=pl.ANY)] * 2,
        scratch_shapes=[
            field(nt), field(nt), field(1), field(1), field(1), field(1), field(nt), field(nt), field(nt), field(1),
            pltpu.SemaphoreType.DMA((tiles * (CORES * (1 + nt // 2) + 4 * nt + 2) + 6 * nt - 6,)),
            pltpu.SemaphoreType.DMA((recv_total,)),
        ],
        compiler_params=pltpu.CompilerParams(collective_id=0, has_side_effects=True, vmem_limit_bytes=VMEM_BYTES),
    )(*(pltpu.with_memory_space_constraint(ref, pltpu.HBM) for ref in (initial, coarse_guess[0], react_rate)))
    return settle(corrected, defect)


def quarter_rows(nt, across):
    wide = -(-(2 * STEPS + max(nt - 2, 0)) // SUBLANES) * SUBLANES
    return wide, (across - 4 * wide) // nt


def takes_quarters(nt, planes, across, width):
    wide, inner = quarter_rows(nt, across)
    fits = inner > 0 and (across - 4 * wide) % (nt * SUBLANES) == 0 and nt - 2 <= planes
    return nt % 2 == 0 and nt > 2 and planes >= STEPS and width % LANES == 0 and fits


def on_device(nt, ns, initial, coarse_guess, react_rate):
    planes, across, width = initial.shape
    if takes_quarters(nt, planes, across, width):
        return quarter_device(nt, ns, initial, coarse_guess, react_rate)
    half = across // 2
    wide = -(-(2 * STEPS + max(nt - 2, 0)) // SUBLANES) * SUBLANES
    length = 2 * planes + 2 * STEPS
    field = pltpu.VMEM((length, half + 2 * wide, width), jnp.float32)
    slot_of, total = slots(planes)
    shape = jax.ShapeDtypeStruct(initial.shape, jnp.float32)
    corrected, defect = pl.pallas_call(
        functools.partial(kernel, nt, ns, planes, half, wide, slot_of),
        out_shape=(shape, shape),
        in_specs=[pl.BlockSpec(memory_space=pl.ANY)] * 3,
        out_specs=[pl.BlockSpec(memory_space=pl.ANY)] * 2,
        scratch_shapes=[field] * 11
        + [
            pltpu.VMEM((half + 2 * wide, width), jnp.float32),
            pltpu.SemaphoreType.DMA((total,)),
            pltpu.SemaphoreType.DMA((total,)),
            pltpu.SemaphoreType.DMA((3 + planes,)),
        ],
        compiler_params=pltpu.CompilerParams(collective_id=0, has_side_effects=True),
    )(initial, coarse_guess[0], react_rate)
    return corrected[None], defect[None]


def solution(mesh):
    in_specs = (P("space", None, None), P("tm", "space", None, None), P("space", None, None))
    out_specs = (P("tm", "space", None, None), P("tm", "space", None, None))
    return jax.shard_map(
        functools.partial(on_device, mesh.shape["tm"], mesh.shape["space"]),
        mesh=mesh, in_specs=in_specs, out_specs=out_specs, check_vma=False,
    )
```

```python
import functools

import jax
import jax.numpy as jnp
from jax import lax
from jax.experimental import pallas as pl
from jax.experimental.pallas import tpu as pltpu
from jax.sharding import PartitionSpec as P

STEPS = 3
SUBLANES = 8

fine_diffuse = 0.04
fine_growth = 0.05
coarse_ratio = 4.0

MESH = pl.DeviceIdType.MESH

PIECES = 4
LANES = 128
CORES = 2
VMEM_BYTES = 40 << 20


def slots(planes):
    kinds = dict(
        start=2 + PIECES, start_edge=1 + PIECES, rate=1, rate_edge=2, rate_core=3, again=PIECES, again_edge=2 * PIECES,
        chain=2 * planes, chain_edge=2, defect=1, corrected=planes,
    )
    first, total = {}, 0
    for kind, number in kinds.items():
        first[kind] = total
        total += number
    return first, total


def kernel(
    nt, ns, planes, half, wide, slot_of,
    initial, guess, rate_in, corrected_out, defect_out,
    start, rate, again, before, first, second, relaxed, coarse, offset, defect, after, reach,
    send, recv, local,
):
    tm, space = lax.axis_index("tm"), lax.axis_index("space")
    pair, side = lax.div(space, 2), lax.rem(space, 2)
    pairs = ns // 2
    mate = space + 1 - 2 * side
    block = 2 * planes
    length = block + 2 * STEPS
    rows = half + 2 * wide
    has_low, has_high = pair > 0, pair < pairs - 1
    has_next, has_previous = tm < nt - 1, tm > 0
    own = pl.ds(STEPS, block)

    for ref in (start, rate, again, before):
        zero_plane = jnp.zeros((STEPS,) + ref.shape[1:], jnp.float32)
        zero_rows = jnp.zeros((block, wide, ref.shape[2]), jnp.float32)
        ref[0:STEPS] = zero_plane
        ref[STEPS + block : length] = zero_plane
        ref[STEPS : STEPS + block, 0:wide] = zero_rows
        ref[STEPS : STEPS + block, wide + half : rows] = zero_rows

    barrier = pltpu.get_barrier_semaphore()
    count = jnp.int32(0)
    for step in (-1, 0, 1):
        for place in ("own", "mate", "low", "high"):
            if step == 0 and place == "own":
                continue
            there = {"own": space, "mate": mate, "low": space - 2, "high": space + 2}[place]
            tests = []
            if step:
                tests.append(has_next if step > 0 else has_previous)
            if place in ("low", "high"):
                tests.append(has_low if place == "low" else has_high)
            target = {"tm": tm + step, "space": there}
            if tests:
                valid = functools.reduce(jnp.logical_and, tests)

                @pl.when(valid)
                def _(target=target):
                    pl.semaphore_signal(barrier, inc=1, device_id=target, device_id_type=MESH)

                count = count + valid.astype(jnp.int32)
            else:
                pl.semaphore_signal(barrier, inc=1, device_id=target, device_id_type=MESH)
                count = count + 1
    for here, there in ((tm == 0, nt - 1), (tm == nt - 1, 0)):

        @pl.when(here)
        def _(there=there):
            pl.semaphore_signal(
                barrier, inc=1, device_id={"tm": there, "space": mate}, device_id_type=MESH
            )

        count = count + here.astype(jnp.int32)
    pl.semaphore_wait(barrier, count)

    def remote(src, dst, slot, to_tm, to_space):
        return pltpu.make_async_remote_copy(
            src_ref=src,
            dst_ref=dst,
            send_sem=send.at[slot],
            recv_sem=recv.at[slot],
            device_id={"tm": to_tm, "space": to_space},
            device_id_type=MESH,
        )

    def cut(ref, target):
        return ref.at[:, pl.ds(pl.multiple_of(target * (half - wide), SUBLANES), half + wide), :]

    def spot(ref, target, begin, size):
        at = pl.multiple_of(wide * (1 - target), SUBLANES)
        return ref.at[pl.ds(begin, size), pl.ds(at, half + wide), :]

    slab = STEPS + planes * side
    other = STEPS + planes * (1 - side)

    core = lax.rem(tm, 2)
    twin = tm + 1 - 2 * core
    lanes = start.shape[2] // 2

    def lane_half(ref, which):
        return ref.at[:, :, pl.ds(pl.multiple_of(which * lanes, lanes), lanes)]

    groups = (half + wide) // SUBLANES
    bounds = [groups * piece // PIECES * SUBLANES for piece in range(PIECES + 1)]

    def piece_of(ref, begin, size, piece, target=side):
        at = pl.multiple_of(wide * (1 - target) + bounds[piece], SUBLANES)
        return ref.at[pl.ds(begin, size), pl.ds(at, bounds[piece + 1] - bounds[piece]), :]

    def cut_piece(ref, target, piece):
        at = pl.multiple_of(target * (half - wide) + bounds[piece], SUBLANES)
        return ref.at[:, pl.ds(at, bounds[piece + 1] - bounds[piece]), :]

    rate_own = pltpu.make_async_copy(cut(rate_in, side), spot(rate, side, slab, planes), local.at[0])
    rate_mate = remote(
        lane_half(cut(rate_in, 1 - side), core),
        lane_half(spot(rate, 1 - side, slab, planes), core),
        slot_of["rate"],
        tm,
        mate,
    )
    initial_own = pltpu.make_async_copy(cut(initial, side), spot(start, side, slab, planes), local.at[1])
    guess_own = remote(
        cut(guess, side), spot(start, side, slab, planes), slot_of["start"], tm + 1, space
    )

    def to_mate(ref, to_tm):
        return [
            remote(
                cut_piece(ref, 1 - side, piece),
                piece_of(start, slab, planes, piece, 1 - side),
                slot_of["start"] + 1 + piece,
                to_tm,
                mate,
            )
            for piece in range(PIECES)
        ]

    guess_mate = to_mate(guess, tm + 1)
    initial_mate = to_mate(initial, 0)
    is_last = tm == nt - 1

    rate_mate.start()
    rate_own.start()

    @pl.when(has_next)
    def _():
        guess_own.start()
        for copy in guess_mate:
            copy.start()

    @pl.when(is_last)
    def _():
        for copy in initial_mate:
            copy.start()

    @pl.when(tm == 0)
    def _():
        initial_own.start()

    for ref in (first, second):
        @pl.when(jnp.logical_not(has_low))
        def _(ref=ref):
            ref[0:STEPS] = jnp.zeros((STEPS,) + ref.shape[1:], jnp.float32)

        @pl.when(jnp.logical_not(has_high))
        def _(ref=ref):
            ref[STEPS + block : length] = jnp.zeros((STEPS,) + ref.shape[1:], jnp.float32)

    row = lax.broadcasted_iota(jnp.int32, reach.shape, 0)
    outside = jnp.logical_or(
        jnp.logical_and(side == 0, row < wide), jnp.logical_and(side == 1, row >= wide + half)
    )
    reach[...] = jnp.where(outside, 0.0, fine_diffuse)

    low_place, high_place = STEPS + block, 0

    def edge_pieces(piece):
        slot = slot_of["start_edge"] + 1 + piece
        low = remote(
            piece_of(start, STEPS, STEPS, piece), piece_of(start, low_place, STEPS, piece),
            slot, tm, space - 2,
        )
        high = remote(
            piece_of(start, block, STEPS, piece), piece_of(start, high_place, STEPS, piece),
            slot, tm, space + 2,
        )
        return low, high

    start_edges = [edge_pieces(piece) for piece in range(PIECES)]
    start_low = remote(
        spot(start, side, STEPS, STEPS), spot(start, side, low_place, STEPS),
        slot_of["start_edge"], tm, space - 2,
    )
    start_high = remote(
        spot(start, side, block, STEPS), spot(start, side, high_place, STEPS),
        slot_of["start_edge"], tm, space + 2,
    )
    reach_rate = STEPS - 1
    rate_low_spot = lane_half(spot(rate, side, low_place, reach_rate), core)
    rate_high_spot = lane_half(spot(rate, side, high_place + 1, reach_rate), core)
    rate_low = remote(
        lane_half(spot(rate, side, STEPS, reach_rate), core), rate_low_spot,
        slot_of["rate_edge"], tm, space - 2,
    )
    rate_high = remote(
        lane_half(spot(rate, side, STEPS + block - reach_rate, reach_rate), core), rate_high_spot,
        slot_of["rate_edge"] + 1, tm, space + 2,
    )
    rate_other_spot = lane_half(spot(rate, side, other, planes), core)
    twin_mate = remote(rate_other_spot, rate_other_spot, slot_of["rate_core"], twin, space)
    twin_low = remote(rate_low_spot, rate_low_spot, slot_of["rate_core"] + 1, twin, space)
    twin_high = remote(rate_high_spot, rate_high_spot, slot_of["rate_core"] + 2, twin, space)

    own_low = jnp.logical_and(side == 0, has_low)
    own_high = jnp.logical_and(side == 1, has_high)
    other_low = jnp.logical_and(side == 1, has_low)
    other_high = jnp.logical_and(side == 0, has_high)

    rate_own.wait()
    pl.when(own_low)(rate_low.start)
    pl.when(own_high)(rate_high.start)

    @pl.when(tm == 0)
    def _():
        initial_own.wait()

    @pl.when(has_previous)
    def _():
        guess_own.wait_recv()

    pl.when(own_low)(start_low.start)
    pl.when(own_high)(start_high.start)

    rate_mate.wait_recv()
    pl.when(other_low)(rate_low.start)
    pl.when(other_high)(rate_high.start)
    twin_mate.start()

    for piece in range(PIECES):
        guess_mate[piece].wait_recv()
        pl.when(other_low)(start_edges[piece][0].start)
        pl.when(other_high)(start_edges[piece][1].start)

    @pl.when(has_high)
    def _():
        rate_low.wait_recv()
        twin_low.start()

    @pl.when(has_low)
    def _():
        rate_high.wait_recv()
        twin_high.start()

    twin_mate.wait_recv()
    pl.when(has_high)(twin_low.wait_recv)
    pl.when(has_low)(twin_high.wait_recv)

    @pl.when(jnp.logical_and(side == 0, has_high))
    def _():
        start_low.wait_recv()

    @pl.when(jnp.logical_and(side == 1, has_low))
    def _():
        start_high.wait_recv()

    @pl.when(jnp.logical_and(side == 1, has_high))
    def _():
        for low, high in start_edges:
            low.wait_recv()

    @pl.when(jnp.logical_and(side == 0, has_low))
    def _():
        for low, high in start_edges:
            high.wait_recv()

    keep = pltpu.make_async_copy(start, again, local.at[1])

    @pl.when(tm == 0)
    def _():
        keep.start()

    width = start.shape[2]
    lane = lax.broadcasted_iota(jnp.int32, reach.shape, 1)

    def change(ref, z):
        middle = ref[z]
        beside = ref[z + 1] + ref[z - 1]
        beside = beside + pltpu.roll(middle, 1, 0) + pltpu.roll(middle, rows - 1, 0)
        beside = beside + jnp.where(lane == 0, 0.0, pltpu.roll(middle, 1, 1))
        beside = beside + jnp.where(lane == width - 1, 0.0, pltpu.roll(middle, width - 1, 1))
        growth = rate[z] * (fine_growth - fine_growth * (middle * middle))
        return middle, reach[...] * beside + middle * (growth - 6.0 * fine_diffuse)

    def span(step):
        low = jnp.where(has_low, step, max(step, STEPS))
        high = jnp.where(has_high, length - step, min(length - step, STEPS + block))
        return low, high

    def fine(src, dst, step):
        def plane(z, carry):
            middle, delta = change(src, z)
            dst[z] = middle + delta
            return carry

        lax.fori_loop(*span(step), plane, 0)

    fine(start, first, 1)
    fine(first, second, 2)
    fine(second, relaxed, 3)

    given, given_low, given_high = [], [], []
    for piece in range(PIECES):
        slot = slot_of["again_edge"] + 2 * piece
        given.append(
            remote(
                piece_of(relaxed, STEPS, block, piece),
                piece_of(again, STEPS, block, piece),
                slot_of["again"] + piece,
                tm + 1,
                space,
            )
        )
        given_low.append(
            remote(
                piece_of(again, STEPS, STEPS, piece),
                piece_of(again, STEPS + block, STEPS, piece),
                slot,
                tm,
                space - 2,
            )
        )
        given_high.append(
            remote(
                piece_of(again, block, STEPS, piece),
                piece_of(again, 0, STEPS, piece),
                slot + 1,
                tm,
                space + 2,
            )
        )

    @pl.when(has_next)
    def _():
        for piece in range(PIECES):
            given[piece].start()

    @pl.when(tm == 0)
    def _():
        keep.wait()

    @pl.when(has_previous)
    def _():
        for piece in range(PIECES):
            given[piece].wait_recv()
            pl.when(has_low)(given_low[piece].start)
            pl.when(has_high)(given_high[piece].start)
        for piece in range(PIECES):
            pl.when(has_high)(given_low[piece].wait_recv)
            pl.when(has_low)(given_high[piece].wait_recv)

    def first_plane(z, carry):
        middle, delta = change(again, z)
        first[z] = middle + delta
        coarse[z] = middle + coarse_ratio * delta
        return carry

    lax.fori_loop(*span(1), first_plane, 0)
    fine(first, second, 2)

    order = []
    for depth in range(planes):
        order += [STEPS + depth, STEPS + block - 1 - depth]

    def row_span(z):
        at = pl.multiple_of(wide * (1 - side), SUBLANES)
        return (pl.ds(z, 1), pl.ds(at, half + wide), slice(None))

    passed = {
        z: remote(
            after.at[row_span(z)], before.at[row_span(z)], slot_of["chain"] + z - STEPS, tm + 1, space
        )
        for z in order
    }
    low_edge, high_edge = STEPS, STEPS + block - 1
    passed_low = remote(
        before.at[row_span(low_edge)], before.at[row_span(high_edge + 1)],
        slot_of["chain_edge"], tm, space - 2,
    )
    passed_high = remote(
        before.at[row_span(high_edge)], before.at[row_span(low_edge - 1)],
        slot_of["chain_edge"] + 1, tm, space + 2,
    )

    mine = pl.ds(pl.multiple_of(side * half, SUBLANES), half)
    middle_rows = pl.ds(wide, half)
    defect_stay = pltpu.make_async_copy(
        defect.at[pl.ds(slab, planes), middle_rows, :], defect_out.at[:, mine, :], local.at[2]
    )
    defect_go = remote(
        defect.at[pl.ds(other, planes), middle_rows, :], defect_out.at[:, mine, :],
        slot_of["defect"], tm, mate,
    )
    stay, go = {}, {}
    for z in order:
        place = (z - STEPS) % planes
        src = after.at[pl.ds(z, 1), middle_rows, :]
        dst = corrected_out.at[pl.ds(place, 1), mine, :]
        stay[z] = pltpu.make_async_copy(src, dst, local.at[3 + place])
        go[z] = remote(src, dst, slot_of["corrected"] + place, tm, mate)

    def at_home(z):
        return side == (z - STEPS) // planes

    def hand_in(z):
        pl.when(at_home(z))(stay[z].start)
        pl.when(jnp.logical_not(at_home(z)))(go[z].start)

    def last_plane(z):
        middle, delta = change(second, z)
        end = middle + delta
        defect[z] = end - relaxed[z]
        shift = end - coarse[z]
        offset[z] = shift
        after[z] = coarse[z] + shift

    def take_edges():
        passed[low_edge].wait_recv()
        pl.when(has_low)(passed_low.start)
        passed[high_edge].wait_recv()
        pl.when(has_high)(passed_high.start)

    pl.when(tm == 2)(take_edges)
    opens = jnp.logical_and(tm == 1, has_next)
    for index, z in enumerate(order):
        last_plane(z)
        if index:
            pl.when(opens)(passed[order[index - 1]].start)
    pl.when(opens)(passed[order[-1]].start)
    defect_go.start()
    defect_stay.start()

    later = tm > 1

    @pl.when(jnp.logical_not(later))
    def _():
        for z in order:
            hand_in(z)

    @pl.when(later)
    def _():
        pl.when(tm > 2)(take_edges)
        queue = order[2:]
        waiting = set(queue)

        def leave(z):
            pl.when(has_next)(passed[z].start)
            hand_in(z)

        for index, z in enumerate(order):
            while waiting & {z - 1, z, z + 1}:
                come = queue.pop(0)
                waiting.remove(come)
                passed[come].wait_recv()
            if z == low_edge:
                pl.when(has_low)(passed_high.wait_recv)
            if z == high_edge:
                pl.when(has_high)(passed_low.wait_recv)
            middle, delta = change(before, z)
            after[z] = middle + coarse_ratio * delta + offset[z]
            if index:
                leave(order[index - 1])
        leave(order[-1])
        pl.when(has_low)(passed_low.wait_send)
        pl.when(has_high)(passed_high.wait_send)

    onward = jnp.logical_and(tm > 0, has_next)

    @pl.when(is_last)
    def _():
        for copy in initial_mate:
            copy.wait_send()

    @pl.when(has_next)
    def _():
        guess_own.wait_send()
        for copy in guess_mate:
            copy.wait_send()

    rate_mate.wait_send()
    twin_mate.wait_send()
    pl.when(has_high)(twin_low.wait_send)
    pl.when(has_low)(twin_high.wait_send)
    pl.when(has_low)(rate_low.wait_send)
    pl.when(has_high)(rate_high.wait_send)
    pl.when(own_low)(start_low.wait_send)
    pl.when(own_high)(start_high.wait_send)

    @pl.when(other_low)
    def _():
        for low, high in start_edges:
            low.wait_send()

    @pl.when(other_high)
    def _():
        for low, high in start_edges:
            high.wait_send()

    @pl.when(has_next)
    def _():
        for piece in range(PIECES):
            given[piece].wait_send()

    @pl.when(has_previous)
    def _():
        for piece in range(PIECES):
            pl.when(has_low)(given_low[piece].wait_send)
            pl.when(has_high)(given_high[piece].wait_send)

    @pl.when(onward)
    def _():
        for z in order:
            passed[z].wait_send()

    defect_stay.wait()
    defect_go.wait()
    for z in order:
        pl.when(at_home(z))(stay[z].wait)
        pl.when(at_home(z))(go[z].wait_recv)
        pl.when(jnp.logical_not(at_home(z)))(go[z].wait_send)


def quarter_slots(nt, tiles):
    kinds = dict(
        initial=CORES * tiles, rate=CORES * tiles, guess=nt * tiles, low_start=nt * tiles, high_start=nt * tiles,
        low_rate=tiles, high_rate=tiles, low_again=nt, high_again=nt, low_first=1, high_first=1,
        low_offset=nt, high_offset=nt, corrected=nt, defect=nt,
    )
    first, total = {}, 0
    for kind, number in kinds.items():
        first[kind] = total
        total += number
    return first, total


def quarter_kernel(
    nt, ns, planes, inner, wide, recv_of,
    initial, guess, rate_in, corrected_out, defect_out,
    start, again, rate, first, second, coarse, chain, offset, defect, end,
    send, recv,
):
    tm, space = lax.axis_index("tm"), lax.axis_index("space")
    y, core = lax.div(tm, 2), lax.rem(tm, 2)
    pair, x = lax.div(space, 2), lax.rem(space, 2)
    levels, pairs = nt // 2, ns // 2
    length = planes + 2 * STEPS
    outer, most = inner + 2 * wide, inner + 3 * wide
    less = most - wide
    across = initial.shape[1]
    tiles = start.shape[2]
    low_own, high_own = STEPS, STEPS + planes
    slab = 2 * pair + core
    has_low, has_high = slab > 0, slab < ns - 1
    edge = y == levels - 1
    inside = jnp.logical_not(edge)
    first_row, last_row = jnp.logical_and(edge, x == 0), jnp.logical_and(edge, x == 1)
    low_to = {"tm": tm + 1 - 2 * core, "space": space - 2 * (1 - core)}
    high_to = {"tm": tm + 1 - 2 * core, "space": space + 2 * core}

    def begin_of(to_y, to_x):
        own_begin = outer + inner * (2 * to_y + to_x)
        begin = jnp.where(to_y == levels - 1, to_x * (across - most), own_begin - wide)
        return pl.multiple_of(begin, SUBLANES)

    my_begin = begin_of(y, x)
    my_part = jnp.where(edge, x * (nt - 1), 1 + 2 * y + x)
    inset = pl.multiple_of(jnp.where(first_row, 0, wide), SUBLANES)
    body = pl.ds(wide, most)

    edge_zero = jnp.zeros((length, tiles, wide, LANES), jnp.float32)
    plane_zero = jnp.zeros((STEPS,) + start.shape[2:], jnp.float32)

    def clear_rows(ref, k):
        @pl.when(first_row)
        def _():
            ref[k, :, :, 0:wide] = edge_zero

        @pl.when(last_row)
        def _():
            ref[k, :, :, wide + most : 2 * wide + most] = edge_zero

    def clear_planes(ref, k):
        @pl.when(jnp.logical_not(has_low))
        def _():
            ref[k, 0:low_own] = plane_zero

        @pl.when(jnp.logical_not(has_high))
        def _():
            ref[k, high_own:length] = plane_zero

    barrier = pltpu.get_barrier_semaphore()
    for dy in range(levels):
        for dx in range(2):
            for dc in range(2):
                if dy or dx or dc:
                    there = {
                        "tm": 2 * lax.rem(y + dy, levels) + lax.rem(core + dc, 2),
                        "space": 2 * pair + lax.rem(x + dx, 2),
                    }
                    pl.semaphore_signal(barrier, inc=1, device_id=there, device_id_type=MESH)
    count = jnp.int32(2 * nt - 1)
    for far, there in (
        (jnp.logical_and(core == 0, has_low), low_to),
        (jnp.logical_and(core == 1, has_high), high_to),
    ):

        @pl.when(far)
        def _(there=there):
            pl.semaphore_signal(barrier, inc=1, device_id=there, device_id_type=MESH)

        count = count + far.astype(jnp.int32)

    for k in range(nt):
        clear_rows(start, k)
        clear_planes(start, k)
    for k in range(nt - 1):
        clear_rows(again, k)
        clear_planes(again, k)
        clear_rows(chain, k)
    clear_rows(first, 0)
    clear_rows(second, 0)
    clear_planes(rate, 0)
    clear_planes(chain, 1)
    for j in range(2, nt - 1):
        clear_planes(offset, j)

    pl.semaphore_wait(barrier, count)

    sends = []
    send_count = [0]

    def launch(make, slot, there, condition, wider):
        number = send_count[0]
        send_count[0] += 1
        for rows, fits in ((most, wider), (less, jnp.logical_not(wider))):
            src, dst = make(rows)
            copy = pltpu.make_async_remote_copy(
                src_ref=src, dst_ref=dst, send_sem=send.at[number], recv_sem=recv.at[slot],
                device_id=there, device_id_type=MESH,
            )
            sends.append((copy, jnp.logical_and(condition, fits)))
            pl.when(jnp.logical_and(condition, fits))(copy.start)

    def local(make, slot, condition):
        for rows, fits in ((most, edge), (less, inside)):
            src, dst = make(rows)
            pl.when(jnp.logical_and(condition, fits))(pltpu.make_async_copy(src, dst, recv.at[slot]).start)

    def arrive(dst_of, slot, condition=True):
        for rows, fits in ((most, edge), (less, inside)):
            dst = dst_of(rows)
            pl.when(jnp.logical_and(condition, fits))(pltpu.make_async_copy(dst, dst, recv.at[slot]).wait)

    own = pl.ds(low_own, planes)
    home = core == x
    away = jnp.logical_not(home)

    cut = -(-most // (CORES * SUBLANES)) * SUBLANES

    def filling(src, begin, ref, k, tile, turn=None):
        def make(rows):
            at, size = (0, rows) if turn is None else (cut * turn, min(cut * (turn + 1), rows) - cut * turn)
            from_rows = pl.ds(pl.multiple_of(begin + at, SUBLANES), size)
            return src.at[:, from_rows, pl.ds(tile * LANES, LANES)], ref.at[k, own, tile, pl.ds(wide + at, size), :]

        return make

    def arrive_filling(ref, k, tile, slot, turn=None):
        arrive(lambda rows: filling(initial, 0, ref, k, tile, turn)(rows)[1], slot)

    def give_split(src, ref, kind, to_y, condition, wider):
        begin = begin_of(to_y, 1 - x)
        for tile in range(tiles):
            for turn in range(CORES):
                launch(
                    filling(src, begin, ref, 0, tile, turn), recv_of[kind] + CORES * tile + turn,
                    {"tm": 2 * to_y + x, "space": space + 1 - 2 * x}, jnp.logical_and(condition, core == turn), wider,
                )

    give_split(initial, start, "initial", y, jnp.bool_(True), edge)
    for ref, src, kind in ((start, initial, "initial"), (rate, rate_in, "rate")):
        for tile in range(tiles):
            for turn in range(CORES):
                local(filling(src, my_begin, ref, 0, tile, turn), recv_of[kind] + CORES * tile + turn, home)

    for to_y in range(levels):
        give_split(rate_in, rate, "rate", to_y, edge, jnp.bool_(to_y == levels - 1))

    def give_guess(turn):
        gives = jnp.logical_and(tm < nt - 1, core == turn)
        number = jnp.minimum(tm + 1, nt - 1)
        for tile in range(tiles):
            slot = recv_of["guess"] + number * tiles + tile
            for dy in range(levels):
                for dx in (1, 0):
                    to_y, to_x = lax.rem(y + dy, levels), lax.rem(x + dx, 2)
                    make = filling(guess, begin_of(to_y, to_x), start, number, tile)
                    there = {"tm": 2 * to_y + x, "space": 2 * pair + to_x}
                    if dy or dx:
                        launch(make, slot, there, gives, to_y == levels - 1)
                    else:
                        launch(make, slot, there, jnp.logical_and(gives, away), edge)
                        local(make, slot, jnp.logical_and(gives, home))

    give_guess(0)

    reaches = [jnp.where(inside_of, fine_diffuse, 0.0) for inside_of in (has_low, True, has_high)]
    reaches[1] = fine_diffuse

    def share(view, depth, high_slot, low_slot):
        def low(rows):
            return view(pl.ds(low_own, depth), rows), view(pl.ds(high_own, depth), rows)

        def high(rows):
            return view(pl.ds(high_own - depth, depth), rows), view(pl.ds(low_own - depth, depth), rows)

        launch(low, high_slot, low_to, has_low, edge)
        launch(high, low_slot, high_to, has_high, edge)

    def shared(view, depth, high_slot, low_slot):
        arrive(lambda rows: view(pl.ds(high_own, depth), rows), high_slot, has_high)
        arrive(lambda rows: view(pl.ds(low_own - depth, depth), rows), low_slot, has_low)

    def tile_view(ref, k, tile):
        return lambda zs, rows: ref.at[k, zs, tile, pl.ds(wide, rows), :]

    def relay_start(k):
        for tile in range(tiles):
            if k:
                arrive_filling(start, k, tile, recv_of["guess"] + k * tiles + tile)
            else:
                for turn in range(CORES):
                    arrive_filling(start, 0, tile, recv_of["initial"] + CORES * tile + turn, turn)
            at = k * tiles + tile
            share(tile_view(start, k, tile), STEPS, recv_of["high_start"] + at, recv_of["low_start"] + at)

    def start_ready(k):
        for tile in range(tiles):
            at = k * tiles + tile
            shared(tile_view(start, k, tile), STEPS, recv_of["high_start"] + at, recv_of["low_start"] + at)

    def relay_rate():
        for tile in range(tiles):
            for turn in range(CORES):
                arrive_filling(rate, 0, tile, recv_of["rate"] + CORES * tile + turn, turn)
            share(tile_view(rate, 0, tile), STEPS - 1, recv_of["high_rate"] + tile, recv_of["low_rate"] + tile)

    def rate_ready():
        for tile in range(tiles):
            shared(tile_view(rate, 0, tile), STEPS - 1, recv_of["high_rate"] + tile, recv_of["low_rate"] + tile)

    def body_view(ref, k):
        return lambda zs, rows: ref.at[k, zs, :, pl.ds(wide, rows), :]

    tall = next(number for number in (64, 32, 16, 8) if most % number == 0)
    lane = lax.broadcasted_iota(jnp.int32, (tall, LANES), 1)

    def march(src, k, low, high, emit):
        def block(number, carry):
            at = pl.multiple_of(wide + number * tall, SUBLANES)
            here = pl.ds(at, tall)

            def load(z):
                return [src[k, z, tile, here, :] for tile in range(tiles)]

            under, middle = load(low - 1), load(low)
            for z in range(low, high):
                over = load(z + 1)
                zone = 0 if z < low_own else 1 if z < high_own else 2
                after = [pltpu.roll(part_of, 1, 1) for part_of in middle]
                ahead = [pltpu.roll(part_of, LANES - 1, 1) for part_of in middle]
                for tile in range(tiles):
                    value = middle[tile]
                    left = after[tile - 1] if tile else 0.0
                    right = ahead[tile + 1] if tile + 1 < tiles else 0.0
                    beside = over[tile] + under[tile]
                    beside = beside + src[k, z, tile, pl.ds(at - 1, tall), :] + src[k, z, tile, pl.ds(at + 1, tall), :]
                    beside = beside + jnp.where(lane == 0, left, after[tile])
                    beside = beside + jnp.where(lane == LANES - 1, right, ahead[tile])
                    growth = rate[0, z, tile, here, :] * (fine_growth - fine_growth * (value * value))
                    stepped = reaches[zone] * beside + value * (growth + (1.0 - 6.0 * fine_diffuse))
                    emit((z, tile, here), value, stepped)
                under, middle = middle, over
            return carry

        lax.fori_loop(0, most // tall, block, 0)

    def rough_of(value, stepped):
        return value + coarse_ratio * (stepped - value)

    def put(ref, k, spot, value):
        z, tile, here = spot
        ref[k, z, tile, here, :] = value

    def get(ref, k, spot):
        z, tile, here = spot
        return ref[k, z, tile, here, :]

    def fine(src, source_k, dst, halo, rough=False):
        def emit(spot, value, stepped):
            put(dst, 0, spot, stepped)
            if rough and low_own <= spot[0] < high_own:
                put(coarse, 0, spot, rough_of(value, stepped))

        march(src, source_k, low_own - halo, high_own + halo, emit)

    def own_begin(number):
        return outer + inner * (number - 1) if number else 0

    def hand_in(ref, k, out, kind, j):
        begin = pl.multiple_of(my_begin + inset, SUBLANES)
        slot = recv_of[kind] + my_part

        def make(rows):
            size = outer if rows == most else inner
            src = ref.at[k, own, :, pl.ds(pl.multiple_of(wide + inset, SUBLANES), size), :]
            return src, out.at[:, :, pl.ds(begin, size), :]

        stays = jnp.logical_and(tm == j, home)
        launch(make, slot, {"tm": j, "space": 2 * pair + core}, jnp.logical_not(stays), edge)
        local(make, slot, stays)

    def relax(k):
        fine(start, k, first, STEPS - 1, rough=k == 0)
        fine(first, 0, second, STEPS - 2)

        def emit(spot, value, stepped):
            if k == nt - 1:
                put(defect, k, spot, get(end, 0, spot) - stepped)
                return
            put(again, k, spot, stepped)
            if k == 0:
                put(defect, 0, spot, stepped - stepped)
                base = get(coarse, 0, spot)
                put(chain, 0, spot, base + (stepped - base))

        march(second, 0, low_own, high_own, emit)

    def send_again(k):
        share(body_view(again, k), STEPS, recv_of["high_again"] + k, recv_of["low_again"] + k)

    def finish(k):
        shared(body_view(again, k), STEPS, recv_of["high_again"] + k, recv_of["low_again"] + k)
        fine(again, k, first, STEPS - 1, rough=True)
        fine(first, 0, second, STEPS - 2)

        def emit(spot, value, stepped):
            if k + 1 < nt - 1:
                put(defect, k + 1, spot, stepped - get(again, k + 1, spot))
            else:
                put(end, 0, spot, stepped)
            base = get(coarse, 0, spot)
            if k:
                put(offset, k + 1, spot, stepped - base)
            else:
                put(chain, 1, spot, base + (stepped - base))

        march(second, 0, low_own, high_own, emit)

    def lift_between(j, low, high):
        def emit(spot, value, stepped):
            put(chain, j, spot, rough_of(value, stepped) + get(offset, j, spot))

        march(chain, j - 1, low, high, emit)

    def edges_of(j):
        slots = recv_of["high_offset"] + j, recv_of["low_offset"] + j
        return body_view(offset, j), nt - 1 - j, *slots

    def lift_around(j):
        halo = nt - 1 - j
        if halo:
            shared(*edges_of(j))
            lift_between(j, low_own - halo, low_own)
            lift_between(j, high_own, high_own + halo)

    relay_start(0)
    relay_rate()
    give_guess(1)
    relay_start(1)
    start_ready(0)
    rate_ready()
    relax(0)
    send_again(0)
    hand_in(chain, 0, corrected_out, "corrected", 0)
    hand_in(defect, 0, defect_out, "defect", 0)
    relay_start(2)
    start_ready(1)
    relax(1)
    send_again(1)
    finish(0)
    first_edges = body_view(chain, 1), nt - 2, recv_of["high_first"], recv_of["low_first"]
    share(*first_edges)
    hand_in(chain, 1, corrected_out, "corrected", 1)
    hand_in(defect, 1, defect_out, "defect", 1)
    for j in range(2, nt):
        if j < nt - 1:
            start_ready(j)
            relax(j)
            send_again(j)
        finish(j - 1)
        if j < nt - 1:
            share(*edges_of(j))
            relay_start(j + 1)
            hand_in(defect, j, defect_out, "defect", j)
        if j == 2:
            shared(*first_edges)
        else:
            lift_around(j - 1)
        lift_between(j, low_own, high_own)
        hand_in(chain, j, corrected_out, "corrected", j)
    start_ready(nt - 1)
    relax(nt - 1)
    hand_in(defect, nt - 1, defect_out, "defect", nt - 1)

    for copy, condition in sends:
        pl.when(condition)(copy.wait_send)
    for out, kind in ((corrected_out, "corrected"), (defect_out, "defect")):
        for number in range(nt):
            size = inner if 0 < number < nt - 1 else outer
            dst = out.at[:, :, pl.ds(own_begin(number), size), :]
            pltpu.make_async_copy(dst, dst, recv.at[recv_of[kind] + number]).wait()


def settle_kernel(corrected, defect, corrected_out, defect_out, local):
    copies = []
    for src, dst in ((corrected, corrected_out), (defect, defect_out)):
        for tile in range(src.shape[1]):
            to = dst.at[0, :, :, pl.ds(tile * LANES, LANES)]
            copies.append(pltpu.make_async_copy(src.at[:, tile], to, local.at[len(copies)]))
    for copy in copies:
        copy.start()
    for copy in copies:
        copy.wait()


def settle(corrected, defect):
    planes, tiles, across, lanes = corrected.shape
    shape = jax.ShapeDtypeStruct((1, planes, across, tiles * lanes), jnp.float32)
    return pl.pallas_call(
        settle_kernel,
        out_shape=(shape, shape),
        in_specs=[pl.BlockSpec(memory_space=pl.ANY)] * 2,
        out_specs=[pl.BlockSpec(memory_space=pl.ANY)] * 2,
        scratch_shapes=[pltpu.SemaphoreType.DMA((2 * tiles,))],
        compiler_params=pltpu.CompilerParams(vmem_limit_bytes=1 << 20),
    )(corrected, defect)


def quarter_device(nt, ns, initial, coarse_guess, react_rate):
    planes, across, width = initial.shape
    wide, inner = quarter_rows(nt, across)
    length = planes + 2 * STEPS
    tall = inner + 5 * wide
    tiles = width // LANES
    recv_of, recv_total = quarter_slots(nt, tiles)

    def field(number):
        return pltpu.VMEM((number, length, tiles, tall, LANES), jnp.float32)

    shape = jax.ShapeDtypeStruct((planes, tiles, across, LANES), jnp.float32)
    corrected, defect = pl.pallas_call(
        functools.partial(quarter_kernel, nt, ns, planes, inner, wide, recv_of),
        out_shape=(shape, shape),
        in_specs=[pl.BlockSpec(memory_space=pltpu.HBM)] * 3,
        out_specs=[pl.BlockSpec(memory_space=pl.ANY)] * 2,
        scratch_shapes=[
            field(nt), field(nt), field(1), field(1), field(1), field(1), field(nt), field(nt), field(nt), field(1),
            pltpu.SemaphoreType.DMA((tiles * (CORES * (1 + nt // 2) + 4 * nt + 2) + 6 * nt - 6,)),
            pltpu.SemaphoreType.DMA((recv_total,)),
        ],
        compiler_params=pltpu.CompilerParams(collective_id=0, has_side_effects=True, vmem_limit_bytes=VMEM_BYTES),
    )(*(pltpu.with_memory_space_constraint(ref, pltpu.HBM) for ref in (initial, coarse_guess[0], react_rate)))
    return settle(corrected, defect)


def quarter_rows(nt, across):
    wide = -(-(2 * STEPS + max(nt - 2, 0)) // SUBLANES) * SUBLANES
    return wide, (across - 4 * wide) // nt


def takes_quarters(nt, planes, across, width):
    wide, inner = quarter_rows(nt, across)
    fits = inner > 0 and (across - 4 * wide) % (nt * SUBLANES) == 0 and nt - 2 <= planes
    return nt % 2 == 0 and nt > 2 and planes >= STEPS and width % LANES == 0 and fits


def on_device(nt, ns, initial, coarse_guess, react_rate):
    planes, across, width = initial.shape
    if takes_quarters(nt, planes, across, width):
        return quarter_device(nt, ns, initial, coarse_guess, react_rate)
    half = across // 2
    wide = -(-(2 * STEPS + max(nt - 2, 0)) // SUBLANES) * SUBLANES
    length = 2 * planes + 2 * STEPS
    field = pltpu.VMEM((length, half + 2 * wide, width), jnp.float32)
    slot_of, total = slots(planes)
    shape = jax.ShapeDtypeStruct(initial.shape, jnp.float32)
    corrected, defect = pl.pallas_call(
        functools.partial(kernel, nt, ns, planes, half, wide, slot_of),
        out_shape=(shape, shape),
        in_specs=[pl.BlockSpec(memory_space=pl.ANY)] * 3,
        out_specs=[pl.BlockSpec(memory_space=pl.ANY)] * 2,
        scratch_shapes=[field] * 11
        + [
            pltpu.VMEM((half + 2 * wide, width), jnp.float32),
            pltpu.SemaphoreType.DMA((total,)),
            pltpu.SemaphoreType.DMA((total,)),
            pltpu.SemaphoreType.DMA((3 + planes,)),
        ],
        compiler_params=pltpu.CompilerParams(collective_id=0, has_side_effects=True),
    )(initial, coarse_guess[0], react_rate)
    return corrected[None], defect[None]


def solution(mesh):
    in_specs = (P("space", None, None), P("tm", "space", None, None), P("space", None, None))
    out_specs = (P("tm", "space", None, None), P("tm", "space", None, None))
    return jax.shard_map(
        functools.partial(on_device, mesh.shape["tm"], mesh.shape["space"]),
        mesh=mesh, in_specs=in_specs, out_specs=out_specs, check_vma=False,
    )
```
